256 devices in a mesh: tm: 4 (over y), det: 64 (over z, x, core).
Axes of the slice: x: 4, y: 4, z: 8, core: 2. Of those that a mesh axis runs over, the one named last changes fastest.
Arguments:
- offset_amplitude_array: float32 [128, 16], P('det', 'tm'), may hold values from -6 to 6
- system_remainder: float32 [128, 16], P('det', 'tm'), may hold values from -6 to 6
- conjugate_heading: float32 [128, 16], P('det', 'tm'), may hold values from -6 to 6
- region_cell_numbers: int32 [128, 16384], P('det', 'tm'), may hold values from 0 to 255
- stokes_reading_rotation: float32 [128, 16384], P('det', 'tm'), may hold values from -3.140625 to 3.140625
- scan_patch_places: int32 [128, 128], P('det', 'tm'), may hold values from 0 to 127
- holder_visited_regions: int32 [4, 64, 64, 2], P('tm', 'det'), may hold values from 0 to 47, as said below
- stokes_precision_matrices: float32 [3072, 6, 256], P('det'), as said below
Outputs:
- refreshed_offset_amplitudes: float32 [128, 16], P('det', 'tm')
- updated_residual_vector: float32 [128, 16], P('det', 'tm')
- updated_search_direction: float32 [128, 16], P('det', 'tm')
The draws below stay inside these ranges and needn't reach their ends.
Inputs may be any that keep to these rules, and one draw needn't show every extreme that they name: For each device (i, j) and owner o, holder_visited_regions[i, j, o, :] holds 2 distinct local submaps. `stokes_precision_matrices`: each pixel's 3x3 block is symmetric positive definite.
All inputs are finite; a program needn't handle non-finite values.
Results may differ from the reference program's by a relative error of at most 0.00005.
Values sent between devices are 32-bit elements; how exact they have to be, the bound alone decides.
No kernel may reach another device: no remote copies, remote signals or barrier semaphores. Data moves between devices by JAX's collectives and lax.ppermute only.
A program may use at most 64 MiB of HBM per device.

```python
import jax
import jax.numpy as jnp

DET_DEV = 2
SAMP_DEV = 4096
TILE = 128
WINDOW = 256
BASE_LEN = 1024
SUB_DEV = 48
HPO = 2
SUBMAPS = 3072
SLOTS = 128
RECEIVER_NUMBER = 128
SAMPLES = 16384
OFFSET_NUMBER = 16
N_TM = 4
N_DET = 64


def draw_holder_visited_regions(key, part):
    keys = jax.random.split(key, N_TM * N_DET * N_DET)
    shuffled = jax.vmap(lambda single: jax.random.permutation(single, SUB_DEV))(keys)
    return shuffled[:, :HPO].reshape(N_TM, N_DET, N_DET, HPO).astype(jnp.int32)


def draw_stokes_precision_matrices(key, part):
    first_key, second_key = jax.random.split(jax.random.fold_in(key, 17))
    lowest = jnp.log(0.3)
    diagonal = jnp.exp(jax.random.uniform(first_key, (SUBMAPS, 3, WINDOW), jnp.float32, lowest, jnp.log(3.0)))
    offdiag = jax.random.uniform(second_key, (SUBMAPS, 3, WINDOW), jnp.float32, -1.0, 1.0)
    diag_one = diagonal[:, 0]
    diag_two = diagonal[:, 1]
    diag_three = diagonal[:, 2]
    cross_one = 0.3 * offdiag[:, 0] * jnp.minimum(diag_one, diag_two)
    cross_two = 0.3 * offdiag[:, 1] * jnp.minimum(diag_one, diag_three)
    cross_three = 0.3 * offdiag[:, 2] * jnp.minimum(diag_two, diag_three)
    return jnp.stack([diag_one, cross_one, cross_two, diag_two, cross_three, diag_three], axis=1).astype(jnp.float32)


def set_ends(result, rng, least, high):
    dims = result.shape
    index_at = [jax.random.randint(jax.random.fold_in(rng, axis), (), 0, dims[axis]) for axis in range(len(dims))]
    result = result.at[tuple(index_at)].set(least)
    longest = dims.index(max(dims))
    index_at[longest] = (index_at[longest] + 1) % dims[longest]
    return result.at[tuple(index_at)].set(high)


def level_of(rng, dims, cuts, least, high):
    gain, own = 1.0, jax.random.fold_in(rng, 6)
    for dim, parts in cuts:
        steps = jnp.exp(jax.random.uniform(jax.random.fold_in(own, dim), (parts,), jnp.float32, least / len(cuts), high / len(cuts)))
        gain = gain * jnp.repeat(steps, dims[dim] // parts).reshape([-1 if axis == dim else 1 for axis in range(len(dims))])
    return gain


def bell_draw(stream_key, dims, deviation, limit, cuts=(), held_as=jnp.bfloat16):
    result = deviation * jax.random.normal(stream_key, dims, jnp.float32)
    if cuts:
        result = result * level_of(stream_key, dims, cuts, -0.22, 0.18)
    return jnp.clip(result, -limit, limit).astype(held_as)


def setup_inputs(seed: int = 0) -> dict:
    streams_of = jax.random.split(jax.random.key(seed), 9)
    offset_amplitude_array = bell_draw(streams_of[0], (RECEIVER_NUMBER, OFFSET_NUMBER), 1.0, 6.0, ((0, 64), (1, 4)), jnp.float32)
    system_remainder = bell_draw(streams_of[1], (RECEIVER_NUMBER, OFFSET_NUMBER), 1.0, 6.0, ((0, 64), (1, 4)), jnp.float32)
    conjugate_heading = bell_draw(streams_of[2], (RECEIVER_NUMBER, OFFSET_NUMBER), 1.0, 6.0, ((0, 64), (1, 4)), jnp.float32)
    region_cell_numbers = set_ends(jax.random.randint(streams_of[3], (RECEIVER_NUMBER, SAMPLES), 0, WINDOW), jax.random.fold_in(streams_of[3], 1), 0, WINDOW - 1).astype(jnp.int32)
    stokes_reading_rotation = jnp.clip(jax.random.uniform(streams_of[4], (RECEIVER_NUMBER, SAMPLES), jnp.float32, -3.140625, 3.140625), -3.140625, 3.140625)
    scan_patch_places = set_ends(jax.random.randint(streams_of[5], (RECEIVER_NUMBER, SAMPLES // TILE), 0, SLOTS), jax.random.fold_in(streams_of[5], 1), 0, SLOTS - 1).astype(jnp.int32)
    holder_visited_regions = draw_holder_visited_regions(jax.random.fold_in(streams_of[8], 71), 0)
    stokes_precision_matrices = draw_stokes_precision_matrices(jax.random.fold_in(streams_of[8], 71), 0)
    return {"offset_amplitude_array": offset_amplitude_array, "system_remainder": system_remainder, "conjugate_heading": conjugate_heading, "region_cell_numbers": region_cell_numbers, "stokes_reading_rotation": stokes_reading_rotation, "scan_patch_places": scan_patch_places, "holder_visited_regions": holder_visited_regions, "stokes_precision_matrices": stokes_precision_matrices}


stiffness = 0.5


def solve_blocks(binned, stokes_precision_matrices):
    first = binned[:, 0]
    second = binned[:, 1]
    third = binned[:, 2]
    out_first = stokes_precision_matrices[:, 0] * first + stokes_precision_matrices[:, 1] * second + stokes_precision_matrices[:, 2] * third
    out_second = stokes_precision_matrices[:, 1] * first + stokes_precision_matrices[:, 3] * second + stokes_precision_matrices[:, 4] * third
    out_third = stokes_precision_matrices[:, 2] * first + stokes_precision_matrices[:, 4] * second + stokes_precision_matrices[:, 5] * third
    return jnp.stack([out_first, out_second, out_third], axis=1)


def reference(offset_amplitude_array, system_remainder, conjugate_heading, region_cell_numbers, stokes_reading_rotation, scan_patch_places, holder_visited_regions, stokes_precision_matrices):
    det_count, sample_count = region_cell_numbers.shape
    stream = jnp.repeat(conjugate_heading, BASE_LEN, axis=1)
    twice = 2.0 * stokes_reading_rotation
    cos_weight = jnp.cos(twice)
    sin_weight = jnp.sin(twice)
    slot_index = jnp.repeat(scan_patch_places, TILE, axis=1)
    det_group = (jnp.arange(det_count, dtype=jnp.int32) // DET_DEV)[:, None]
    time_span = (jnp.arange(sample_count, dtype=jnp.int32) // SAMP_DEV)[None, :]
    owner = slot_index // HPO
    local_submap = holder_visited_regions[time_span, det_group, owner, slot_index % HPO]
    cell = ((owner * SUB_DEV + local_submap) * (3 * WINDOW) + region_cell_numbers).astype(jnp.int32)
    values = jnp.concatenate([stream.ravel(), (stream * cos_weight).ravel(), (stream * sin_weight).ravel()])
    targets = jnp.concatenate([cell.ravel(), (cell + WINDOW).ravel(), (cell + 2 * WINDOW).ravel()])
    binned = jax.ops.segment_sum(values, targets, num_segments=SUBMAPS * 3 * WINDOW).reshape(SUBMAPS, 3, WINDOW)
    sky_map = solve_blocks(binned, stokes_precision_matrices).reshape(-1)
    scanned = sky_map[cell] + cos_weight * sky_map[cell + WINDOW] + sin_weight * sky_map[cell + 2 * WINDOW]
    folded = scanned.reshape(det_count, -1, BASE_LEN).sum(axis=2) / BASE_LEN
    padded = jnp.pad(conjugate_heading, ((0, 0), (1, 1)))
    applied = conjugate_heading + folded + stiffness * (2.0 * conjugate_heading - padded[:, :-2] - padded[:, 2:])
    norm_now = jnp.sum(system_remainder * system_remainder)
    curvature = jnp.sum(conjugate_heading * applied)
    conjugate_update_factor = norm_now / curvature
    refreshed_offset_amplitudes = offset_amplitude_array + conjugate_update_factor * conjugate_heading
    updated_residual_vector = system_remainder - conjugate_update_factor * applied
    norm_next = jnp.sum(updated_residual_vector * updated_residual_vector)
    updated_search_direction = updated_residual_vector + (norm_next / norm_now) * conjugate_heading
    return (refreshed_offset_amplitudes, updated_residual_vector, updated_search_direction)
```

```python
import functools

import jax
import jax.numpy as jnp
import numpy as np
from jax import lax
from jax.experimental import pallas as pl
from jax.experimental.pallas import tpu as pltpu
from jax.sharding import PartitionSpec as P

TILE = 128
WINDOW = 256
STIFFNESS = 0.5
BF16 = jnp.bfloat16
F32 = jnp.float32
I32 = jnp.int32
NT = (((1,), (1,)), ((), ()))
NN = (((1,), (0,)), ((), ()))


def iota(shape, dim):
    return lax.broadcasted_iota(I32, shape, dim)


def dot(a, b, dims=NN):
    return lax.dot_general(a, b, dims, preferred_element_type=F32)


def split(x):
    high = x.astype(BF16)
    return high, (x - high.astype(F32)).astype(BF16)


def cos_sin(x):
    n = jnp.floor(x * np.float32(2.0 / np.pi) + 0.5)
    r = x - n * np.float32(1.5703125)
    r = r - n * np.float32(4.837512969970703e-4)
    r = r - n * np.float32(7.549789948768648e-8)
    z = r * r
    s = np.float32(-1.9515295891e-4) * z + np.float32(8.3321608736e-3)
    s = (s * z + np.float32(-1.6666654611e-1)) * z * r + r
    c = np.float32(2.443315711809948e-5) * z + np.float32(-1.388731625493765e-3)
    c = (c * z + np.float32(4.166664568298827e-2)) * z * z - 0.5 * z + 1.0
    q = n.astype(I32)
    odd = (q & 1) == 1
    cosine = jnp.where(odd, s, c)
    sine = jnp.where(odd, c, s)
    cosine = jnp.where(((q + 1) & 2) == 2, -cosine, cosine)
    sine = jnp.where((q & 2) == 2, -sine, sine)
    return cosine, sine


def tile_parts(row, slot, pix_ref, cos_ref, sin_ref):
    hot = iota((WINDOW, TILE), 0) == pix_ref[pl.ds(row, 1), :]
    hot = jnp.where(hot, 1.0, 0.0).astype(BF16)
    sub = iota((8, TILE), 0)
    part = sub & 3
    weight = jnp.where(
        part == 0, 1.0, jnp.where(part == 1, cos_ref[pl.ds(row, 1), :], sin_ref[pl.ds(row, 1), :])
    )
    mine = (sub >> 2) == ((slot >> 1) & 1)
    weight = jnp.where(mine & (part < 3), weight, 0.0)
    return hot, weight


def bin_kernel(slot_ref, dir_ref, pix_ref, ang_ref, hits_ref, out_ref, cos_ref, sin_ref, acc_ref):
    c, s = cos_sin(2.0 * ang_ref[...])
    cos_ref[...] = c
    sin_ref[...] = s
    acc_ref[...] = jnp.zeros_like(acc_ref)
    tiles = pix_ref.shape[0]
    dets, bases = dir_ref.shape
    span = tiles // dets // bases

    def group(g, carry):
        det, base = g % dets, g // dets
        height = dir_ref[det, base]
        for t in range(span):
            tile = base * span + t
            slot = slot_ref[det, tile]
            hot, weight = tile_parts(tile * dets + det, slot, pix_ref, cos_ref, sin_ref)
            high = weight.astype(BF16).astype(F32)
            both = jnp.concatenate([high, weight - high], axis=0).astype(BF16)
            res = dot(both, hot, NT)
            res = (res[:8] + res[8:]) * height
            place = (slot & 1) * (acc_ref.shape[0] // 2) + (slot >> 2)
            acc_ref[place] = acc_ref[place] + res
        return carry

    lax.fori_loop(0, dets * bases, group, 0)

    pairs = acc_ref.shape[0] // 2
    sub = iota((8, TILE), 0)
    left = iota((8, TILE), 1) < 64
    last = (sub & 3) == 3
    hits = jnp.broadcast_to(hits_ref[...], (8, TILE))
    for u in range(pairs):
        for b in range(2):
            first = acc_ref[u, :, b * TILE : (b + 1) * TILE]
            second = acc_ref[pairs + u, :, b * TILE : (b + 1) * TILE]
            even = jnp.where(left, first, pltpu.roll(second, 64, 1))
            odd = jnp.where(left, pltpu.roll(first, 64, 1), second)
            for q, value in ((2 * b, even), (2 * b + 1, odd)):
                at = (q * pairs + u) * 8
                out_ref[at : at + 8, :] = jnp.where(last, hits, value)


def own_kernel(me_ref, in_ref, prec_ref, out_ref):
    me = me_ref[0]
    quarter = me_ref[1]
    sources = in_ref.shape[0] // 4
    subs = prec_ref.shape[1]
    ids = in_ref[pl.ds(3, sources, stride=4), :].astype(BF16)
    lane = iota((16, TILE), 1)
    row = iota((16, TILE), 0)
    pick = jnp.where((lane == me + 64 * row) & (row < 2), 1.0, 0.0).astype(BF16)
    id_rows = dot(pick, ids, NT).astype(I32)
    sub = iota((subs, sources), 0)
    hot = jnp.concatenate(
        [
            jnp.where(sub == id_rows[0:1, :], 1.0, 0.0),
            jnp.where(sub == id_rows[1:2, :], 1.0, 0.0),
        ],
        axis=0,
    ).astype(BF16)
    left = iota((subs, TILE), 1) < 64
    binned = []
    for c in range(3):
        high, low = split(in_ref[pl.ds(c, sources, stride=4), :])
        res = dot(hot, jnp.concatenate([high, low], axis=1))
        res = res[:, :TILE] + res[:, TILE:]
        res = jnp.where(left, res[:subs], res[subs:])
        binned.append(res + pltpu.roll(res, 64, 1))

    block = quarter // 2
    keep = left == ((quarter % 2) == 0)
    prec = []
    for e in range(6):
        value = jnp.where(block == 0, prec_ref[e, :, :TILE], prec_ref[e, :, TILE:])
        value = jnp.where(keep, value, 0.0)
        prec.append(value + pltpu.roll(value, 64, 1))
    sky = [
        prec[0] * binned[0] + prec[1] * binned[1] + prec[2] * binned[2],
        prec[1] * binned[0] + prec[3] * binned[1] + prec[4] * binned[2],
        prec[2] * binned[0] + prec[4] * binned[1] + prec[5] * binned[2],
    ]

    deep, wide = iota((TILE, TILE), 0), iota((TILE, TILE), 1)
    spread = jnp.where(deep == me + (wide & 64), 1.0, 0.0).astype(BF16)
    named = dot(ids, spread).astype(I32)
    back = jnp.where(named == (iota((sources, TILE), 1) & 63), 1.0, 0.0).astype(BF16)
    back = jnp.concatenate([back, back], axis=1)
    gap = jnp.zeros((64 - subs, TILE), F32)
    for c in range(3):
        first = jnp.where(left, sky[c], 0.0)
        second = jnp.where(left, 0.0, sky[c])
        high, low = split(jnp.concatenate([first, gap, second, gap], axis=0))
        out_ref[pl.ds(c, sources, stride=4), :] = dot(back, jnp.concatenate([high, low], axis=0))
    out_ref[pl.ds(3, sources, stride=4), :] = jnp.zeros((sources, TILE), F32)


def scan_kernel(
    slot_ref, dir_ref, res_ref, pix_ref, ang_ref, in_ref, out_ref, cos_ref, sin_ref, sky_ref, sum_ref
):
    c, s = cos_sin(2.0 * ang_ref[...])
    cos_ref[...] = c
    sin_ref[...] = s
    pairs = sky_ref.shape[0] // 2
    left = iota((8, TILE), 1) < 64
    for u in range(pairs):
        for b in range(2):
            at = (2 * b * pairs + u) * 8
            even = in_ref[at : at + 8, :]
            at = ((2 * b + 1) * pairs + u) * 8
            odd = in_ref[at : at + 8, :]
            sky_ref[u, :, b * TILE : (b + 1) * TILE] = jnp.where(left, even, pltpu.roll(odd, 64, 1))
            sky_ref[pairs + u, :, b * TILE : (b + 1) * TILE] = jnp.where(
                left, pltpu.roll(even, 64, 1), odd
            )
    tiles = pix_ref.shape[0]
    dets, bases = dir_ref.shape
    span = tiles // dets // bases

    def group(g, carry):
        det, base = g % dets, g // dets
        total = jnp.zeros((8, TILE), F32)
        for t in range(span):
            tile = base * span + t
            slot = slot_ref[det, tile]
            hot, weight = tile_parts(tile * dets + det, slot, pix_ref, cos_ref, sin_ref)
            place = (slot & 1) * pairs + (slot >> 2)
            value = sky_ref[place]
            high = value.astype(BF16).astype(F32)
            both = jnp.concatenate([high, value - high], axis=0).astype(BF16)
            res = dot(both, hot)
            total = total + (res[:8] + res[8:]) * weight
        sum_ref[pl.ds(det * bases + base, 1), :] = jnp.sum(total, axis=0, keepdims=True)
        return carry

    lax.fori_loop(0, dets * bases, group, 0)
    count = dets * bases
    sums = jnp.sum(sum_ref[...], axis=1, keepdims=True) * np.float32(1.0 / (span * TILE))
    lane, sub = iota((count, TILE), 1), iota((count, TILE), 0)
    row = jnp.sum(jnp.where(lane == sub, sums, 0.0), axis=0, keepdims=True)
    lane = iota((1, TILE), 1)
    for d in range(dets):
        for b in range(bases):
            k = d * bases + b
            row = jnp.where(lane == count + k, dir_ref[d, b], row)
            row = jnp.where(lane == 2 * count + k, res_ref[d, b], row)
    out_ref[...] = jnp.broadcast_to(row, out_ref.shape)


def end_kernel(me_ref, in_ref, amp_ref, amp_out, res_out, dir_out, keep_ref):
    rows = in_ref.shape[0]
    dets, bases = amp_ref.shape
    count = dets * bases
    owners = me_ref[2]
    x = in_ref[...]
    lane = iota((rows, TILE), 1)
    valid = lane < count
    base = lane % bases
    scan = jnp.where(valid, x, 0.0)
    way = jnp.where(valid, pltpu.roll(x, TILE - count, 1), 0.0)
    rest = jnp.where(valid, pltpu.roll(x, TILE - 2 * count, 1), 0.0)
    step = rows // 4
    zero = jnp.zeros((step, TILE), F32)
    from_left = pltpu.roll(jnp.concatenate([zero, way[:-step]], axis=0), TILE - (bases - 1), 1)
    from_right = pltpu.roll(jnp.concatenate([way[step:], zero], axis=0), bases - 1, 1)
    before = jnp.where(base == 0, from_left, pltpu.roll(way, 1, 1))
    after = jnp.where(base == bases - 1, from_right, pltpu.roll(way, TILE - 1, 1))
    applied = scan + way + STIFFNESS * (2.0 * way - before - after)
    applied = jnp.where(valid, applied, 0.0)

    def total(v):
        return jnp.sum(jnp.sum(v, axis=0, keepdims=True), axis=1, keepdims=True)

    now = total(rest * rest)
    factor = now / total(way * applied)
    fresh = rest - factor * applied
    ratio = total(fresh * fresh) / now
    keep_ref[0] = fresh
    keep_ref[1] = way
    mine = me_ref[1] * step + me_ref[0]
    my_fresh = keep_ref[0, pl.ds(mine, 1), :]
    my_way = keep_ref[1, pl.ds(mine, 1), :]
    move = factor * my_way
    turn = my_fresh + ratio * my_way
    for d in range(dets):
        lo, hi = d * bases, (d + 1) * bases
        amp_out[d : d + 1, :] = amp_ref[d : d + 1, :] + move[:, lo:hi]
        res_out[d : d + 1, :] = my_fresh[:, lo:hi]
        dir_out[d : d + 1, :] = turn[:, lo:hi]


SMEM = pl.BlockSpec(memory_space=pltpu.SMEM)
VMEM = pl.BlockSpec(memory_space=pltpu.VMEM)
AXES = ("tm", "det")


def exchange(value, rows):
    peers = value.shape[0] // rows
    moved = lax.all_to_all(value.reshape(peers, rows, TILE), AXES, 0, 0, tiled=True)
    return moved.reshape(value.shape)


def shards(amp, res, way, pix, ang, places, hits, prec):
    dets, samples = pix.shape
    per_det = samples // TILE
    tiles = dets * per_det
    owners = hits.shape[2]
    slots = owners * hits.shape[3]
    peers = 4 * owners
    subs = prec.shape[0]

    def rows_of(v):
        return v.reshape(dets, per_det, TILE).transpose(1, 0, 2).reshape(tiles, TILE)

    pix, ang = rows_of(pix), rows_of(ang)
    hit_row = hits.reshape(owners, 2).T.reshape(1, slots).astype(F32)
    me = jnp.stack([lax.axis_index("det"), lax.axis_index("tm"), owners]).astype(I32)

    binned = pl.pallas_call(
        bin_kernel,
        out_shape=jax.ShapeDtypeStruct((peers * 4, TILE), F32),
        in_specs=[SMEM, SMEM, VMEM, VMEM, VMEM],
        out_specs=VMEM,
        scratch_shapes=[
            pltpu.VMEM((tiles, TILE), F32),
            pltpu.VMEM((tiles, TILE), F32),
            pltpu.VMEM((slots // 2, 8, WINDOW), F32),
        ],
        name="bin_tiles",
    )(places, way, pix, ang, hit_row)
    binned = exchange(binned, 4)

    sky = pl.pallas_call(
        own_kernel,
        out_shape=jax.ShapeDtypeStruct((peers * 4, TILE), F32),
        in_specs=[SMEM, VMEM, VMEM],
        out_specs=VMEM,
        name="own_solve",
    )(me, binned, prec.transpose(1, 0, 2))
    sky = exchange(sky, 4)

    last = pl.pallas_call(
        scan_kernel,
        out_shape=jax.ShapeDtypeStruct((peers, TILE), F32),
        in_specs=[SMEM, SMEM, SMEM, VMEM, VMEM, VMEM],
        out_specs=VMEM,
        scratch_shapes=[
            pltpu.VMEM((tiles, TILE), F32),
            pltpu.VMEM((tiles, TILE), F32),
            pltpu.VMEM((slots // 2, 8, WINDOW), F32),
            pltpu.VMEM((8, TILE), F32),
        ],
        name="scan_tiles",
    )(places, way, res, pix, ang, sky)
    last = exchange(last, 1)

    return pl.pallas_call(
        end_kernel,
        out_shape=[jax.ShapeDtypeStruct(amp.shape, F32)] * 3,
        in_specs=[SMEM, VMEM, VMEM],
        out_specs=[VMEM] * 3,
        scratch_shapes=[pltpu.VMEM((2, peers, TILE), F32)],
        name="end_step",
    )(me, last, amp)


def solution(mesh):
    return jax.shard_map(
        shards,
        mesh=mesh,
        in_specs=(
            P("det", "tm"),
            P("det", "tm"),
            P("det", "tm"),
            P("det", "tm"),
            P("det", "tm"),
            P("det", "tm"),
            P("tm", "det", None, None),
            P("det", None, None),
        ),
        out_specs=(P("det", "tm"), P("det", "tm"), P("det", "tm")),
        check_vma=False,
    )
```

```python
import jax
import jax.numpy as jnp
import numpy as np
from jax import lax
from jax.experimental import pallas as pl
from jax.experimental.pallas import tpu as pltpu
from jax.sharding import PartitionSpec as P

TILE = 128
WINDOW = 256
STIFFNESS = 0.5

ROOM = 23
CHUNK = 2 * ROOM + 2
CODES = 2 * ROOM
HITS = 2 * ROOM + 1
COUNT = 32
OVER = 33
WAYS = 40
PLANES = 8
NEAR = 8
BF16 = jnp.bfloat16
F32 = jnp.float32
I32 = jnp.int32
NT = (((1,), (1,)), ((), ()))
NN = (((1,), (0,)), ((), ()))


def iota(shape, dim):
    return lax.broadcasted_iota(I32, shape, dim)


def dot(a, b, dims=NN):
    return lax.dot_general(a, b, dims, preferred_element_type=F32)


def split(x):
    high = x.astype(BF16)
    return high, (x - high.astype(F32)).astype(BF16)


def cos_sin(x):
    n = jnp.floor(x * np.float32(2.0 / np.pi) + 0.5)
    r = x - n * np.float32(1.5703125)
    r = r - n * np.float32(4.837512969970703e-4)
    r = r - n * np.float32(7.549789948768648e-8)
    z = r * r
    s = np.float32(-1.9515295891e-4) * z + np.float32(8.3321608736e-3)
    s = (s * z + np.float32(-1.6666654611e-1)) * z * r + r
    c = np.float32(2.443315711809948e-5) * z + np.float32(-1.388731625493765e-3)
    c = (c * z + np.float32(4.166664568298827e-2)) * z * z - 0.5 * z + 1.0
    q = n.astype(I32)
    odd = (q & 1) == 1
    cosine = jnp.where(odd, s, c)
    sine = jnp.where(odd, c, s)
    cosine = jnp.where(((q + 1) & 2) == 2, -cosine, cosine)
    sine = jnp.where((q & 2) == 2, -sine, sine)
    return cosine, sine


def tile_parts(pixels, cosine, sine, half):
    hot = iota((WINDOW, TILE), 0) == pixels
    hot = jnp.where(hot, 1.0, 0.0).astype(BF16)
    sub = iota((8, TILE), 0)
    part = sub & 3
    weight = jnp.where(part == 0, 1.0, jnp.where(part == 1, cosine, sine))
    weight = jnp.where(((sub >> 2) == half) & (part < 3), weight, 0.0)
    return hot, weight


def bin_tile(hot, weight):
    high = weight.astype(BF16).astype(F32)
    both = jnp.concatenate([high, weight - high], axis=0).astype(BF16)
    res = dot(both, hot, NT)
    return res[:8] + res[8:]


def scan_tile(hot, weight, value):
    high = value.astype(BF16).astype(F32)
    both = jnp.concatenate([high, value - high], axis=0).astype(BF16)
    res = dot(both, hot)
    return (res[:8] + res[8:]) * weight


def put_bins(acc_ref, out_ref, extra):
    pairs = acc_ref.shape[0] // 2
    left = iota((8, TILE), 1) < 64
    last = (iota((8, TILE), 0) & 3) == 3
    for u in range(pairs):
        for b in range(2):
            first = acc_ref[u, :, b * TILE : (b + 1) * TILE]
            second = acc_ref[pairs + u, :, b * TILE : (b + 1) * TILE]
            even = jnp.where(left, first, pltpu.roll(second, 64, 1))
            odd = jnp.where(left, pltpu.roll(first, 64, 1), second)
            for q, value in ((2 * b, even), (2 * b + 1, odd)):
                at = (q * pairs + u) * 8
                out_ref[at : at + 8, :] = jnp.where(last, extra[u % len(extra)], value)


def get_sky(in_ref, sky_ref):
    pairs = sky_ref.shape[0] // 2
    left = iota((8, TILE), 1) < 64
    for u in range(pairs):
        for b in range(2):
            at = (2 * b * pairs + u) * 8
            even = in_ref[at : at + 8, :]
            at = ((2 * b + 1) * pairs + u) * 8
            odd = in_ref[at : at + 8, :]
            sky_ref[u, :, b * TILE : (b + 1) * TILE] = jnp.where(left, even, pltpu.roll(odd, 64, 1))
            sky_ref[pairs + u, :, b * TILE : (b + 1) * TILE] = jnp.where(
                left, pltpu.roll(even, 64, 1), odd
            )


def pack_kernel(slot_ref, way_ref, res_ref, amp_ref, pix_ref, ang_ref, hits_ref, out_ref, own_ref):
    dets, bases = way_ref.shape
    per_det = slot_ref.shape[1]
    span = per_det // bases
    lane1 = iota((1, TILE), 1)
    values = jnp.zeros((1, TILE), F32)
    amps = jnp.zeros((1, TILE), F32)
    for d in range(dets):
        for b in range(bases):
            k = d * bases + b
            values = jnp.where((lane1 == WAYS + k) | (lane1 == 72 + k), way_ref[d, b], values)
            values = jnp.where(lane1 == 64 + k, res_ref[d, b], values)
            amps = jnp.where(lane1 == k, amp_ref[d, b], amps)
    own_ref[...] = jnp.zeros_like(own_ref)
    own_ref[0:1, :] = values
    own_ref[1:2, :] = amps

    out_ref[...] = jnp.zeros_like(out_ref)
    sub, lane = iota((PLANES, TILE), 0), iota((PLANES, TILE), 1)

    def tile_step(t, carry):
        low, high, codes = carry
        for d in range(dets):
            slot = slot_ref[d, t]
            plane = slot // (2 * NEAR)
            shift = (plane & 3) * 8
            upper = plane >> 2
            place = (jnp.where(upper == 1, high, low) >> shift) & 255
            one = jnp.left_shift(jnp.int32(1), shift)
            low = jnp.where(upper == 1, low, low + one)
            high = jnp.where(upper == 1, high + one, high)
            place = jnp.minimum(place, ROOM - 1)
            row = t * dets + d
            at = plane * CHUNK + place
            out_ref[pl.ds(at, 1), :] = pix_ref[pl.ds(row, 1), :].astype(F32)
            out_ref[pl.ds(at + ROOM, 1), :] = ang_ref[pl.ds(row, 1), :]
            code = (slot & (2 * NEAR - 1)) * 8 + d * bases + t // span
            codes = jnp.where((sub == plane) & (lane == place), code, codes)
        return low, high, codes

    zero = jnp.int32(0)
    low, high, codes = lax.fori_loop(
        0, per_det, tile_step, (zero, zero, jnp.zeros((PLANES, TILE), I32)), unroll=4
    )
    over = zero
    for z in range(PLANES):
        count = ((high if z >= 4 else low) >> (8 * (z & 3))) & 255
        over = jnp.maximum(over, jnp.where(count > ROOM, 1, 0))
        codes = jnp.where((sub == z) & (lane == COUNT), jnp.minimum(count, ROOM), codes)
    codes = jnp.where(lane == OVER, over, codes)
    codes = jnp.where(lane < WAYS, codes.astype(F32), values)
    out_ref[pl.ds(CODES, PLANES, stride=CHUNK), :] = codes
    hits = jnp.concatenate([hits_ref[0:1, :], hits_ref[1:2, :]], axis=1).astype(F32)
    out_ref[pl.ds(HITS, PLANES, stride=CHUNK), :] = jnp.broadcast_to(hits, (PLANES, TILE))


def start_codes(in_ref, code_ref, sems):
    copies = [
        pltpu.make_async_copy(
            in_ref.at[pl.ds(z * CHUNK + CODES, 1), :], code_ref.at[pl.ds(z, 1), :], sems.at[z]
        )
        for z in range(PLANES)
    ]
    for copy in copies:
        copy.start()
    return copies


def each_tile(in_ref, code_ref, cos_ref, sin_ref, use, group=4):
    def source(z, carry):
        count = code_ref[z, COUNT].astype(I32)

        def some(g, carry):
            for k in range(group):
                p = g * group + k
                code = code_ref[z, p].astype(I32)
                base = code & 7
                row = z * CHUNK + p
                hot, weight = tile_parts(
                    in_ref[pl.ds(row, 1), :].astype(I32),
                    cos_ref[pl.ds(row + ROOM, 1), :],
                    sin_ref[pl.ds(row + ROOM, 1), :],
                    z & 1,
                )
                use(z, code >> 3, base, p < count, hot, weight)
            return carry

        return lax.fori_loop(0, (count + group - 1) // group, some, carry)

    lax.fori_loop(0, PLANES, source, 0)


def place_of(z, local):
    return (local & 1) * (NEAR * PLANES // 2) + (local >> 1) * (PLANES // 2) + (z >> 1)


def bin_kernel(in_ref, out_ref, cos_ref, sin_ref, acc_ref, code_ref, sems):
    copies = start_codes(in_ref, code_ref, sems)
    c, s = cos_sin(2.0 * in_ref[...])
    cos_ref[...] = c
    sin_ref[...] = s
    acc_ref[...] = jnp.zeros_like(acc_ref)
    for copy in copies:
        copy.wait()

    def use(z, local, base, valid, hot, weight):
        height = jnp.where(valid, code_ref[z, WAYS + base], 0.0)
        place = place_of(z, local)
        acc_ref[place] = acc_ref[place] + bin_tile(hot, weight) * height

    each_tile(in_ref, code_ref, cos_ref, sin_ref, use)
    upper = iota((8, TILE), 0) < 4
    hits = []
    for z in range(0, PLANES, 2):
        first, second = (in_ref[y * CHUNK + HITS : y * CHUNK + HITS + 1, :] for y in (z, z + 1))
        hits.append(jnp.where(upper, first, second))
    put_bins(acc_ref, out_ref, hits)


def own_kernel(me_ref, in_ref, prec_ref, out_ref):
    me = me_ref[0]
    quarter = me_ref[1]
    sources = in_ref.shape[0] // 4
    subs = prec_ref.shape[1]
    ids = in_ref[pl.ds(3, sources, stride=4), :].astype(BF16)
    lane = iota((16, TILE), 1)
    row = iota((16, TILE), 0)
    pick = jnp.where((lane == me + 64 * row) & (row < 2), 1.0, 0.0).astype(BF16)
    id_rows = dot(pick, ids, NT).astype(I32)
    sub = iota((subs, sources), 0)
    hot = jnp.concatenate(
        [
            jnp.where(sub == id_rows[0:1, :], 1.0, 0.0),
            jnp.where(sub == id_rows[1:2, :], 1.0, 0.0),
        ],
        axis=0,
    ).astype(BF16)
    left = iota((subs, TILE), 1) < 64
    binned = []
    for c in range(3):
        high, low = split(in_ref[pl.ds(c, sources, stride=4), :])
        res = dot(hot, jnp.concatenate([high, low], axis=1))
        res = res[:, :TILE] + res[:, TILE:]
        res = jnp.where(left, res[:subs], res[subs:])
        binned.append(res + pltpu.roll(res, 64, 1))

    block = quarter // 2
    keep = left == ((quarter % 2) == 0)
    prec = []
    for e in range(6):
        value = jnp.where(block == 0, prec_ref[e, :, :TILE], prec_ref[e, :, TILE:])
        value = jnp.where(keep, value, 0.0)
        prec.append(value + pltpu.roll(value, 64, 1))
    sky = [
        prec[0] * binned[0] + prec[1] * binned[1] + prec[2] * binned[2],
        prec[1] * binned[0] + prec[3] * binned[1] + prec[4] * binned[2],
        prec[2] * binned[0] + prec[4] * binned[1] + prec[5] * binned[2],
    ]

    deep, wide = iota((TILE, TILE), 0), iota((TILE, TILE), 1)
    spread = jnp.where(deep == me + (wide & 64), 1.0, 0.0).astype(BF16)
    named = dot(ids, spread).astype(I32)
    back = jnp.where(named == (iota((sources, TILE), 1) & 63), 1.0, 0.0).astype(BF16)
    back = jnp.concatenate([back, back], axis=1)
    gap = jnp.zeros((64 - subs, TILE), F32)
    for c in range(3):
        first = jnp.where(left, sky[c], 0.0)
        second = jnp.where(left, 0.0, sky[c])
        high, low = split(jnp.concatenate([first, gap, second, gap], axis=0))
        out_ref[pl.ds(c, sources, stride=4), :] = dot(back, jnp.concatenate([high, low], axis=0))
    out_ref[pl.ds(3, sources, stride=4), :] = jnp.zeros((sources, TILE), F32)


def scan_kernel(
    in_ref, sky_in_ref, own_ref, out_ref, cos_ref, sin_ref, sky_ref, sum_ref, code_ref, sems
):
    copies = start_codes(in_ref, code_ref, sems)
    c, s = cos_sin(2.0 * in_ref[...])
    cos_ref[...] = c
    sin_ref[...] = s
    get_sky(sky_in_ref, sky_ref)
    sum_ref[...] = jnp.zeros_like(sum_ref)
    for copy in copies:
        copy.wait()

    def use(z, local, base, valid, hot, weight):
        res = scan_tile(hot, weight, sky_ref[place_of(z, local)])
        sum_ref[z * 8 + base] = sum_ref[z * 8 + base] + res * jnp.where(valid, 1.0, 0.0)

    each_tile(in_ref, code_ref, cos_ref, sin_ref, use)
    count = PLANES * 8
    sums = jnp.sum(jnp.sum(sum_ref[...], axis=1), axis=1, keepdims=True)
    lane, sub = iota((count, TILE), 1), iota((count, TILE), 0)
    row = jnp.sum(jnp.where(lane == sub, sums, 0.0), axis=0, keepdims=True)
    row = row * np.float32(1.0 / 1024)
    lane = iota((1, TILE), 1)
    row = jnp.where(lane < 64, row, jnp.where(lane < 80, own_ref[0:1, :], 0.0))
    over = code_ref[0, OVER]
    for z in range(1, PLANES):
        over = jnp.maximum(over, code_ref[z, OVER])
    row = jnp.where(lane == 96, over, row)
    out_ref[...] = jnp.broadcast_to(row, out_ref.shape)


def end_kernel(me_ref, in_ref, own_ref, amp_out, res_out, dir_out, over_out, keep_ref):
    dets, bases = amp_out.shape
    spans = in_ref.shape[0] // (PLANES * NEAR)
    lane = iota((NEAR, TILE), 1)
    valid = lane < PLANES * 8
    base = lane % bases
    scan, way, rest = [], [], []
    over = jnp.zeros((NEAR, TILE), F32)
    for i in range(spans):
        a = w = r = jnp.zeros((NEAR, TILE), F32)
        for z in range(PLANES):
            at = (i * PLANES + z) * NEAR
            x = in_ref[at : at + NEAR, :]
            a = a + x
            over = jnp.maximum(over, x)
            group = lane >> 3
            r = r + pltpu.roll(jnp.where(group == 8, x, 0.0), (z * 8 - 64) % TILE, 1)
            w = w + pltpu.roll(jnp.where(group == 9, x, 0.0), (z * 8 - 72) % TILE, 1)
        scan.append(a)
        way.append(w)
        rest.append(r)
    over = jnp.max(jnp.where(lane == 96, over, 0.0))
    zero = jnp.zeros((NEAR, TILE), F32)
    applied = []
    for i in range(spans):
        from_left = pltpu.roll(way[i - 1] if i else zero, TILE - (bases - 1), 1)
        from_right = pltpu.roll(way[i + 1] if i < spans - 1 else zero, bases - 1, 1)
        before = jnp.where(base == 0, from_left, pltpu.roll(way[i], 1, 1))
        after = jnp.where(base == bases - 1, from_right, pltpu.roll(way[i], TILE - 1, 1))
        v = scan[i] + way[i] + STIFFNESS * (2.0 * way[i] - before - after)
        applied.append(jnp.where(valid, v, 0.0))

    def total(terms):
        v = terms[0]
        for term in terms[1:]:
            v = v + term
        return jnp.sum(jnp.sum(v, axis=0, keepdims=True), axis=1, keepdims=True)

    now = total([r * r for r in rest])
    factor = now / total([w * a for w, a in zip(way, applied)])
    fresh = [r - factor * a for r, a in zip(rest, applied)]
    ratio = total([f * f for f in fresh]) / now
    for i in range(spans):
        keep_ref[i * NEAR : (i + 1) * NEAR, :] = fresh[i]
    mine = jnp.broadcast_to(keep_ref[pl.ds(me_ref[1] * NEAR + me_ref[0] % NEAR, 1), :], (8, TILE))
    mine = pltpu.roll(mine, (TILE - (me_ref[0] // NEAR) * 8) % TILE, 1)[0:1]
    my_way = own_ref[0:1, 72:80]
    my_fresh = mine[:, 0:8]
    moved = own_ref[1:2, 0:8] + factor * my_way
    turn = my_fresh + ratio * my_way
    for d in range(dets):
        lo, hi = d * bases, (d + 1) * bases
        amp_out[d : d + 1, :] = moved[:, lo:hi]
        res_out[d : d + 1, :] = my_fresh[:, lo:hi]
        dir_out[d : d + 1, :] = turn[:, lo:hi]
    over_out[0] = over


def slow_bin_kernel(slot_ref, dir_ref, pix_ref, ang_ref, hits_ref, out_ref, cos_ref, sin_ref, acc_ref):
    c, s = cos_sin(2.0 * ang_ref[...])
    cos_ref[...] = c
    sin_ref[...] = s
    acc_ref[...] = jnp.zeros_like(acc_ref)
    tiles = pix_ref.shape[0]
    dets, bases = dir_ref.shape
    span = tiles // dets // bases

    def group(g, carry):
        det, base = g % dets, g // dets
        height = dir_ref[det, base]
        for t in range(span):
            tile = base * span + t
            slot = slot_ref[det, tile]
            row = pl.ds(tile * dets + det, 1)
            hot, weight = tile_parts(
                pix_ref[row, :], cos_ref[row, :], sin_ref[row, :], (slot >> 1) & 1
            )
            place = (slot & 1) * (acc_ref.shape[0] // 2) + (slot >> 2)
            acc_ref[place] = acc_ref[place] + bin_tile(hot, weight) * height
        return carry

    lax.fori_loop(0, dets * bases, group, 0)

    put_bins(acc_ref, out_ref, [jnp.broadcast_to(hits_ref[...], (8, TILE))])


def slow_scan_kernel(
    slot_ref, dir_ref, res_ref, pix_ref, ang_ref, in_ref, out_ref, cos_ref, sin_ref, sky_ref, sum_ref
):
    c, s = cos_sin(2.0 * ang_ref[...])
    cos_ref[...] = c
    sin_ref[...] = s
    get_sky(in_ref, sky_ref)
    pairs = sky_ref.shape[0] // 2
    tiles = pix_ref.shape[0]
    dets, bases = dir_ref.shape
    span = tiles // dets // bases

    def group(g, carry):
        det, base = g % dets, g // dets
        total = jnp.zeros((8, TILE), F32)
        for t in range(span):
            tile = base * span + t
            slot = slot_ref[det, tile]
            row = pl.ds(tile * dets + det, 1)
            hot, weight = tile_parts(
                pix_ref[row, :], cos_ref[row, :], sin_ref[row, :], (slot >> 1) & 1
            )
            place = (slot & 1) * pairs + (slot >> 2)
            total = total + scan_tile(hot, weight, sky_ref[place])
        sum_ref[pl.ds(det * bases + base, 1), :] = jnp.sum(total, axis=0, keepdims=True)
        return carry

    lax.fori_loop(0, dets * bases, group, 0)
    count = dets * bases
    sums = jnp.sum(sum_ref[...], axis=1, keepdims=True) * np.float32(1.0 / (span * TILE))
    lane, sub = iota((count, TILE), 1), iota((count, TILE), 0)
    row = jnp.sum(jnp.where(lane == sub, sums, 0.0), axis=0, keepdims=True)
    lane = iota((1, TILE), 1)
    for d in range(dets):
        for b in range(bases):
            k = d * bases + b
            row = jnp.where(lane == count + k, dir_ref[d, b], row)
            row = jnp.where(lane == 2 * count + k, res_ref[d, b], row)
    out_ref[...] = jnp.broadcast_to(row, out_ref.shape)


def slow_end_kernel(me_ref, in_ref, amp_ref, amp_out, res_out, dir_out, keep_ref):
    rows = in_ref.shape[0]
    dets, bases = amp_ref.shape
    count = dets * bases
    owners = me_ref[2]
    x = in_ref[...]
    lane = iota((rows, TILE), 1)
    valid = lane < count
    base = lane % bases
    scan = jnp.where(valid, x, 0.0)
    way = jnp.where(valid, pltpu.roll(x, TILE - count, 1), 0.0)
    rest = jnp.where(valid, pltpu.roll(x, TILE - 2 * count, 1), 0.0)
    step = rows // 4
    zero = jnp.zeros((step, TILE), F32)
    from_left = pltpu.roll(jnp.concatenate([zero, way[:-step]], axis=0), TILE - (bases - 1), 1)
    from_right = pltpu.roll(jnp.concatenate([way[step:], zero], axis=0), bases - 1, 1)
    before = jnp.where(base == 0, from_left, pltpu.roll(way, 1, 1))
    after = jnp.where(base == bases - 1, from_right, pltpu.roll(way, TILE - 1, 1))
    applied = scan + way + STIFFNESS * (2.0 * way - before - after)
    applied = jnp.where(valid, applied, 0.0)

    def total(v):
        return jnp.sum(jnp.sum(v, axis=0, keepdims=True), axis=1, keepdims=True)

    now = total(rest * rest)
    factor = now / total(way * applied)
    fresh = rest - factor * applied
    ratio = total(fresh * fresh) / now
    keep_ref[0] = fresh
    keep_ref[1] = way
    mine = me_ref[1] * step + me_ref[0]
    my_fresh = keep_ref[0, pl.ds(mine, 1), :]
    my_way = keep_ref[1, pl.ds(mine, 1), :]
    move = factor * my_way
    turn = my_fresh + ratio * my_way
    for d in range(dets):
        lo, hi = d * bases, (d + 1) * bases
        amp_out[d : d + 1, :] = amp_ref[d : d + 1, :] + move[:, lo:hi]
        res_out[d : d + 1, :] = my_fresh[:, lo:hi]
        dir_out[d : d + 1, :] = turn[:, lo:hi]


SMEM = pl.BlockSpec(memory_space=pltpu.SMEM)
VMEM = pl.BlockSpec(memory_space=pltpu.VMEM)
SMALL = pltpu.CompilerParams(vmem_limit_bytes=12 << 20)
DET = ("z", "x", "core")
ALL = ("tm",) + DET
PLANE = ("tm", "x", "core")


def exchange(value, axes, rows):
    peers = value.shape[0] // rows
    moved = lax.all_to_all(value.reshape(peers, rows, TILE), axes, 0, 0, tiled=True)
    return moved.reshape(value.shape)


def f32(*shape):
    return jax.ShapeDtypeStruct(shape, F32)


def slow(me, amp, res, way, pix, ang, places, hits, prec):
    tiles = pix.shape[0]
    slots = hits.shape[1] * 2
    peers = 4 * hits.shape[1]
    hit_row = hits.reshape(1, slots).astype(F32)
    table = [pltpu.VMEM((tiles, TILE), F32)] * 2 + [pltpu.VMEM((slots // 2, 8, WINDOW), F32)]
    binned = pl.pallas_call(
        slow_bin_kernel,
        out_shape=f32(peers * 4, TILE),
        in_specs=[SMEM, SMEM, VMEM, VMEM, VMEM],
        out_specs=VMEM,
        scratch_shapes=table,
        name="slow_bin",
    )(places, way, pix, ang, hit_row)
    sky = solve(me, exchange(binned, ALL, 4), prec)
    last = pl.pallas_call(
        slow_scan_kernel,
        out_shape=f32(peers, TILE),
        in_specs=[SMEM, SMEM, SMEM, VMEM, VMEM, VMEM],
        out_specs=VMEM,
        scratch_shapes=table + [pltpu.VMEM((8, TILE), F32)],
        name="slow_scan",
    )(places, way, res, pix, ang, exchange(sky, ALL, 4))
    return pl.pallas_call(
        slow_end_kernel,
        out_shape=[f32(*amp.shape)] * 3,
        in_specs=[SMEM, VMEM, VMEM],
        out_specs=[VMEM] * 3,
        scratch_shapes=[pltpu.VMEM((2, peers, TILE), F32)],
        name="slow_end",
    )(me, exchange(last, ALL, 1), amp)


def solve(me, binned, prec):
    return pl.pallas_call(
        own_kernel,
        out_shape=f32(*binned.shape),
        in_specs=[SMEM, VMEM, VMEM],
        out_specs=VMEM,
        compiler_params=SMALL,
        name="own_solve",
    )(me, binned, prec)


def shards(amp, res, way, pix, ang, places, hits, prec):
    dets, samples = pix.shape
    per_det = samples // TILE
    tiles = dets * per_det
    owners = hits.shape[2]
    peers = 4 * owners

    def rows_of(v):
        return v.reshape(dets, per_det, TILE).transpose(1, 0, 2).reshape(tiles, TILE)

    pix, ang = rows_of(pix), rows_of(ang)
    hits = hits.reshape(owners, 2).T
    prec = prec.transpose(1, 0, 2)
    me = jnp.stack([lax.axis_index(DET), lax.axis_index("tm"), owners]).astype(I32)

    packed, own = pl.pallas_call(
        pack_kernel,
        out_shape=[f32(PLANES * CHUNK, TILE), f32(8, TILE)],
        in_specs=[SMEM, SMEM, SMEM, SMEM, VMEM, VMEM, VMEM],
        out_specs=[VMEM, VMEM],
        name="pack_tiles",
    )(places, way, res, amp, pix, ang, hits)
    packed = exchange(packed, "z", CHUNK)

    angles = [pltpu.VMEM((PLANES * CHUNK, TILE), F32)] * 2
    table = pltpu.VMEM((NEAR * PLANES, 8, WINDOW), F32)
    codes = [pltpu.SMEM((PLANES, TILE), F32), pltpu.SemaphoreType.DMA((PLANES,))]
    binned = pl.pallas_call(
        bin_kernel,
        out_shape=f32(peers * 4, TILE),
        in_specs=[VMEM],
        out_specs=VMEM,
        scratch_shapes=angles + [table] + codes,
        compiler_params=SMALL,
        name="bin_tiles",
    )(packed)
    sky = solve(me, exchange(binned, PLANE, 4 * PLANES), prec)
    sky = exchange(sky, PLANE, 4 * PLANES)

    last = pl.pallas_call(
        scan_kernel,
        out_shape=f32(peers, TILE),
        in_specs=[VMEM, VMEM, VMEM],
        out_specs=VMEM,
        scratch_shapes=angles + [table, pltpu.VMEM((PLANES * 8, 8, TILE), F32)] + codes,
        compiler_params=SMALL,
        name="scan_tiles",
    )(packed, sky, own)
    *out, over = pl.pallas_call(
        end_kernel,
        out_shape=[f32(*amp.shape)] * 3 + [f32(1)],
        in_specs=[SMEM, VMEM, VMEM],
        out_specs=[VMEM] * 3 + [SMEM],
        scratch_shapes=[pltpu.VMEM((4 * NEAR, TILE), F32)],
        compiler_params=SMALL,
        name="end_step",
    )(me, exchange(last, ALL, 1), own)
    return lax.cond(
        over[0] > 0,
        lambda: tuple(slow(me, amp, res, way, pix, ang, places, hits, prec)),
        lambda: tuple(out),
    )


def solution(mesh):
    spans = mesh.shape["tm"]
    split_mesh = jax.sharding.Mesh(
        mesh.devices.reshape(spans, PLANES, NEAR // 2, 2), ("tm", "z", "x", "core")
    )
    return jax.shard_map(
        shards,
        mesh=split_mesh,
        in_specs=(P(DET, "tm"),) * 6 + (P("tm", DET, None, None), P(DET, None, None)),
        out_specs=(P(DET, "tm"),) * 3,
        check_vma=False,
    )
```

```python
import jax
import jax.numpy as jnp
import numpy as np
from jax import lax
from jax.experimental import pallas as pl
from jax.experimental.pallas import tpu as pltpu
from jax.sharding import PartitionSpec as P

TILE = 128
WINDOW = 256
STIFFNESS = 0.5

ROOM = 23
CHUNK = 2 * ROOM + 2
CODES = 2 * ROOM
HITS = 2 * ROOM + 1
ANGLES = 24
COUNT = 32
OVER = 33
WAYS = 40
PLANES = 8
NEAR = 8
BF16 = jnp.bfloat16
F32 = jnp.float32
I32 = jnp.int32
NT = (((1,), (1,)), ((), ()))
NN = (((1,), (0,)), ((), ()))


def iota(shape, dim):
    return lax.broadcasted_iota(I32, shape, dim)


def dot(a, b, dims=NN):
    return lax.dot_general(a, b, dims, preferred_element_type=F32)


def split(x):
    high = x.astype(BF16)
    return high, (x - high.astype(F32)).astype(BF16)


def cos_sin(x):
    n = jnp.floor(x * np.float32(2.0 / np.pi) + 0.5)
    r = x - n * np.float32(1.5703125)
    r = r - n * np.float32(4.837512969970703e-4)
    r = r - n * np.float32(7.549789948768648e-8)
    z = r * r
    s = np.float32(-1.9515295891e-4) * z + np.float32(8.3321608736e-3)
    s = (s * z + np.float32(-1.6666654611e-1)) * z * r + r
    c = np.float32(2.443315711809948e-5) * z + np.float32(-1.388731625493765e-3)
    c = (c * z + np.float32(4.166664568298827e-2)) * z * z - 0.5 * z + 1.0
    q = n.astype(I32)
    odd = (q & 1) == 1
    cosine = jnp.where(odd, s, c)
    sine = jnp.where(odd, c, s)
    cosine = jnp.where(((q + 1) & 2) == 2, -cosine, cosine)
    sine = jnp.where((q & 2) == 2, -sine, sine)
    return cosine, sine


def tile_parts(pixels, cosine, sine, half):
    hot = iota((WINDOW, TILE), 0) == pixels
    hot = jnp.where(hot, 1.0, 0.0).astype(BF16)
    sub = iota((8, TILE), 0)
    part = sub & 3
    weight = jnp.where(part == 0, 1.0, jnp.where(part == 1, cosine, sine))
    weight = jnp.where(((sub >> 2) == half) & (part < 3), weight, 0.0)
    return hot, weight


def bin_tile(hot, weight):
    high = weight.astype(BF16).astype(F32)
    both = jnp.concatenate([high, weight - high], axis=0).astype(BF16)
    res = dot(both, hot, NT)
    return res[:8] + res[8:]


def scan_tile(hot, weight, value):
    high = value.astype(BF16).astype(F32)
    both = jnp.concatenate([high, value - high], axis=0).astype(BF16)
    res = dot(both, hot)
    return (res[:8] + res[8:]) * weight


def put_bins(acc_ref, out_ref, extra):
    pairs = acc_ref.shape[0] // 2
    left = iota((8, TILE), 1) < 64
    last = (iota((8, TILE), 0) & 3) == 3
    for u in range(pairs):
        for b in range(2):
            first = acc_ref[u, :, b * TILE : (b + 1) * TILE]
            second = acc_ref[pairs + u, :, b * TILE : (b + 1) * TILE]
            even = jnp.where(left, first, pltpu.roll(second, 64, 1))
            odd = jnp.where(left, pltpu.roll(first, 64, 1), second)
            for q, value in ((2 * b, even), (2 * b + 1, odd)):
                at = (q * pairs + u) * 8
                out_ref[at : at + 8, :] = jnp.where(last, extra[u % len(extra)], value)


def get_sky(in_ref, sky_ref):
    pairs = sky_ref.shape[0] // 2
    left = iota((8, TILE), 1) < 64
    for u in range(pairs):
        for b in range(2):
            at = (2 * b * pairs + u) * 8
            even = in_ref[at : at + 8, :]
            at = ((2 * b + 1) * pairs + u) * 8
            odd = in_ref[at : at + 8, :]
            sky_ref[u, :, b * TILE : (b + 1) * TILE] = jnp.where(left, even, pltpu.roll(odd, 64, 1))
            sky_ref[pairs + u, :, b * TILE : (b + 1) * TILE] = jnp.where(
                left, pltpu.roll(even, 64, 1), odd
            )


def pack_kernel(*refs):
    slot_ref, way_ref, res_ref, amp_ref, pix_ref, ang_ref, hits_ref = refs[9:16]
    out_ref, own_ref = refs[7:9]
    sems = refs[16]
    copies = [pltpu.make_async_copy(refs[k], refs[9 + k], sems.at[k]) for k in range(7)]
    for copy in copies:
        copy.start()
    own_ref[...] = jnp.zeros_like(own_ref)
    out_ref[...] = jnp.zeros_like(out_ref)
    for copy in copies:
        copy.wait()
    dets, bases = way_ref.shape
    per_det = slot_ref.shape[1]
    span = per_det // bases
    lane1 = iota((1, TILE), 1)
    values = jnp.zeros((1, TILE), F32)
    amps = jnp.zeros((1, TILE), F32)
    for d in range(dets):
        for b in range(bases):
            k = d * bases + b
            values = jnp.where((lane1 == WAYS + k) | (lane1 == 72 + k), way_ref[d, b], values)
            values = jnp.where(lane1 == 64 + k, res_ref[d, b], values)
            amps = jnp.where(lane1 == k, amp_ref[d, b], amps)
    own_ref[0:1, :] = values
    own_ref[1:2, :] = amps
    sub, lane = iota((PLANES, TILE), 0), iota((PLANES, TILE), 1)

    def tile_step(t, carry):
        low, high, codes = carry
        for d in range(dets):
            slot = slot_ref[d, t]
            plane = slot // (2 * NEAR)
            shift = (plane & 3) * 8
            upper = plane >> 2
            place = (jnp.where(upper == 1, high, low) >> shift) & 255
            one = jnp.left_shift(jnp.int32(1), shift)
            low = jnp.where(upper == 1, low, low + one)
            high = jnp.where(upper == 1, high + one, high)
            place = jnp.minimum(place, ROOM - 1)
            row = t * dets + d
            at = plane * CHUNK + place
            out_ref[pl.ds(at, 1), :] = ang_ref[pl.ds(row, 1), :]
            pixels = pix_ref[pl.ds(row, 1), :] ^ ((slot & 1) * 64)
            out_ref[pl.ds(at + ROOM, 1), :] = pixels.astype(F32)
            block = (slot & 1) * NEAR + ((slot >> 1) & (NEAR - 1))
            code = block * 8 + d * bases + t // span
            codes = jnp.where((sub == plane) & (lane == place), code, codes)
        return low, high, codes

    zero = jnp.int32(0)
    low, high, codes = lax.fori_loop(
        0, per_det, tile_step, (zero, zero, jnp.zeros((PLANES, TILE), I32)), unroll=4
    )
    over = zero
    for z in range(PLANES):
        count = ((high if z >= 4 else low) >> (8 * (z & 3))) & 255
        over = jnp.maximum(over, jnp.where(count > ROOM, 1, 0))
        codes = jnp.where((sub == z) & (lane == COUNT), jnp.minimum(count, ROOM), codes)
    codes = jnp.where(lane == OVER, over, codes)
    codes = jnp.where(lane < WAYS, codes.astype(F32), values)
    out_ref[pl.ds(CODES, PLANES, stride=CHUNK), :] = codes
    hits = jnp.concatenate([hits_ref[0:1, :], hits_ref[1:2, :]], axis=1).astype(F32)
    out_ref[pl.ds(HITS, PLANES, stride=CHUNK), :] = jnp.broadcast_to(hits, (PLANES, TILE))


def start_codes(in_ref, code_ref, sems):
    name_in, way_in = in_ref
    names, ways = code_ref
    copies = [
        pltpu.make_async_copy(name_in, names, sems.at[PLANES]),
    ]
    for z in range(PLANES):
        copies.append(
            pltpu.make_async_copy(
                way_in.at[pl.ds(z * CHUNK + CODES, 1), :], ways.at[pl.ds(z, 1), :], sems.at[z]
            )
        )
    for copy in copies:
        copy.start()
    return copies


def each_tile(in_ref, names, cos_ref, sin_ref, use):
    part = iota((8, TILE), 0) & 3
    first, second, real = part == 0, part == 1, part < 3
    pixel = iota((WINDOW, TILE), 0).astype(F32).astype(BF16)
    counts = [names[z, COUNT] for z in range(PLANES)]
    steps = jnp.int32(0)
    for z in range(0, PLANES, 2):
        steps = jnp.maximum(steps, (counts[z] + counts[z + 1] + 1) // 2)

    def some(g, carry):
        for k in range(PLANES):
            even = k // 2 * 2
            i = g * 2 + k % 2
            valid = i < counts[even] + counts[even + 1]
            other = i >= counts[even]
            z = even + jnp.where(other, 1, 0)
            p = jnp.minimum(jnp.where(other, i - counts[even], i), ROOM - 1)
            code = names[z, p]
            mine = in_ref[pl.ds(z * CHUNK + ROOM + p, 1), :]
            mine = jnp.broadcast_to(mine, (WINDOW, TILE)).astype(BF16)
            hot = jnp.maximum(1.0 - jnp.abs(pixel - mine), 0.0)
            row = pl.ds(z * ANGLES + p, 1)
            weight = jnp.where(first, 1.0, jnp.where(second, cos_ref[row, :], sin_ref[row, :]))
            use(z, code >> 3, code & 7, valid, hot, jnp.where(real, weight, 0.0))
        return carry

    lax.fori_loop(0, steps, some, 0)


def table_rows(z, block):
    return pl.ds(block * (4 * PLANES) + z, 4, stride=PLANES)


def bin_kernel(in_ref, name_ref, out_ref, cos_ref, sin_ref, acc_ref, names, ways, sems):
    copies = start_codes((name_ref, in_ref), (names, ways), sems)
    for z in range(PLANES):
        c, s = cos_sin(2.0 * in_ref[z * CHUNK : z * CHUNK + ANGLES, :])
        cos_ref[z * ANGLES : (z + 1) * ANGLES, :] = c
        sin_ref[z * ANGLES : (z + 1) * ANGLES, :] = s
    acc_ref[...] = jnp.zeros_like(acc_ref)
    for copy in copies:
        copy.wait()
    upper = iota((8, TILE), 0) < 4

    def use(z, block, base, valid, hot, weight):
        height = jnp.where(valid, ways[z, WAYS + base], 0.0)
        high = weight.astype(BF16).astype(F32)
        both = jnp.where(upper, high, weight - high).astype(BF16)
        res = dot(both, hot, NT)
        rows = table_rows(z, block)
        for b in range(2):
            cols = slice(b * TILE, (b + 1) * TILE)
            acc_ref[b, rows, :] = acc_ref[b, rows, :] + (res[:4, cols] + res[4:, cols]) * height

    each_tile(in_ref, names, cos_ref, sin_ref, use)
    left = iota((8, TILE), 1) < 64
    hits = in_ref[pl.ds(HITS, PLANES, stride=CHUNK), :]
    for xc in range(NEAR):
        for c in range(4):
            for b in range(2):
                first = acc_ref[b, (xc * 4 + c) * 8 : (xc * 4 + c + 1) * 8, :]
                second = acc_ref[b, ((NEAR + xc) * 4 + c) * 8 : ((NEAR + xc) * 4 + c + 1) * 8, :]
                for h, value in (
                    (0, jnp.where(left, first, second)),
                    (1, jnp.where(left, second, first)),
                ):
                    at = (((2 * b + h) * NEAR + xc) * 4 + c) * 8
                    out_ref[at : at + 8, :] = hits if c == 3 else value


def own_kernel(me_ref, in_ref, prec_ref, out_ref):
    peers = in_ref.shape[0]
    sources = peers * PLANES

    def take(c):
        return in_ref[:, c * PLANES : (c + 1) * PLANES, :].reshape(sources, TILE)

    def put(c, value):
        out_ref[:, c * PLANES : (c + 1) * PLANES, :] = value.reshape(peers, PLANES, TILE)

    own_solve(me_ref[0], me_ref[1], sources, take, prec_ref, put, 1)


def slow_own_kernel(me_ref, in_ref, prec_ref, out_ref):
    sources = in_ref.shape[0] // 4

    def take(c):
        return in_ref[pl.ds(c, sources, stride=4), :]

    def put(c, value):
        out_ref[pl.ds(c, sources, stride=4), :] = value

    own_solve(me_ref[0], me_ref[1], sources, take, prec_ref, put, 0)
    put(3, jnp.zeros((sources, TILE), F32))


def own_solve(me, quarter, sources, take, prec_ref, put, swap):
    odd = (quarter % 2) * swap
    subs = prec_ref.shape[1]
    ids = take(3).astype(BF16)
    lane = iota((16, TILE), 1)
    row = iota((16, TILE), 0)
    pick = jnp.where((lane == me + 64 * (row ^ odd)) & (row < 2), 1.0, 0.0).astype(BF16)
    id_rows = dot(pick, ids, NT).astype(I32)
    sub = iota((subs, sources), 0)
    hot = jnp.concatenate(
        [
            jnp.where(sub == id_rows[0:1, :], 1.0, 0.0),
            jnp.where(sub == id_rows[1:2, :], 1.0, 0.0),
        ],
        axis=0,
    ).astype(BF16)
    left = iota((subs, TILE), 1) < 64
    binned = []
    for c in range(3):
        high, low = split(take(c))
        res = dot(hot, jnp.concatenate([high, low], axis=1))
        res = res[:, :TILE] + res[:, TILE:]
        res = jnp.where(left, res[:subs], res[subs:])
        binned.append(res + pltpu.roll(res, 64, 1))

    block = quarter // 2
    keep = left == ((quarter % 2) == 0)
    prec = []
    for e in range(6):
        value = jnp.where(block == 0, prec_ref[e, :, :TILE], prec_ref[e, :, TILE:])
        value = jnp.where(keep, value, 0.0)
        prec.append(value + pltpu.roll(value, 64, 1))
    sky = [
        prec[0] * binned[0] + prec[1] * binned[1] + prec[2] * binned[2],
        prec[1] * binned[0] + prec[3] * binned[1] + prec[4] * binned[2],
        prec[2] * binned[0] + prec[4] * binned[1] + prec[5] * binned[2],
    ]

    deep, wide = iota((TILE, TILE), 0), iota((TILE, TILE), 1)
    spread = jnp.where(deep == me + ((wide & 64) ^ (64 * odd)), 1.0, 0.0).astype(BF16)
    named = dot(ids, spread).astype(I32)
    back = jnp.where(named == (iota((sources, TILE), 1) & 63), 1.0, 0.0).astype(BF16)
    back = jnp.concatenate([back, back], axis=1)
    gap = jnp.zeros((64 - subs, TILE), F32)
    for c in range(3):
        first = jnp.where(left, sky[c], 0.0)
        second = jnp.where(left, 0.0, sky[c])
        high, low = split(jnp.concatenate([first, gap, second, gap], axis=0))
        put(c, dot(back, jnp.concatenate([high, low], axis=0)))


def scan_kernel(
    in_ref, name_ref, cos_ref, sin_ref, sky_in_ref, own_ref, out_ref, sky_ref, sum_ref, names, sems
):
    copy = pltpu.make_async_copy(name_ref, names, sems.at[0])
    copy.start()
    left = iota((8, TILE), 1) < 64
    for xc in range(NEAR):
        for c in range(3):
            for b in range(2):
                at = ((2 * b * NEAR + xc) * 3 + c) * 8
                even = sky_in_ref[at : at + 8, :]
                at = (((2 * b + 1) * NEAR + xc) * 3 + c) * 8
                odd = sky_in_ref[at : at + 8, :]
                at = (xc * 4 + c) * 8
                sky_ref[b, at : at + 8, :] = jnp.where(left, even, odd)
                at = ((NEAR + xc) * 4 + c) * 8
                sky_ref[b, at : at + 8, :] = jnp.where(left, odd, even)
    for block in range(2 * NEAR):
        at = (block * 4 + 3) * 8
        for b in range(2):
            sky_ref[b, at : at + 8, :] = jnp.zeros((8, TILE), F32)
    sum_ref[...] = jnp.zeros_like(sum_ref)
    copy.wait()

    def use(z, block, base, valid, hot, weight):
        rows = table_rows(z, block)
        value = jnp.concatenate([sky_ref[0, rows, :], sky_ref[1, rows, :]], axis=1)
        high = value.astype(BF16).astype(F32)
        both = jnp.concatenate([high, value - high], axis=0).astype(BF16)
        res = dot(both, hot) * weight
        at = z * 8 + base
        sum_ref[at] = sum_ref[at] + res * jnp.where(valid, 1.0, 0.0)

    each_tile(in_ref, names, cos_ref, sin_ref, use)
    count = PLANES * 8
    sums = jnp.sum(jnp.sum(sum_ref[...], axis=1), axis=1, keepdims=True)
    lane, sub = iota((count, TILE), 1), iota((count, TILE), 0)
    row = jnp.sum(jnp.where(lane == sub, sums, 0.0), axis=0, keepdims=True)
    row = row * np.float32(1.0 / 1024)
    lane = iota((1, TILE), 1)
    row = jnp.where(lane < 64, row, jnp.where(lane < 80, own_ref[0:1, :], 0.0))
    over = names[0, OVER]
    for z in range(1, PLANES):
        over = jnp.maximum(over, names[z, OVER])
    row = jnp.where(lane == 96, over.astype(F32), row)
    out_ref[...] = jnp.broadcast_to(row, out_ref.shape)


def end_kernel(me_ref, in_ref, own_ref, amp_out, res_out, dir_out, over_out, keep_ref):
    dets, bases = amp_out.shape
    spans = in_ref.shape[0] // (PLANES * NEAR)
    lane = iota((NEAR, TILE), 1)
    valid = lane < PLANES * 8
    base = lane % bases
    scan, way, rest = [], [], []
    over = jnp.zeros((NEAR, TILE), F32)
    for i in range(spans):
        a = w = r = jnp.zeros((NEAR, TILE), F32)
        for z in range(PLANES):
            at = (i * PLANES + z) * NEAR
            x = in_ref[at : at + NEAR, :]
            a = a + x
            over = jnp.maximum(over, x)
            group = lane >> 3
            r = r + pltpu.roll(jnp.where(group == 8, x, 0.0), (z * 8 - 64) % TILE, 1)
            w = w + pltpu.roll(jnp.where(group == 9, x, 0.0), (z * 8 - 72) % TILE, 1)
        scan.append(a)
        way.append(w)
        rest.append(r)
    over = jnp.max(jnp.where(lane == 96, over, 0.0))
    zero = jnp.zeros((NEAR, TILE), F32)
    applied = []
    for i in range(spans):
        from_left = pltpu.roll(way[i - 1] if i else zero, TILE - (bases - 1), 1)
        from_right = pltpu.roll(way[i + 1] if i < spans - 1 else zero, bases - 1, 1)
        before = jnp.where(base == 0, from_left, pltpu.roll(way[i], 1, 1))
        after = jnp.where(base == bases - 1, from_right, pltpu.roll(way[i], TILE - 1, 1))
        v = scan[i] + way[i] + STIFFNESS * (2.0 * way[i] - before - after)
        applied.append(jnp.where(valid, v, 0.0))

    def total(terms):
        v = terms[0]
        for term in terms[1:]:
            v = v + term
        return jnp.sum(jnp.sum(v, axis=0, keepdims=True), axis=1, keepdims=True)

    now = total([r * r for r in rest])
    factor = now / total([w * a for w, a in zip(way, applied)])
    fresh = [r - factor * a for r, a in zip(rest, applied)]
    ratio = total([f * f for f in fresh]) / now
    for i in range(spans):
        keep_ref[i * NEAR : (i + 1) * NEAR, :] = fresh[i]
    mine = jnp.broadcast_to(keep_ref[pl.ds(me_ref[1] * NEAR + me_ref[0] % NEAR, 1), :], (8, TILE))
    mine = pltpu.roll(mine, (TILE - (me_ref[0] // NEAR) * 8) % TILE, 1)[0:1]
    my_way = own_ref[0:1, 72:80]
    my_fresh = mine[:, 0:8]
    moved = own_ref[1:2, 0:8] + factor * my_way
    turn = my_fresh + ratio * my_way
    for d in range(dets):
        lo, hi = d * bases, (d + 1) * bases
        amp_out[d : d + 1, :] = moved[:, lo:hi]
        res_out[d : d + 1, :] = my_fresh[:, lo:hi]
        dir_out[d : d + 1, :] = turn[:, lo:hi]
    over_out[0] = over


def slow_bin_kernel(slot_ref, dir_ref, pix_ref, ang_ref, hits_ref, out_ref, cos_ref, sin_ref, acc_ref):
    c, s = cos_sin(2.0 * ang_ref[...])
    cos_ref[...] = c
    sin_ref[...] = s
    acc_ref[...] = jnp.zeros_like(acc_ref)
    tiles = pix_ref.shape[0]
    dets, bases = dir_ref.shape
    span = tiles // dets // bases

    def group(g, carry):
        det, base = g % dets, g // dets
        height = dir_ref[det, base]
        for t in range(span):
            tile = base * span + t
            slot = slot_ref[det, tile]
            row = pl.ds(tile * dets + det, 1)
            hot, weight = tile_parts(
                pix_ref[row, :], cos_ref[row, :], sin_ref[row, :], (slot >> 1) & 1
            )
            place = (slot & 1) * (acc_ref.shape[0] // 2) + (slot >> 2)
            acc_ref[place] = acc_ref[place] + bin_tile(hot, weight) * height
        return carry

    lax.fori_loop(0, dets * bases, group, 0)

    put_bins(acc_ref, out_ref, [jnp.broadcast_to(hits_ref[...], (8, TILE))])


def slow_scan_kernel(
    slot_ref, dir_ref, res_ref, pix_ref, ang_ref, in_ref, out_ref, cos_ref, sin_ref, sky_ref, sum_ref
):
    c, s = cos_sin(2.0 * ang_ref[...])
    cos_ref[...] = c
    sin_ref[...] = s
    get_sky(in_ref, sky_ref)
    pairs = sky_ref.shape[0] // 2
    tiles = pix_ref.shape[0]
    dets, bases = dir_ref.shape
    span = tiles // dets // bases

    def group(g, carry):
        det, base = g % dets, g // dets
        total = jnp.zeros((8, TILE), F32)
        for t in range(span):
            tile = base * span + t
            slot = slot_ref[det, tile]
            row = pl.ds(tile * dets + det, 1)
            hot, weight = tile_parts(
                pix_ref[row, :], cos_ref[row, :], sin_ref[row, :], (slot >> 1) & 1
            )
            place = (slot & 1) * pairs + (slot >> 2)
            total = total + scan_tile(hot, weight, sky_ref[place])
        sum_ref[pl.ds(det * bases + base, 1), :] = jnp.sum(total, axis=0, keepdims=True)
        return carry

    lax.fori_loop(0, dets * bases, group, 0)
    count = dets * bases
    sums = jnp.sum(sum_ref[...], axis=1, keepdims=True) * np.float32(1.0 / (span * TILE))
    lane, sub = iota((count, TILE), 1), iota((count, TILE), 0)
    row = jnp.sum(jnp.where(lane == sub, sums, 0.0), axis=0, keepdims=True)
    lane = iota((1, TILE), 1)
    for d in range(dets):
        for b in range(bases):
            k = d * bases + b
            row = jnp.where(lane == count + k, dir_ref[d, b], row)
            row = jnp.where(lane == 2 * count + k, res_ref[d, b], row)
    out_ref[...] = jnp.broadcast_to(row, out_ref.shape)


def slow_end_kernel(me_ref, in_ref, amp_ref, amp_out, res_out, dir_out, keep_ref):
    rows = in_ref.shape[0]
    dets, bases = amp_ref.shape
    count = dets * bases
    owners = me_ref[2]
    x = in_ref[...]
    lane = iota((rows, TILE), 1)
    valid = lane < count
    base = lane % bases
    scan = jnp.where(valid, x, 0.0)
    way = jnp.where(valid, pltpu.roll(x, TILE - count, 1), 0.0)
    rest = jnp.where(valid, pltpu.roll(x, TILE - 2 * count, 1), 0.0)
    step = rows // 4
    zero = jnp.zeros((step, TILE), F32)
    from_left = pltpu.roll(jnp.concatenate([zero, way[:-step]], axis=0), TILE - (bases - 1), 1)
    from_right = pltpu.roll(jnp.concatenate([way[step:], zero], axis=0), bases - 1, 1)
    before = jnp.where(base == 0, from_left, pltpu.roll(way, 1, 1))
    after = jnp.where(base == bases - 1, from_right, pltpu.roll(way, TILE - 1, 1))
    applied = scan + way + STIFFNESS * (2.0 * way - before - after)
    applied = jnp.where(valid, applied, 0.0)

    def total(v):
        return jnp.sum(jnp.sum(v, axis=0, keepdims=True), axis=1, keepdims=True)

    now = total(rest * rest)
    factor = now / total(way * applied)
    fresh = rest - factor * applied
    ratio = total(fresh * fresh) / now
    keep_ref[0] = fresh
    keep_ref[1] = way
    mine = me_ref[1] * step + me_ref[0]
    my_fresh = keep_ref[0, pl.ds(mine, 1), :]
    my_way = keep_ref[1, pl.ds(mine, 1), :]
    move = factor * my_way
    turn = my_fresh + ratio * my_way
    for d in range(dets):
        lo, hi = d * bases, (d + 1) * bases
        amp_out[d : d + 1, :] = amp_ref[d : d + 1, :] + move[:, lo:hi]
        res_out[d : d + 1, :] = my_fresh[:, lo:hi]
        dir_out[d : d + 1, :] = turn[:, lo:hi]


SMEM = pl.BlockSpec(memory_space=pltpu.SMEM)
VMEM = pl.BlockSpec(memory_space=pltpu.VMEM)
SMALL = pltpu.CompilerParams(vmem_limit_bytes=12 << 20)
DET = ("z", "x", "core")
ALL = ("tm",) + DET
PLANE = ("tm", "x", "core")


def exchange(value, axes, rows):
    peers = value.shape[0] // rows
    moved = lax.all_to_all(value.reshape(peers, rows, TILE), axes, 0, 0, tiled=True)
    return moved.reshape(value.shape)


def f32(*shape):
    return jax.ShapeDtypeStruct(shape, F32)


def slow(me, amp, res, way, pix, ang, places, hits, prec):
    tiles = pix.shape[0]
    slots = hits.shape[1] * 2
    peers = 4 * hits.shape[1]
    hit_row = hits.reshape(1, slots).astype(F32)
    table = [pltpu.VMEM((tiles, TILE), F32)] * 2 + [pltpu.VMEM((slots // 2, 8, WINDOW), F32)]
    binned = pl.pallas_call(
        slow_bin_kernel,
        out_shape=f32(peers * 4, TILE),
        in_specs=[SMEM, SMEM, VMEM, VMEM, VMEM],
        out_specs=VMEM,
        scratch_shapes=table,
        name="slow_bin",
    )(places, way, pix, ang, hit_row)
    sky = solve(slow_own_kernel, (me, exchange(binned, ALL, 4), prec), peers * 4)
    last = pl.pallas_call(
        slow_scan_kernel,
        out_shape=f32(peers, TILE),
        in_specs=[SMEM, SMEM, SMEM, VMEM, VMEM, VMEM],
        out_specs=VMEM,
        scratch_shapes=table + [pltpu.VMEM((8, TILE), F32)],
        name="slow_scan",
    )(places, way, res, pix, ang, exchange(sky, ALL, 4))
    return pl.pallas_call(
        slow_end_kernel,
        out_shape=[f32(*amp.shape)] * 3,
        in_specs=[SMEM, VMEM, VMEM],
        out_specs=[VMEM] * 3,
        scratch_shapes=[pltpu.VMEM((2, peers, TILE), F32)],
        name="slow_end",
    )(me, exchange(last, ALL, 1), amp)


def solve(kernel, args, *shape):
    shape = shape + (TILE,)
    return pl.pallas_call(
        kernel,
        out_shape=f32(*shape),
        in_specs=[SMEM, VMEM, VMEM],
        out_specs=VMEM,
        compiler_params=SMALL,
        name=kernel.__name__,
    )(*args)


def shards(amp, res, way, pix, ang, places, hits, prec):
    dets, samples = pix.shape
    per_det = samples // TILE
    tiles = dets * per_det
    owners = hits.shape[2]
    peers = 4 * owners
    near = 4 * NEAR

    def rows_of(v):
        return v.reshape(dets, per_det, TILE).transpose(1, 0, 2).reshape(tiles, TILE)

    pix, ang = rows_of(pix), rows_of(ang)
    hits = hits.reshape(owners, 2).T
    prec = prec.transpose(1, 0, 2)
    me = jnp.stack([lax.axis_index(DET), lax.axis_index("tm"), owners]).astype(I32)

    packed, own = pl.pallas_call(
        pack_kernel,
        out_shape=[f32(PLANES * CHUNK, TILE), f32(8, TILE)],
        in_specs=[pl.BlockSpec(memory_space=pltpu.HBM)] * 7,
        out_specs=[VMEM, VMEM],
        scratch_shapes=[
            pltpu.SMEM(places.shape, I32),
            pltpu.SMEM(way.shape, F32),
            pltpu.SMEM(way.shape, F32),
            pltpu.SMEM(way.shape, F32),
            pltpu.VMEM((tiles, TILE), I32),
            pltpu.VMEM((tiles, TILE), F32),
            pltpu.VMEM(hits.shape, I32),
            pltpu.SemaphoreType.DMA((7,)),
        ],
        compiler_params=SMALL,
        name="pack_tiles",
    )(places, way, res, amp, pix, ang, hits)
    packed = exchange(packed, "z", CHUNK)

    table = pltpu.VMEM((2, 2 * NEAR * 4 * PLANES, TILE), F32)
    names = packed.reshape(PLANES, CHUNK, TILE)[:, CODES].astype(I32)
    sems = pltpu.SemaphoreType.DMA((PLANES + 1,))
    binned, cosine, sine = pl.pallas_call(
        bin_kernel,
        out_shape=[f32(near * 4 * PLANES, TILE)] + [f32(PLANES * ANGLES, TILE)] * 2,
        in_specs=[VMEM] * 2,
        out_specs=[VMEM] * 3,
        scratch_shapes=[
            table,
            pltpu.SMEM((PLANES, TILE), I32),
            pltpu.SMEM((PLANES, TILE), F32),
            sems,
        ],
        compiler_params=SMALL,
        name="bin_tiles",
    )(packed, names)
    binned = exchange(binned, PLANE, 4 * PLANES).reshape(near, 4 * PLANES, TILE)
    sky = solve(own_kernel, (me, binned, prec), near, 3 * PLANES)
    sky = exchange(sky.reshape(near * 3 * PLANES, TILE), PLANE, 3 * PLANES)

    last = pl.pallas_call(
        scan_kernel,
        out_shape=f32(peers, TILE),
        in_specs=[VMEM] * 6,
        out_specs=VMEM,
        scratch_shapes=[
            table,
            pltpu.VMEM((PLANES * 8, 8, TILE), F32),
            pltpu.SMEM((PLANES, TILE), I32),
            sems,
        ],
        compiler_params=SMALL,
        name="scan_tiles",
    )(packed, names, cosine, sine, sky, own)
    *out, over = pl.pallas_call(
        end_kernel,
        out_shape=[f32(*amp.shape)] * 3 + [f32(1)],
        in_specs=[SMEM, VMEM, VMEM],
        out_specs=[VMEM] * 3 + [SMEM],
        scratch_shapes=[pltpu.VMEM((4 * NEAR, TILE), F32)],
        compiler_params=SMALL,
        name="end_step",
    )(me, exchange(last, ALL, 1), own)
    return lax.cond(
        over[0] > 0,
        lambda: tuple(slow(me, amp, res, way, pix, ang, places, hits, prec)),
        lambda: tuple(out),
    )


def solution(mesh):
    spans = mesh.shape["tm"]
    split_mesh = jax.sharding.Mesh(
        mesh.devices.reshape(spans, PLANES, NEAR // 2, 2), ("tm", "z", "x", "core")
    )
    return jax.shard_map(
        shards,
        mesh=split_mesh,
        in_specs=(P(DET, "tm"),) * 6 + (P("tm", DET, None, None), P(DET, None, None)),
        out_specs=(P(DET, "tm"),) * 3,
        check_vma=False,
    )
```

```python
import jax
import jax.numpy as jnp
import numpy as np
from jax import lax
from jax.experimental import pallas as pl
from jax.experimental.pallas import tpu as pltpu
from jax.sharding import PartitionSpec as P

TILE = 128
WINDOW = 256
STIFFNESS = 0.5

ROOM = 23
CHUNK = 2 * ROOM + 2
CODES = 2 * ROOM
HITS = 2 * ROOM + 1
ANGLES = 24
GROUP = 4
PER_STEP = 8
COUNT = 32
OVER = 33
WAYS = 40
PLANES = 8
NEAR = 8
BF16 = jnp.bfloat16
F32 = jnp.float32
I32 = jnp.int32
NT = (((1,), (1,)), ((), ()))
NN = (((1,), (0,)), ((), ()))


def iota(shape, dim):
    return lax.broadcasted_iota(I32, shape, dim)


def dot(a, b, dims=NN):
    return lax.dot_general(a, b, dims, preferred_element_type=F32)


def split(x):
    high = x.astype(BF16)
    return high, (x - high.astype(F32)).astype(BF16)


def cos_sin(x):
    n = jnp.floor(x * np.float32(2.0 / np.pi) + 0.5)
    r = x - n * np.float32(1.5703125)
    r = r - n * np.float32(4.837512969970703e-4)
    r = r - n * np.float32(7.549789948768648e-8)
    z = r * r
    s = np.float32(-1.9515295891e-4) * z + np.float32(8.3321608736e-3)
    s = (s * z + np.float32(-1.6666654611e-1)) * z * r + r
    c = np.float32(2.443315711809948e-5) * z + np.float32(-1.388731625493765e-3)
    c = (c * z + np.float32(4.166664568298827e-2)) * z * z - 0.5 * z + 1.0
    q = n.astype(I32)
    odd = (q & 1) == 1
    cosine = jnp.where(odd, s, c)
    sine = jnp.where(odd, c, s)
    cosine = jnp.where(((q + 1) & 2) == 2, -cosine, cosine)
    sine = jnp.where((q & 2) == 2, -sine, sine)
    return cosine, sine


def tile_parts(pixels, cosine, sine, half):
    hot = iota((WINDOW, TILE), 0) == pixels
    hot = jnp.where(hot, 1.0, 0.0).astype(BF16)
    sub = iota((8, TILE), 0)
    part = sub & 3
    weight = jnp.where(part == 0, 1.0, jnp.where(part == 1, cosine, sine))
    weight = jnp.where(((sub >> 2) == half) & (part < 3), weight, 0.0)
    return hot, weight


def bin_tile(hot, weight):
    high = weight.astype(BF16).astype(F32)
    both = jnp.concatenate([high, weight - high], axis=0).astype(BF16)
    res = dot(both, hot, NT)
    return res[:8] + res[8:]


def scan_tile(hot, weight, value):
    high = value.astype(BF16).astype(F32)
    both = jnp.concatenate([high, value - high], axis=0).astype(BF16)
    res = dot(both, hot)
    return (res[:8] + res[8:]) * weight


def put_bins(acc_ref, out_ref, extra):
    pairs = acc_ref.shape[0] // 2
    left = iota((8, TILE), 1) < 64
    last = (iota((8, TILE), 0) & 3) == 3
    for u in range(pairs):
        for b in range(2):
            first = acc_ref[u, :, b * TILE : (b + 1) * TILE]
            second = acc_ref[pairs + u, :, b * TILE : (b + 1) * TILE]
            even = jnp.where(left, first, pltpu.roll(second, 64, 1))
            odd = jnp.where(left, pltpu.roll(first, 64, 1), second)
            for q, value in ((2 * b, even), (2 * b + 1, odd)):
                at = (q * pairs + u) * 8
                out_ref[at : at + 8, :] = jnp.where(last, extra[u % len(extra)], value)


def get_sky(in_ref, sky_ref):
    pairs = sky_ref.shape[0] // 2
    left = iota((8, TILE), 1) < 64
    for u in range(pairs):
        for b in range(2):
            at = (2 * b * pairs + u) * 8
            even = in_ref[at : at + 8, :]
            at = ((2 * b + 1) * pairs + u) * 8
            odd = in_ref[at : at + 8, :]
            sky_ref[u, :, b * TILE : (b + 1) * TILE] = jnp.where(left, even, pltpu.roll(odd, 64, 1))
            sky_ref[pairs + u, :, b * TILE : (b + 1) * TILE] = jnp.where(
                left, pltpu.roll(even, 64, 1), odd
            )


def coded(number):
    base = number & 7
    return (number >> 3) * 128 + (base >> 2) + (base & 3) * 16


def pack_kernel(*refs):
    slot_ref, way_ref, res_ref, amp_ref, pix_ref, ang_ref, hits_ref = refs[9:16]
    out_ref, own_ref = refs[7:9]
    sems = refs[16]
    copies = [pltpu.make_async_copy(refs[k], refs[9 + k], sems.at[k]) for k in range(7)]
    for copy in copies:
        copy.start()
    own_ref[...] = jnp.zeros_like(own_ref)
    out_ref[...] = jnp.zeros_like(out_ref)
    for copy in copies:
        copy.wait()
    dets, bases = way_ref.shape
    per_det = slot_ref.shape[1]
    lane1 = iota((1, TILE), 1)
    values = jnp.zeros((1, TILE), F32)
    amps = jnp.zeros((1, TILE), F32)
    for d in range(dets):
        for b in range(bases):
            k = d * bases + b
            values = jnp.where((lane1 == WAYS + k) | (lane1 == 72 + k), way_ref[d, b], values)
            values = jnp.where(lane1 == 64 + k, res_ref[d, b], values)
            amps = jnp.where(lane1 == k, amp_ref[d, b], amps)
    own_ref[0:1, :] = values
    own_ref[1:2, :] = amps
    sub, lane = iota((PLANES, TILE), 0), iota((PLANES, TILE), 1)
    pix = pix_ref[...]
    pix_ref[...] = ((pix & 192) << 1) + (pix & 63)

    def tile_step(t, carry):
        low, high, codes = carry
        for d in range(dets):
            slot = slot_ref[d, t]
            plane = slot // (2 * NEAR)
            shift = (plane & 3) * 8
            upper = plane >> 2
            place = (jnp.where(upper == 1, high, low) >> shift) & 255
            one = jnp.left_shift(jnp.int32(1), shift)
            low = jnp.where(upper == 1, low, low + one)
            high = jnp.where(upper == 1, high + one, high)
            place = jnp.minimum(place, ROOM - 1)
            row = t * dets + d
            at = plane * CHUNK + place
            out_ref[pl.ds(at, 1), :] = ang_ref[pl.ds(row, 1), :]
            pixels = pix_ref[pl.ds(row, 1), :] + (slot & 1) * 64
            out_ref[pl.ds(at + ROOM, 1), :] = pixels.astype(F32)
            codes = jnp.where((sub == plane) & (lane == place), slot * 64 + row, codes)
        return low, high, codes

    zero = jnp.int32(0)
    low, high, codes = lax.fori_loop(
        0, per_det, tile_step, (zero, zero, jnp.zeros((PLANES, TILE), I32)), unroll=4
    )
    over = zero
    for z in range(PLANES):
        count = ((high if z >= 4 else low) >> (8 * (z & 3))) & 255
        over = jnp.maximum(over, jnp.where(count > ROOM, 1, 0))
        codes = jnp.where((sub == z) & (lane == COUNT), coded(jnp.minimum(count, ROOM)), codes)
    codes = jnp.where(lane == OVER, coded(over), codes)
    codes = jnp.where(lane < WAYS, codes.astype(F32), values)
    out_ref[pl.ds(CODES, PLANES, stride=CHUNK), :] = codes
    hits = jnp.concatenate([hits_ref[0:1, :], hits_ref[1:2, :]], axis=1).astype(F32)
    out_ref[pl.ds(HITS, PLANES, stride=CHUNK), :] = jnp.broadcast_to(hits, (PLANES, TILE))


def start_codes(in_ref, code_ref, sems):
    name_in, way_in = in_ref
    names, ways = code_ref
    copies = [
        pltpu.make_async_copy(name_in, names, sems.at[PLANES]),
    ]
    for z in range(PLANES):
        copies.append(
            pltpu.make_async_copy(
                way_in.at[pl.ds(z * CHUNK + CODES, 1), :], ways.at[pl.ds(z, 1), :], sems.at[z]
            )
        )
    for copy in copies:
        copy.start()
    return copies


def each_pair(in_ref, names, cos_ref, sin_ref, use):
    part, quarter = iota((16, TILE), 0) & 3, iota((16, TILE), 0) >> 2
    first, second = part == 0, part == 1
    quarter = jnp.where(part < 3, quarter, -1)
    pixel = iota((TILE, TILE), 0).astype(F32).astype(BF16)
    counts = [names[z, COUNT] for z in range(PLANES)]
    ends = []
    for z in range(PLANES):
        ends.append(counts[z] if z % GROUP == 0 else ends[-1] + counts[z])
    steps = jnp.int32(0)
    for z in range(GROUP - 1, PLANES, GROUP):
        steps = jnp.maximum(steps, (ends[z] + PER_STEP - 1) // PER_STEP)

    def tile(group, i):
        low = group * GROUP
        z, start = jnp.int32(low), jnp.int32(0)
        for k in range(GROUP - 1):
            z = z + jnp.where(i >= ends[low + k], 1, 0)
            start = jnp.where(i >= ends[low + k], ends[low + k], start)
        p = jnp.minimum(i - start, ROOM - 1)
        code = names[z, p]
        mine = in_ref[pl.ds(z * CHUNK + ROOM + p, 1), :].astype(I32)
        place = jnp.broadcast_to((mine & 127).astype(F32), (TILE, TILE)).astype(BF16)
        hot = jnp.maximum(1.0 - jnp.abs(pixel - place), 0.0)
        row = pl.ds(z * ANGLES + p, 1)
        weight = jnp.where(first, 1.0, jnp.where(second, cos_ref[row, :], sin_ref[row, :]))
        weight = jnp.where(quarter == (mine >> 7), weight, 0.0)
        return (z, code >> 3, code & 7, i < ends[low + GROUP - 1]), hot, weight

    def some(g, carry):
        for group in range(PLANES // GROUP):
            for k in range(0, PER_STEP, 2):
                use(*zip(*(tile(group, g * PER_STEP + k + n) for n in range(2))))
        return carry

    lax.fori_loop(0, steps, some, 0)


def table_rows(q, owner, z):
    return pl.ds((q * NEAR + owner) * (4 * PLANES) + z, 4, stride=PLANES)


def halves(x):
    high, low = split(x)
    return jnp.concatenate([high, low], axis=0)


def bin_kernel(in_ref, name_ref, out_ref, cos_ref, sin_ref, names, ways, sems):
    copies = start_codes((name_ref, in_ref), (names, ways), sems)
    for z in range(PLANES):
        c, s = cos_sin(2.0 * in_ref[z * CHUNK : z * CHUNK + ANGLES, :])
        cos_ref[z * ANGLES : (z + 1) * ANGLES, :] = c
        sin_ref[z * ANGLES : (z + 1) * ANGLES, :] = s
    hits = in_ref[pl.ds(HITS, PLANES, stride=CHUNK), :]
    for at in range(0, out_ref.shape[0], PLANES):
        last = at // PLANES % 4 == 3
        out_ref[at : at + PLANES, :] = hits if last else jnp.zeros((PLANES, TILE), F32)
    for copy in copies:
        copy.wait()

    def use(tiles, hots, weights):
        both = jnp.concatenate([halves(weight) for weight in weights], axis=0)
        res = dot(both, jnp.concatenate(hots, axis=0), NT)
        for n, (z, owner, base, valid) in enumerate(tiles):
            height = jnp.where(valid, ways[z, WAYS + base], 0.0)
            mine = res[32 * n : 32 * n + 32, n * TILE : (n + 1) * TILE]
            mine = (mine[:16] + mine[16:]) * height
            for q in range(4):
                rows = table_rows(q, owner, z)
                out_ref[rows, :] = out_ref[rows, :] + mine[4 * q : 4 * q + 4]

    each_pair(in_ref, names, cos_ref, sin_ref, use)


def own_kernel(me_ref, in_ref, prec_ref, out_ref):
    peers = in_ref.shape[0]
    sources = peers * PLANES

    def take(c):
        return in_ref[:, c * PLANES : (c + 1) * PLANES, :].reshape(sources, TILE)

    def put(c, value):
        out_ref[:, c * PLANES : (c + 1) * PLANES, :] = value.reshape(peers, PLANES, TILE)

    own_solve(me_ref[0], me_ref[1], sources, take, prec_ref, put)


def slow_own_kernel(me_ref, in_ref, prec_ref, out_ref):
    sources = in_ref.shape[0] // 4

    def take(c):
        return in_ref[pl.ds(c, sources, stride=4), :]

    def put(c, value):
        out_ref[pl.ds(c, sources, stride=4), :] = value

    own_solve(me_ref[0], me_ref[1], sources, take, prec_ref, put)
    put(3, jnp.zeros((sources, TILE), F32))


def own_solve(me, quarter, sources, take, prec_ref, put):
    subs = prec_ref.shape[1]
    ids = take(3).astype(BF16)
    lane = iota((16, TILE), 1)
    row = iota((16, TILE), 0)
    pick = jnp.where((lane == me + 64 * row) & (row < 2), 1.0, 0.0).astype(BF16)
    id_rows = dot(pick, ids, NT).astype(I32)
    sub = iota((subs, sources), 0)
    hot = jnp.concatenate(
        [
            jnp.where(sub == id_rows[0:1, :], 1.0, 0.0),
            jnp.where(sub == id_rows[1:2, :], 1.0, 0.0),
        ],
        axis=0,
    ).astype(BF16)
    left = iota((subs, TILE), 1) < 64
    binned = []
    for c in range(3):
        high, low = split(take(c))
        res = dot(hot, jnp.concatenate([high, low], axis=1))
        res = res[:, :TILE] + res[:, TILE:]
        res = jnp.where(left, res[:subs], res[subs:])
        binned.append(res + pltpu.roll(res, 64, 1))

    block = quarter // 2
    keep = left == ((quarter % 2) == 0)
    prec = []
    for e in range(6):
        value = jnp.where(block == 0, prec_ref[e, :, :TILE], prec_ref[e, :, TILE:])
        value = jnp.where(keep, value, 0.0)
        prec.append(value + pltpu.roll(value, 64, 1))
    sky = [
        prec[0] * binned[0] + prec[1] * binned[1] + prec[2] * binned[2],
        prec[1] * binned[0] + prec[3] * binned[1] + prec[4] * binned[2],
        prec[2] * binned[0] + prec[4] * binned[1] + prec[5] * binned[2],
    ]

    deep, wide = iota((TILE, TILE), 0), iota((TILE, TILE), 1)
    spread = jnp.where(deep == me + (wide & 64), 1.0, 0.0).astype(BF16)
    named = dot(ids, spread).astype(I32)
    back = jnp.where(named == (iota((sources, TILE), 1) & 63), 1.0, 0.0).astype(BF16)
    back = jnp.concatenate([back, back], axis=1)
    gap = jnp.zeros((64 - subs, TILE), F32)
    for c in range(3):
        first = jnp.where(left, sky[c], 0.0)
        second = jnp.where(left, 0.0, sky[c])
        high, low = split(jnp.concatenate([first, gap, second, gap], axis=0))
        put(c, dot(back, jnp.concatenate([high, low], axis=0)))


def scan_kernel(
    in_ref, name_ref, cos_ref, sin_ref, sky_in_ref, own_ref, out_ref, sky_ref, sum_ref, names, sems
):
    copy = pltpu.make_async_copy(name_ref, names, sems.at[0])
    copy.start()
    for peer in range(4 * NEAR):
        for c in range(4):
            at = (peer * 4 + c) * PLANES
            here = (peer * 3 + c) * PLANES
            sky_ref[at : at + PLANES, :] = (
                sky_in_ref[here : here + PLANES, :] if c < 3 else jnp.zeros((PLANES, TILE), F32)
            )
    sum_ref[...] = jnp.zeros_like(sum_ref)
    copy.wait()

    def use(tiles, hots, weights):
        both = []
        for z, owner, _, _ in tiles:
            value = [sky_ref[table_rows(q, owner, z), :] for q in range(4)]
            both.append(halves(jnp.concatenate(value, axis=0)))
        res = dot(jnp.concatenate(both, axis=0), jnp.concatenate(hots, axis=1))
        for n, (z, _, base, valid) in enumerate(tiles):
            mine = res[32 * n : 32 * n + 32, n * TILE : (n + 1) * TILE]
            mine = (mine[:16] + mine[16:]) * weights[n]
            at = z * 8 + base
            sum_ref[at] = sum_ref[at] + (mine[:8] + mine[8:]) * jnp.where(valid, 1.0, 0.0)

    each_pair(in_ref, names, cos_ref, sin_ref, use)
    count = PLANES * 8
    sums = jnp.sum(jnp.sum(sum_ref[...], axis=1), axis=1, keepdims=True)
    lane, sub = iota((count, TILE), 1), iota((count, TILE), 0)
    row = jnp.sum(jnp.where(lane == sub, sums, 0.0), axis=0, keepdims=True)
    row = row * np.float32(1.0 / 1024)
    lane = iota((1, TILE), 1)
    row = jnp.where(lane < 64, row, jnp.where(lane < 80, own_ref[0:1, :], 0.0))
    over = names[0, OVER]
    for z in range(1, PLANES):
        over = jnp.maximum(over, names[z, OVER])
    row = jnp.where(lane == 96, over.astype(F32), row)
    out_ref[...] = jnp.broadcast_to(row, out_ref.shape)


def end_kernel(me_ref, in_ref, own_ref, amp_out, res_out, dir_out, over_out, keep_ref):
    dets, bases = amp_out.shape
    spans = in_ref.shape[0] // (PLANES * NEAR)
    lane = iota((NEAR, TILE), 1)
    valid = lane < PLANES * 8
    base = lane % bases
    scan, way, rest = [], [], []
    over = jnp.zeros((NEAR, TILE), F32)
    for i in range(spans):
        a = w = r = jnp.zeros((NEAR, TILE), F32)
        for z in range(PLANES):
            at = (i * PLANES + z) * NEAR
            x = in_ref[at : at + NEAR, :]
            a = a + x
            over = jnp.maximum(over, x)
            group = lane >> 3
            r = r + pltpu.roll(jnp.where(group == 8, x, 0.0), (z * 8 - 64) % TILE, 1)
            w = w + pltpu.roll(jnp.where(group == 9, x, 0.0), (z * 8 - 72) % TILE, 1)
        scan.append(a)
        way.append(w)
        rest.append(r)
    over = jnp.max(jnp.where(lane == 96, over, 0.0))
    zero = jnp.zeros((NEAR, TILE), F32)
    applied = []
    for i in range(spans):
        from_left = pltpu.roll(way[i - 1] if i else zero, TILE - (bases - 1), 1)
        from_right = pltpu.roll(way[i + 1] if i < spans - 1 else zero, bases - 1, 1)
        before = jnp.where(base == 0, from_left, pltpu.roll(way[i], 1, 1))
        after = jnp.where(base == bases - 1, from_right, pltpu.roll(way[i], TILE - 1, 1))
        v = scan[i] + way[i] + STIFFNESS * (2.0 * way[i] - before - after)
        applied.append(jnp.where(valid, v, 0.0))

    def total(terms):
        v = terms[0]
        for term in terms[1:]:
            v = v + term
        return jnp.sum(jnp.sum(v, axis=0, keepdims=True), axis=1, keepdims=True)

    now = total([r * r for r in rest])
    factor = now / total([w * a for w, a in zip(way, applied)])
    fresh = [r - factor * a for r, a in zip(rest, applied)]
    ratio = total([f * f for f in fresh]) / now
    for i in range(spans):
        keep_ref[i * NEAR : (i + 1) * NEAR, :] = fresh[i]
    mine = jnp.broadcast_to(keep_ref[pl.ds(me_ref[1] * NEAR + me_ref[0] % NEAR, 1), :], (8, TILE))
    mine = pltpu.roll(mine, (TILE - (me_ref[0] // NEAR) * 8) % TILE, 1)[0:1]
    my_way = own_ref[0:1, 72:80]
    my_fresh = mine[:, 0:8]
    moved = own_ref[1:2, 0:8] + factor * my_way
    turn = my_fresh + ratio * my_way
    for d in range(dets):
        lo, hi = d * bases, (d + 1) * bases
        amp_out[d : d + 1, :] = moved[:, lo:hi]
        res_out[d : d + 1, :] = my_fresh[:, lo:hi]
        dir_out[d : d + 1, :] = turn[:, lo:hi]
    over_out[0] = over


def slow_bin_kernel(slot_ref, dir_ref, pix_ref, ang_ref, hits_ref, out_ref, cos_ref, sin_ref, acc_ref):
    c, s = cos_sin(2.0 * ang_ref[...])
    cos_ref[...] = c
    sin_ref[...] = s
    acc_ref[...] = jnp.zeros_like(acc_ref)
    tiles = pix_ref.shape[0]
    dets, bases = dir_ref.shape
    span = tiles // dets // bases

    def group(g, carry):
        det, base = g % dets, g // dets
        height = dir_ref[det, base]
        for t in range(span):
            tile = base * span + t
            slot = slot_ref[det, tile]
            row = pl.ds(tile * dets + det, 1)
            hot, weight = tile_parts(
                pix_ref[row, :], cos_ref[row, :], sin_ref[row, :], (slot >> 1) & 1
            )
            place = (slot & 1) * (acc_ref.shape[0] // 2) + (slot >> 2)
            acc_ref[place] = acc_ref[place] + bin_tile(hot, weight) * height
        return carry

    lax.fori_loop(0, dets * bases, group, 0)

    put_bins(acc_ref, out_ref, [jnp.broadcast_to(hits_ref[...], (8, TILE))])


def slow_scan_kernel(
    slot_ref, dir_ref, res_ref, pix_ref, ang_ref, in_ref, out_ref, cos_ref, sin_ref, sky_ref, sum_ref
):
    c, s = cos_sin(2.0 * ang_ref[...])
    cos_ref[...] = c
    sin_ref[...] = s
    get_sky(in_ref, sky_ref)
    pairs = sky_ref.shape[0] // 2
    tiles = pix_ref.shape[0]
    dets, bases = dir_ref.shape
    span = tiles // dets // bases

    def group(g, carry):
        det, base = g % dets, g // dets
        total = jnp.zeros((8, TILE), F32)
        for t in range(span):
            tile = base * span + t
            slot = slot_ref[det, tile]
            row = pl.ds(tile * dets + det, 1)
            hot, weight = tile_parts(
                pix_ref[row, :], cos_ref[row, :], sin_ref[row, :], (slot >> 1) & 1
            )
            place = (slot & 1) * pairs + (slot >> 2)
            total = total + scan_tile(hot, weight, sky_ref[place])
        sum_ref[pl.ds(det * bases + base, 1), :] = jnp.sum(total, axis=0, keepdims=True)
        return carry

    lax.fori_loop(0, dets * bases, group, 0)
    count = dets * bases
    sums = jnp.sum(sum_ref[...], axis=1, keepdims=True) * np.float32(1.0 / (span * TILE))
    lane, sub = iota((count, TILE), 1), iota((count, TILE), 0)
    row = jnp.sum(jnp.where(lane == sub, sums, 0.0), axis=0, keepdims=True)
    lane = iota((1, TILE), 1)
    for d in range(dets):
        for b in range(bases):
            k = d * bases + b
            row = jnp.where(lane == count + k, dir_ref[d, b], row)
            row = jnp.where(lane == 2 * count + k, res_ref[d, b], row)
    out_ref[...] = jnp.broadcast_to(row, out_ref.shape)


def slow_end_kernel(me_ref, in_ref, amp_ref, amp_out, res_out, dir_out, keep_ref):
    rows = in_ref.shape[0]
    dets, bases = amp_ref.shape
    count = dets * bases
    owners = me_ref[2]
    x = in_ref[...]
    lane = iota((rows, TILE), 1)
    valid = lane < count
    base = lane % bases
    scan = jnp.where(valid, x, 0.0)
    way = jnp.where(valid, pltpu.roll(x, TILE - count, 1), 0.0)
    rest = jnp.where(valid, pltpu.roll(x, TILE - 2 * count, 1), 0.0)
    step = rows // 4
    zero = jnp.zeros((step, TILE), F32)
    from_left = pltpu.roll(jnp.concatenate([zero, way[:-step]], axis=0), TILE - (bases - 1), 1)
    from_right = pltpu.roll(jnp.concatenate([way[step:], zero], axis=0), bases - 1, 1)
    before = jnp.where(base == 0, from_left, pltpu.roll(way, 1, 1))
    after = jnp.where(base == bases - 1, from_right, pltpu.roll(way, TILE - 1, 1))
    applied = scan + way + STIFFNESS * (2.0 * way - before - after)
    applied = jnp.where(valid, applied, 0.0)

    def total(v):
        return jnp.sum(jnp.sum(v, axis=0, keepdims=True), axis=1, keepdims=True)

    now = total(rest * rest)
    factor = now / total(way * applied)
    fresh = rest - factor * applied
    ratio = total(fresh * fresh) / now
    keep_ref[0] = fresh
    keep_ref[1] = way
    mine = me_ref[1] * step + me_ref[0]
    my_fresh = keep_ref[0, pl.ds(mine, 1), :]
    my_way = keep_ref[1, pl.ds(mine, 1), :]
    move = factor * my_way
    turn = my_fresh + ratio * my_way
    for d in range(dets):
        lo, hi = d * bases, (d + 1) * bases
        amp_out[d : d + 1, :] = amp_ref[d : d + 1, :] + move[:, lo:hi]
        res_out[d : d + 1, :] = my_fresh[:, lo:hi]
        dir_out[d : d + 1, :] = turn[:, lo:hi]


SMEM = pl.BlockSpec(memory_space=pltpu.SMEM)
VMEM = pl.BlockSpec(memory_space=pltpu.VMEM)
SMALL = pltpu.CompilerParams(vmem_limit_bytes=12 << 20)
DET = ("z", "x", "core")
ALL = ("tm",) + DET
PLANE = ("tm", "x", "core")


def exchange(value, axes, rows):
    peers = value.shape[0] // rows
    moved = lax.all_to_all(value.reshape(peers, rows, TILE), axes, 0, 0, tiled=True)
    return moved.reshape(value.shape)


def f32(*shape):
    return jax.ShapeDtypeStruct(shape, F32)


def slow(me, amp, res, way, pix, ang, places, hits, prec):
    tiles = pix.shape[0]
    slots = hits.shape[1] * 2
    peers = 4 * hits.shape[1]
    hit_row = hits.reshape(1, slots).astype(F32)
    table = [pltpu.VMEM((tiles, TILE), F32)] * 2 + [pltpu.VMEM((slots // 2, 8, WINDOW), F32)]
    binned = pl.pallas_call(
        slow_bin_kernel,
        out_shape=f32(peers * 4, TILE),
        in_specs=[SMEM, SMEM, VMEM, VMEM, VMEM],
        out_specs=VMEM,
        scratch_shapes=table,
        name="slow_bin",
    )(places, way, pix, ang, hit_row)
    sky = solve(slow_own_kernel, (me, exchange(binned, ALL, 4), prec), peers * 4)
    last = pl.pallas_call(
        slow_scan_kernel,
        out_shape=f32(peers, TILE),
        in_specs=[SMEM, SMEM, SMEM, VMEM, VMEM, VMEM],
        out_specs=VMEM,
        scratch_shapes=table + [pltpu.VMEM((8, TILE), F32)],
        name="slow_scan",
    )(places, way, res, pix, ang, exchange(sky, ALL, 4))
    return pl.pallas_call(
        slow_end_kernel,
        out_shape=[f32(*amp.shape)] * 3,
        in_specs=[SMEM, VMEM, VMEM],
        out_specs=[VMEM] * 3,
        scratch_shapes=[pltpu.VMEM((2, peers, TILE), F32)],
        name="slow_end",
    )(me, exchange(last, ALL, 1), amp)


def solve(kernel, args, *shape):
    shape = shape + (TILE,)
    return pl.pallas_call(
        kernel,
        out_shape=f32(*shape),
        in_specs=[SMEM, VMEM, VMEM],
        out_specs=VMEM,
        compiler_params=SMALL,
        name=kernel.__name__,
    )(*args)


def shards(amp, res, way, pix, ang, places, hits, prec):
    dets, samples = pix.shape
    per_det = samples // TILE
    tiles = dets * per_det
    owners = hits.shape[2]
    peers = 4 * owners
    near = 4 * NEAR

    def rows_of(v):
        return v.reshape(dets, per_det, TILE).transpose(1, 0, 2).reshape(tiles, TILE)

    pix, ang = rows_of(pix), rows_of(ang)
    hits = hits.reshape(owners, 2).T
    prec = prec.transpose(1, 0, 2)
    me = jnp.stack([lax.axis_index(DET), lax.axis_index("tm"), owners]).astype(I32)

    me, places = lax.optimization_barrier((me, places))
    packed, own = pl.pallas_call(
        pack_kernel,
        out_shape=[f32(PLANES * CHUNK, TILE), f32(8, TILE)],
        in_specs=[pl.BlockSpec(memory_space=pltpu.HBM)] * 7,
        out_specs=[VMEM, VMEM],
        scratch_shapes=[
            pltpu.SMEM(places.shape, I32),
            pltpu.SMEM(way.shape, F32),
            pltpu.SMEM(way.shape, F32),
            pltpu.SMEM(way.shape, F32),
            pltpu.VMEM((tiles, TILE), I32),
            pltpu.VMEM((tiles, TILE), F32),
            pltpu.VMEM(hits.shape, I32),
            pltpu.SemaphoreType.DMA((7,)),
        ],
        compiler_params=SMALL,
        name="pack_tiles",
    )(places, way, res, amp, pix, ang, hits)
    packed = exchange(packed, "z", CHUNK)

    raw = packed.reshape(PLANES, CHUNK, TILE)[:, CODES].astype(I32)
    slot, row = raw >> 6, raw & 63
    base = row % dets * way.shape[1] + row // (tiles // way.shape[1])
    names = (slot // 2 % NEAR) * 8 + base
    sems = pltpu.SemaphoreType.DMA((PLANES + 1,))
    binned, cosine, sine = pl.pallas_call(
        bin_kernel,
        out_shape=[f32(near * 4 * PLANES, TILE)] + [f32(PLANES * ANGLES, TILE)] * 2,
        in_specs=[VMEM] * 2,
        out_specs=[VMEM] * 3,
        scratch_shapes=[
            pltpu.SMEM((PLANES, TILE), I32),
            pltpu.SMEM((PLANES, TILE), F32),
            sems,
        ],
        compiler_params=SMALL,
        name="bin_tiles",
    )(packed, names)
    binned = exchange(binned, PLANE, 4 * PLANES).reshape(near, 4 * PLANES, TILE)
    sky = solve(own_kernel, (me, binned, prec), near, 3 * PLANES)
    sky = exchange(sky.reshape(near * 3 * PLANES, TILE), PLANE, 3 * PLANES)

    last = pl.pallas_call(
        scan_kernel,
        out_shape=f32(peers, TILE),
        in_specs=[VMEM] * 6,
        out_specs=VMEM,
        scratch_shapes=[
            pltpu.VMEM((near * 4 * PLANES, TILE), F32),
            pltpu.VMEM((PLANES * 8, 8, TILE), F32),
            pltpu.SMEM((PLANES, TILE), I32),
            sems,
        ],
        compiler_params=SMALL,
        name="scan_tiles",
    )(packed, names, cosine, sine, sky, own)
    *out, over = pl.pallas_call(
        end_kernel,
        out_shape=[f32(*amp.shape)] * 3 + [f32(1)],
        in_specs=[SMEM, VMEM, VMEM],
        out_specs=[VMEM] * 3 + [SMEM],
        scratch_shapes=[pltpu.VMEM((4 * NEAR, TILE), F32)],
        compiler_params=SMALL,
        name="end_step",
    )(me, exchange(last, ALL, 1), own)
    return lax.cond(
        over[0] > 0,
        lambda: tuple(slow(me, amp, res, way, pix, ang, places, hits, prec)),
        lambda: tuple(out),
    )


def solution(mesh):
    spans = mesh.shape["tm"]
    split_mesh = jax.sharding.Mesh(
        mesh.devices.reshape(spans, PLANES, NEAR // 2, 2), ("tm", "z", "x", "core")
    )
    return jax.shard_map(
        shards,
        mesh=split_mesh,
        in_specs=(P(DET, "tm"),) * 6 + (P("tm", DET, None, None), P(DET, None, None)),
        out_specs=(P(DET, "tm"),) * 3,
        check_vma=False,
    )
```

```python
import jax
import jax.numpy as jnp
import numpy as np
from jax import lax
from jax.experimental import pallas as pl
from jax.experimental.pallas import tpu as pltpu
from jax.sharding import PartitionSpec as P

TILE = 128
WINDOW = 256
STIFFNESS = 0.5

ROOM = 23
CHUNK = 2 * ROOM + 2
CODES = 2 * ROOM
HITS = 2 * ROOM + 1
ANGLES = 24
GROUP = 4
PER_STEP = 8
COUNT = 32
OVER = 33
HERE = 34
WAYS = 40
PLANES = 8
NEAR = 8
BINS = 3 * PLANES + 1
BF16 = jnp.bfloat16
F32 = jnp.float32
I32 = jnp.int32
NT = (((1,), (1,)), ((), ()))
NN = (((1,), (0,)), ((), ()))


def iota(shape, dim):
    return lax.broadcasted_iota(I32, shape, dim)


def dot(a, b, dims=NN):
    return lax.dot_general(a, b, dims, preferred_element_type=F32)


def split(x):
    high = x.astype(BF16)
    return high, (x - high.astype(F32)).astype(BF16)


def cos_sin(x):
    n = jnp.floor(x * np.float32(2.0 / np.pi) + 0.5)
    r = x - n * np.float32(1.5703125)
    r = r - n * np.float32(4.837512969970703e-4)
    r = r - n * np.float32(7.549789948768648e-8)
    z = r * r
    s = np.float32(-1.9515295891e-4) * z + np.float32(8.3321608736e-3)
    s = (s * z + np.float32(-1.6666654611e-1)) * z * r + r
    c = np.float32(2.443315711809948e-5) * z + np.float32(-1.388731625493765e-3)
    c = (c * z + np.float32(4.166664568298827e-2)) * z * z - 0.5 * z + 1.0
    q = n.astype(I32)
    odd = (q & 1) == 1
    cosine = jnp.where(odd, s, c)
    sine = jnp.where(odd, c, s)
    cosine = jnp.where(((q + 1) & 2) == 2, -cosine, cosine)
    sine = jnp.where((q & 2) == 2, -sine, sine)
    return cosine, sine


def tile_parts(pixels, cosine, sine, half):
    hot = iota((WINDOW, TILE), 0) == pixels
    hot = jnp.where(hot, 1.0, 0.0).astype(BF16)
    sub = iota((8, TILE), 0)
    part = sub & 3
    weight = jnp.where(part == 0, 1.0, jnp.where(part == 1, cosine, sine))
    weight = jnp.where(((sub >> 2) == half) & (part < 3), weight, 0.0)
    return hot, weight


def bin_tile(hot, weight):
    high = weight.astype(BF16).astype(F32)
    both = jnp.concatenate([high, weight - high], axis=0).astype(BF16)
    res = dot(both, hot, NT)
    return res[:8] + res[8:]


def scan_tile(hot, weight, value):
    high = value.astype(BF16).astype(F32)
    both = jnp.concatenate([high, value - high], axis=0).astype(BF16)
    res = dot(both, hot)
    return (res[:8] + res[8:]) * weight


def put_bins(acc_ref, out_ref, extra):
    pairs = acc_ref.shape[0] // 2
    left = iota((8, TILE), 1) < 64
    last = (iota((8, TILE), 0) & 3) == 3
    for u in range(pairs):
        for b in range(2):
            first = acc_ref[u, :, b * TILE : (b + 1) * TILE]
            second = acc_ref[pairs + u, :, b * TILE : (b + 1) * TILE]
            even = jnp.where(left, first, pltpu.roll(second, 64, 1))
            odd = jnp.where(left, pltpu.roll(first, 64, 1), second)
            for q, value in ((2 * b, even), (2 * b + 1, odd)):
                at = (q * pairs + u) * 8
                out_ref[at : at + 8, :] = jnp.where(last, extra[u % len(extra)], value)


def get_sky(in_ref, sky_ref):
    pairs = sky_ref.shape[0] // 2
    left = iota((8, TILE), 1) < 64
    for u in range(pairs):
        for b in range(2):
            at = (2 * b * pairs + u) * 8
            even = in_ref[at : at + 8, :]
            at = ((2 * b + 1) * pairs + u) * 8
            odd = in_ref[at : at + 8, :]
            sky_ref[u, :, b * TILE : (b + 1) * TILE] = jnp.where(left, even, pltpu.roll(odd, 64, 1))
            sky_ref[pairs + u, :, b * TILE : (b + 1) * TILE] = jnp.where(
                left, pltpu.roll(even, 64, 1), odd
            )


def coded(number):
    base = number & 7
    return (number >> 3) * 128 + (base >> 2) + (base & 3) * 16


def pack_kernel(*refs):
    operands, (out_ref, own_ref), kept = refs[:7], refs[7:9], refs[9:16]
    slot_ref, way_ref, res_ref, amp_ref, pixel_ref, next_ref, sems = refs[16:]
    pix_ref, ang_ref, hits_ref = kept[4:]
    targets = kept + (slot_ref, way_ref, res_ref, amp_ref)
    copies = [
        pltpu.make_async_copy(operands[k % 7], target, sems.at[k])
        for k, target in enumerate(targets)
    ]
    for copy in copies:
        copy.start()
    own_ref[...] = jnp.zeros_like(own_ref)
    out_ref[...] = jnp.zeros_like(out_ref)
    for z in range(PLANES):
        next_ref[z] = z * CHUNK
    for copy in copies:
        copy.wait()
    dets, bases = way_ref.shape
    per_det = slot_ref.shape[1]
    lane1 = iota((1, TILE), 1)
    values = jnp.zeros((1, TILE), F32)
    amps = jnp.zeros((1, TILE), F32)
    for d in range(dets):
        for b in range(bases):
            k = d * bases + b
            values = jnp.where((lane1 == WAYS + k) | (lane1 == 72 + k), way_ref[d, b], values)
            values = jnp.where(lane1 == 64 + k, res_ref[d, b], values)
            amps = jnp.where(lane1 == k, amp_ref[d, b], amps)
    own_ref[0:1, :] = values
    own_ref[1:2, :] = amps
    sub, lane = iota((PLANES, TILE), 0), iota((PLANES, TILE), 1)
    at_row = sub * CHUNK + lane
    pix = pix_ref[...]
    pixel_ref[...] = ((pix & 192) << 1) + (pix & 63)

    def tile_step(t, codes):
        for d in range(dets):
            slot = slot_ref[d, t]
            plane = slot // (2 * NEAR)
            at = next_ref[plane]
            next_ref[plane] = at + 1
            at = jnp.minimum(at, out_ref.shape[0] - ROOM - 1)
            row = t * dets + d
            out_ref[pl.ds(at, 1), :] = ang_ref[pl.ds(row, 1), :]
            pixels = pixel_ref[pl.ds(row, 1), :] + (slot & 1) * 64
            out_ref[pl.ds(at + ROOM, 1), :] = pixels.astype(F32)
            codes = jnp.where(at_row == at, slot * 64 + row, codes)
        return codes

    codes = lax.fori_loop(0, per_det, tile_step, jnp.zeros((PLANES, TILE), I32), unroll=4)
    over = jnp.int32(0)
    for z in range(PLANES):
        count = next_ref[z] - z * CHUNK
        over = jnp.maximum(over, jnp.where(count > ROOM, 1, 0))
        codes = jnp.where((sub == z) & (lane == COUNT), coded(jnp.minimum(count, ROOM)), codes)
    codes = jnp.where(lane == OVER, coded(over), codes)
    codes = jnp.where(lane == HERE, coded(sub), codes)
    codes = jnp.where(lane < WAYS, codes.astype(F32), values)
    out_ref[pl.ds(CODES, PLANES, stride=CHUNK), :] = codes
    hits = jnp.concatenate([hits_ref[0:1, :], hits_ref[1:2, :]], axis=1).astype(F32)
    out_ref[pl.ds(HITS, PLANES, stride=CHUNK), :] = jnp.broadcast_to(hits, (PLANES, TILE))


def start_codes(in_ref, code_ref, sems):
    name_in, way_in = in_ref
    names, ways = code_ref
    copies = [
        pltpu.make_async_copy(name_in, names, sems.at[PLANES]),
    ]
    for z in range(PLANES):
        copies.append(
            pltpu.make_async_copy(
                way_in.at[pl.ds(z * CHUNK + CODES, 1), :], ways.at[pl.ds(z, 1), :], sems.at[z]
            )
        )
    for copy in copies:
        copy.start()
    return copies


def each_pair(in_ref, names, cos_ref, sin_ref, use):
    part, quarter = iota((16, TILE), 0) & 3, iota((16, TILE), 0) >> 2
    first, second = part == 0, part == 1
    quarter = jnp.where(part < 3, quarter, -1)
    pixel = iota((TILE, TILE), 0).astype(F32).astype(BF16)
    counts = [names[z, COUNT] for z in range(PLANES)]
    ends = []
    for z in range(PLANES):
        ends.append(counts[z] if z % GROUP == 0 else ends[-1] + counts[z])
    steps = jnp.int32(0)
    for z in range(GROUP - 1, PLANES, GROUP):
        steps = jnp.maximum(steps, (ends[z] + PER_STEP - 1) // PER_STEP)

    def tile(group, i):
        low = group * GROUP
        z, start = jnp.int32(low), jnp.int32(0)
        for k in range(GROUP - 1):
            z = z + jnp.where(i >= ends[low + k], 1, 0)
            start = jnp.where(i >= ends[low + k], ends[low + k], start)
        p = jnp.minimum(i - start, ROOM - 1)
        code = names[z, p]
        mine = in_ref[pl.ds(z * CHUNK + ROOM + p, 1), :].astype(I32)
        place = jnp.broadcast_to((mine & 127).astype(F32), (TILE, TILE)).astype(BF16)
        hot = jnp.maximum(1.0 - jnp.abs(pixel - place), 0.0)
        row = pl.ds(z * ANGLES + p, 1)
        weight = jnp.where(first, 1.0, jnp.where(second, cos_ref[row, :], sin_ref[row, :]))
        weight = jnp.where(quarter == (mine >> 7), weight, 0.0)
        return (z, code >> 3, code & 7, i < ends[low + GROUP - 1]), hot, weight

    def some(g, carry):
        for group in range(PLANES // GROUP):
            for k in range(0, PER_STEP, 2):
                use(*zip(*(tile(group, g * PER_STEP + k + n) for n in range(2))))
        return carry

    lax.fori_loop(0, steps, some, 0)


def table_rows(q, owner, z, chunk, count):
    return pl.ds((q * NEAR + owner) * chunk + z, count, stride=PLANES)


def halves(x):
    high, low = split(x)
    return jnp.concatenate([high, low], axis=0)


def bin_kernel(in_ref, name_ref, out_ref, cos_ref, sin_ref, names, ways, sems):
    copies = start_codes((name_ref, in_ref), (names, ways), sems)
    for z in range(PLANES):
        c, s = cos_sin(2.0 * in_ref[z * CHUNK : z * CHUNK + ANGLES, :])
        cos_ref[z * ANGLES : (z + 1) * ANGLES, :] = c
        sin_ref[z * ANGLES : (z + 1) * ANGLES, :] = s
    out_ref[...] = jnp.zeros_like(out_ref)
    for copy in copies:
        copy.wait()
    hits = in_ref[pl.ds(HITS, PLANES, stride=CHUNK), :].astype(BF16)
    lane, deep = iota((TILE, TILE), 1), iota((TILE, TILE), 0)
    here = (lane & 1) * 64 + names[0, HERE] * NEAR + ((lane >> 1) & (NEAR - 1))
    moved = dot(hits, jnp.where(deep == here, 1.0, 0.0).astype(BF16))
    moved = jnp.where(iota((PLANES, TILE), 1) >> 4 == iota((PLANES, TILE), 0), moved, 0.0)
    moved = jnp.sum(moved, axis=0, keepdims=True)
    for at in range(BINS - 1, out_ref.shape[0], BINS):
        out_ref[at : at + 1, :] = moved

    def use(tiles, hots, weights):
        both = jnp.concatenate([halves(weight) for weight in weights], axis=0)
        res = dot(both, jnp.concatenate(hots, axis=0), NT)
        for n, (z, owner, base, valid) in enumerate(tiles):
            height = jnp.where(valid, ways[z, WAYS + base], 0.0)
            mine = res[32 * n : 32 * n + 32, n * TILE : (n + 1) * TILE]
            mine = (mine[:16] + mine[16:]) * height
            for q in range(4):
                rows = table_rows(q, owner, z, BINS, 3)
                out_ref[rows, :] = out_ref[rows, :] + mine[4 * q : 4 * q + 3]

    each_pair(in_ref, names, cos_ref, sin_ref, use)


def own_kernel(me_ref, in_ref, prec_ref, out_ref):
    peers = in_ref.shape[0] // BINS
    sources = peers * PLANES
    owner = me_ref[0:1, :] & (NEAR - 1)

    def take(c):
        if c < 3:
            at = [w * BINS + c * PLANES for w in range(peers)]
            return jnp.concatenate([in_ref[a : a + PLANES, :] for a in at], axis=0)
        mine = iota((PLANES, TILE), 1) >> 4 == iota((PLANES, TILE), 0)
        at = [w * BINS + BINS - 1 for w in range(peers)]
        return jnp.concatenate([jnp.where(mine, in_ref[a : a + 1, :], 0.0) for a in at], axis=0)

    def put(c, value):
        out_ref[:, c * PLANES : (c + 1) * PLANES, :] = value.reshape(peers, PLANES, TILE)

    def place(lane, k):
        return (lane & 15) == 2 * owner + k

    own_solve(place, me_ref[1:2, :], sources, take, prec_ref, put)


def slow_own_kernel(me_ref, in_ref, prec_ref, out_ref):
    sources = in_ref.shape[0] // 4

    def take(c):
        return in_ref[pl.ds(c, sources, stride=4), :]

    def put(c, value):
        out_ref[pl.ds(c, sources, stride=4), :] = value

    def place(lane, k):
        return lane == me_ref[0:1, :] + 64 * k

    own_solve(place, me_ref[1:2, :], sources, take, prec_ref, put)
    put(3, jnp.zeros((sources, TILE), F32))


def own_solve(place, quarter, sources, take, prec_ref, put):
    subs = prec_ref.shape[1]
    ids = take(3).astype(BF16)
    lane = iota((16, TILE), 1)
    row = iota((16, TILE), 0)
    pick = jnp.where(place(lane, row) & (row < 2), 1.0, 0.0).astype(BF16)
    id_rows = dot(pick, ids, NT).astype(I32)
    sub = iota((subs, sources), 0)
    hot = jnp.concatenate(
        [
            jnp.where(sub == id_rows[0:1, :], 1.0, 0.0),
            jnp.where(sub == id_rows[1:2, :], 1.0, 0.0),
        ],
        axis=0,
    ).astype(BF16)
    left = iota((subs, TILE), 1) < 64
    binned = []
    for c in range(3):
        high, low = split(take(c))
        res = dot(hot, jnp.concatenate([high, low], axis=1))
        res = res[:, :TILE] + res[:, TILE:]
        res = jnp.where(left, res[:subs], res[subs:])
        binned.append(res + pltpu.roll(res, 64, 1))

    quarter = jnp.broadcast_to(quarter, (subs, TILE))
    keep = (iota((subs, TILE), 1) >> 6) == (quarter & 1)
    block = quarter >> 1
    prec = []
    for e in range(6):
        value = jnp.where(block == 0, prec_ref[e, :, :TILE], prec_ref[e, :, TILE:])
        value = jnp.where(keep, value, 0.0)
        prec.append(value + pltpu.roll(value, 64, 1))
    sky = [
        prec[0] * binned[0] + prec[1] * binned[1] + prec[2] * binned[2],
        prec[1] * binned[0] + prec[3] * binned[1] + prec[4] * binned[2],
        prec[2] * binned[0] + prec[4] * binned[1] + prec[5] * binned[2],
    ]

    deep, wide = iota((TILE, TILE), 0), iota((TILE, TILE), 1)
    spread = jnp.where(place(deep, wide >> 6), 1.0, 0.0).astype(BF16)
    named = dot(ids, spread).astype(I32)
    back = jnp.where(named == (iota((sources, TILE), 1) & 63), 1.0, 0.0).astype(BF16)
    back = jnp.concatenate([back, back], axis=1)
    gap = jnp.zeros((64 - subs, TILE), F32)
    for c in range(3):
        first = jnp.where(left, sky[c], 0.0)
        second = jnp.where(left, 0.0, sky[c])
        high, low = split(jnp.concatenate([first, gap, second, gap], axis=0))
        put(c, dot(back, jnp.concatenate([high, low], axis=0)))


def scan_kernel(
    in_ref, name_ref, cos_ref, sin_ref, sky_in_ref, own_ref, out_ref, sky_ref, sum_ref, names, sems
):
    copy = pltpu.make_async_copy(name_ref, names, sems.at[0])
    copy.start()
    for peer in range(4 * NEAR):
        for c in range(4):
            at = (peer * 4 + c) * PLANES
            here = (peer * 3 + c) * PLANES
            sky_ref[at : at + PLANES, :] = (
                sky_in_ref[here : here + PLANES, :] if c < 3 else jnp.zeros((PLANES, TILE), F32)
            )
    sum_ref[...] = jnp.zeros_like(sum_ref)
    copy.wait()

    def use(tiles, hots, weights):
        both = []
        for z, owner, _, _ in tiles:
            value = [sky_ref[table_rows(q, owner, z, 4 * PLANES, 4), :] for q in range(4)]
            both.append(halves(jnp.concatenate(value, axis=0)))
        res = dot(jnp.concatenate(both, axis=0), jnp.concatenate(hots, axis=1))
        for n, (z, _, base, valid) in enumerate(tiles):
            mine = res[32 * n : 32 * n + 32, n * TILE : (n + 1) * TILE]
            mine = (mine[:16] + mine[16:]) * weights[n]
            at = z * 8 + base
            sum_ref[at] = sum_ref[at] + (mine[:8] + mine[8:]) * jnp.where(valid, 1.0, 0.0)

    each_pair(in_ref, names, cos_ref, sin_ref, use)
    count = PLANES * 8
    sums = jnp.sum(jnp.sum(sum_ref[...], axis=1), axis=1, keepdims=True)
    lane, sub = iota((count, TILE), 1), iota((count, TILE), 0)
    row = jnp.sum(jnp.where(lane == sub, sums, 0.0), axis=0, keepdims=True)
    row = row * np.float32(1.0 / 1024)
    lane = iota((1, TILE), 1)
    row = jnp.where(lane < 64, row, jnp.where(lane < 80, own_ref[0:1, :], 0.0))
    over = names[0, OVER]
    for z in range(1, PLANES):
        over = jnp.maximum(over, names[z, OVER])
    row = jnp.where(lane == 96, over.astype(F32), row)
    out_ref[...] = jnp.broadcast_to(row, out_ref.shape)


def end_kernel(me_ref, in_ref, own_ref, amp_out, res_out, dir_out, over_out):
    dets, bases = amp_out.shape
    spans = in_ref.shape[0] // (PLANES * NEAR)
    lane = iota((NEAR, TILE), 1)
    valid = lane < PLANES * 8
    base = lane % bases
    scan, way, rest = [], [], []
    over = jnp.zeros((NEAR, TILE), F32)
    for i in range(spans):
        a = w = r = jnp.zeros((NEAR, TILE), F32)
        for z in range(PLANES):
            at = (i * PLANES + z) * NEAR
            x = in_ref[at : at + NEAR, :]
            a = a + x
            over = jnp.maximum(over, x)
            group = lane >> 3
            r = r + pltpu.roll(jnp.where(group == 8, x, 0.0), (z * 8 - 64) % TILE, 1)
            w = w + pltpu.roll(jnp.where(group == 9, x, 0.0), (z * 8 - 72) % TILE, 1)
        scan.append(a)
        way.append(w)
        rest.append(r)
    over = jnp.where(lane == 96, over, 0.0)
    zero = jnp.zeros((NEAR, TILE), F32)
    applied = []
    for i in range(spans):
        from_left = pltpu.roll(way[i - 1] if i else zero, TILE - (bases - 1), 1)
        from_right = pltpu.roll(way[i + 1] if i < spans - 1 else zero, bases - 1, 1)
        before = jnp.where(base == 0, from_left, pltpu.roll(way[i], 1, 1))
        after = jnp.where(base == bases - 1, from_right, pltpu.roll(way[i], TILE - 1, 1))
        v = scan[i] + way[i] + STIFFNESS * (2.0 * way[i] - before - after)
        applied.append(jnp.where(valid, v, 0.0))

    def total(terms):
        v = terms[0]
        for term in terms[1:]:
            v = v + term
        return jnp.sum(jnp.sum(v, axis=0, keepdims=True), axis=1, keepdims=True)

    now = total([r * r for r in rest])
    factor = now / total([w * a for w, a in zip(way, applied)])
    fresh = [r - factor * a for r, a in zip(rest, applied)]
    ratio = total([f * f for f in fresh]) / now
    sub = iota((NEAR, TILE), 0)
    det = jnp.broadcast_to(me_ref[0:1, :], (NEAR, TILE))
    span = jnp.broadcast_to(me_ref[1:2, :], (NEAR, TILE))
    here = (sub == (det & (NEAR - 1))) & ((lane >> 3) == (det >> 3))
    mine = zero
    for i in range(spans):
        mine = mine + jnp.where(here & (span == i), fresh[i], 0.0)
    for shift in (64, 32, 16, 8):
        mine = mine + pltpu.roll(mine, shift, 1)
    mine = jnp.sum(mine, axis=0, keepdims=True)
    my_way = own_ref[0:1, 72:80]
    my_fresh = mine[:, 0:8]
    moved = own_ref[1:2, 0:8] + factor * my_way
    turn = my_fresh + ratio * my_way
    for d in range(dets):
        lo, hi = d * bases, (d + 1) * bases
        amp_out[d : d + 1, :] = moved[:, lo:hi]
        res_out[d : d + 1, :] = my_fresh[:, lo:hi]
        dir_out[d : d + 1, :] = turn[:, lo:hi]
    over_out[0] = jnp.max(over)


def slow_bin_kernel(slot_ref, dir_ref, pix_ref, ang_ref, hits_ref, out_ref, cos_ref, sin_ref, acc_ref):
    c, s = cos_sin(2.0 * ang_ref[...])
    cos_ref[...] = c
    sin_ref[...] = s
    acc_ref[...] = jnp.zeros_like(acc_ref)
    tiles = pix_ref.shape[0]
    dets, bases = dir_ref.shape
    span = tiles // dets // bases

    def group(g, carry):
        det, base = g % dets, g // dets
        height = dir_ref[det, base]
        for t in range(span):
            tile = base * span + t
            slot = slot_ref[det, tile]
            row = pl.ds(tile * dets + det, 1)
            hot, weight = tile_parts(
                pix_ref[row, :], cos_ref[row, :], sin_ref[row, :], (slot >> 1) & 1
            )
            place = (slot & 1) * (acc_ref.shape[0] // 2) + (slot >> 2)
            acc_ref[place] = acc_ref[place] + bin_tile(hot, weight) * height
        return carry

    lax.fori_loop(0, dets * bases, group, 0)

    put_bins(acc_ref, out_ref, [jnp.broadcast_to(hits_ref[...], (8, TILE))])


def slow_scan_kernel(
    slot_ref, dir_ref, res_ref, pix_ref, ang_ref, in_ref, out_ref, cos_ref, sin_ref, sky_ref, sum_ref
):
    c, s = cos_sin(2.0 * ang_ref[...])
    cos_ref[...] = c
    sin_ref[...] = s
    get_sky(in_ref, sky_ref)
    pairs = sky_ref.shape[0] // 2
    tiles = pix_ref.shape[0]
    dets, bases = dir_ref.shape
    span = tiles // dets // bases

    def group(g, carry):
        det, base = g % dets, g // dets
        total = jnp.zeros((8, TILE), F32)
        for t in range(span):
            tile = base * span + t
            slot = slot_ref[det, tile]
            row = pl.ds(tile * dets + det, 1)
            hot, weight = tile_parts(
                pix_ref[row, :], cos_ref[row, :], sin_ref[row, :], (slot >> 1) & 1
            )
            place = (slot & 1) * pairs + (slot >> 2)
            total = total + scan_tile(hot, weight, sky_ref[place])
        sum_ref[pl.ds(det * bases + base, 1), :] = jnp.sum(total, axis=0, keepdims=True)
        return carry

    lax.fori_loop(0, dets * bases, group, 0)
    count = dets * bases
    sums = jnp.sum(sum_ref[...], axis=1, keepdims=True) * np.float32(1.0 / (span * TILE))
    lane, sub = iota((count, TILE), 1), iota((count, TILE), 0)
    row = jnp.sum(jnp.where(lane == sub, sums, 0.0), axis=0, keepdims=True)
    lane = iota((1, TILE), 1)
    for d in range(dets):
        for b in range(bases):
            k = d * bases + b
            row = jnp.where(lane == count + k, dir_ref[d, b], row)
            row = jnp.where(lane == 2 * count + k, res_ref[d, b], row)
    out_ref[...] = jnp.broadcast_to(row, out_ref.shape)


def slow_end_kernel(me_ref, in_ref, amp_ref, amp_out, res_out, dir_out, keep_ref):
    rows = in_ref.shape[0]
    dets, bases = amp_ref.shape
    count = dets * bases
    owners = me_ref[2]
    x = in_ref[...]
    lane = iota((rows, TILE), 1)
    valid = lane < count
    base = lane % bases
    scan = jnp.where(valid, x, 0.0)
    way = jnp.where(valid, pltpu.roll(x, TILE - count, 1), 0.0)
    rest = jnp.where(valid, pltpu.roll(x, TILE - 2 * count, 1), 0.0)
    step = rows // 4
    zero = jnp.zeros((step, TILE), F32)
    from_left = pltpu.roll(jnp.concatenate([zero, way[:-step]], axis=0), TILE - (bases - 1), 1)
    from_right = pltpu.roll(jnp.concatenate([way[step:], zero], axis=0), bases - 1, 1)
    before = jnp.where(base == 0, from_left, pltpu.roll(way, 1, 1))
    after = jnp.where(base == bases - 1, from_right, pltpu.roll(way, TILE - 1, 1))
    applied = scan + way + STIFFNESS * (2.0 * way - before - after)
    applied = jnp.where(valid, applied, 0.0)

    def total(v):
        return jnp.sum(jnp.sum(v, axis=0, keepdims=True), axis=1, keepdims=True)

    now = total(rest * rest)
    factor = now / total(way * applied)
    fresh = rest - factor * applied
    ratio = total(fresh * fresh) / now
    keep_ref[0] = fresh
    keep_ref[1] = way
    mine = me_ref[1] * step + me_ref[0]
    my_fresh = keep_ref[0, pl.ds(mine, 1), :]
    my_way = keep_ref[1, pl.ds(mine, 1), :]
    move = factor * my_way
    turn = my_fresh + ratio * my_way
    for d in range(dets):
        lo, hi = d * bases, (d + 1) * bases
        amp_out[d : d + 1, :] = amp_ref[d : d + 1, :] + move[:, lo:hi]
        res_out[d : d + 1, :] = my_fresh[:, lo:hi]
        dir_out[d : d + 1, :] = turn[:, lo:hi]


SMEM = pl.BlockSpec(memory_space=pltpu.SMEM)
VMEM = pl.BlockSpec(memory_space=pltpu.VMEM)
SMALL = pltpu.CompilerParams(vmem_limit_bytes=12 << 20)
DET = ("z", "x", "core")
ALL = ("tm",) + DET
PLANE = ("tm", "x", "core")


def exchange(value, axes, rows):
    if rows % 4:
        moved = lax.all_to_all(value.reshape(-1, 1, TILE), axes, 0, 0, tiled=True)
        return moved.reshape(value.shape)
    peers = value.shape[0] // rows
    moved = lax.all_to_all(value.reshape(peers, rows, TILE), axes, 0, 0, tiled=True)
    return moved.reshape(value.shape)


def f32(*shape):
    return jax.ShapeDtypeStruct(shape, F32)


def slow(spot, me, prec, places, way, res, amp, pix, ang, hits):
    tiles = pix.shape[0]
    slots = hits.shape[1] * 2
    peers = 4 * hits.shape[1]
    hit_row = hits.reshape(1, slots).astype(F32)
    table = [pltpu.VMEM((tiles, TILE), F32)] * 2 + [pltpu.VMEM((slots // 2, 8, WINDOW), F32)]
    binned = pl.pallas_call(
        slow_bin_kernel,
        out_shape=f32(peers * 4, TILE),
        in_specs=[SMEM, SMEM, VMEM, VMEM, VMEM],
        out_specs=VMEM,
        scratch_shapes=table,
        name="slow_bin",
    )(places, way, pix, ang, hit_row)
    sky = solve(slow_own_kernel, (me, exchange(binned, ALL, 4), prec), peers * 4)
    last = pl.pallas_call(
        slow_scan_kernel,
        out_shape=f32(peers, TILE),
        in_specs=[SMEM, SMEM, SMEM, VMEM, VMEM, VMEM],
        out_specs=VMEM,
        scratch_shapes=table + [pltpu.VMEM((8, TILE), F32)],
        name="slow_scan",
    )(places, way, res, pix, ang, exchange(sky, ALL, 4))
    return pl.pallas_call(
        slow_end_kernel,
        out_shape=[f32(*amp.shape)] * 3,
        in_specs=[SMEM, VMEM, VMEM],
        out_specs=[VMEM] * 3,
        scratch_shapes=[pltpu.VMEM((2, peers, TILE), F32)],
        name="slow_end",
    )(spot, exchange(last, ALL, 1), amp)


def solve(kernel, args, *shape):
    shape = shape + (TILE,)
    return pl.pallas_call(
        kernel,
        out_shape=f32(*shape),
        in_specs=[VMEM] * 3,
        out_specs=VMEM,
        compiler_params=SMALL,
        name=kernel.__name__,
    )(*args)


def shards(amp, res, way, pix, ang, places, hits, prec):
    dets, samples = pix.shape
    per_det = samples // TILE
    tiles = dets * per_det
    owners = hits.shape[2]
    peers = 4 * owners
    near = 4 * NEAR

    def rows_of(v):
        return v.reshape(dets, per_det, TILE).transpose(1, 0, 2).reshape(tiles, TILE)

    pix, ang = rows_of(pix), rows_of(ang)
    hits = hits.reshape(owners, 2).T
    prec = prec.transpose(1, 0, 2)
    spot = jnp.stack([lax.axis_index(DET), lax.axis_index("tm"), owners]).astype(I32)
    me = jnp.broadcast_to(jnp.pad(spot, (0, 5))[:, None], (8, TILE))

    me, places = lax.optimization_barrier((me, places))
    given = (places, way, res, amp, pix, ang, hits)
    given = tuple(pltpu.with_memory_space_constraint(v, pltpu.HBM) for v in given)
    packed, own, *given = pl.pallas_call(
        pack_kernel,
        out_shape=[f32(PLANES * CHUNK, TILE), f32(8, TILE)]
        + [jax.ShapeDtypeStruct(v.shape, v.dtype) for v in given],
        in_specs=[pl.BlockSpec(memory_space=pltpu.HBM)] * 7,
        out_specs=[VMEM] * 9,
        scratch_shapes=[pltpu.SMEM(v.shape, v.dtype) for v in given[:4]]
        + [
            pltpu.VMEM((tiles, TILE), I32),
            pltpu.SMEM((PLANES,), I32),
            pltpu.SemaphoreType.DMA((11,)),
        ],
        compiler_params=SMALL,
        name="pack_tiles",
    )(*given)
    packed = exchange(packed, "z", CHUNK)

    raw = packed.reshape(PLANES, CHUNK, TILE)[:, CODES].astype(I32)
    slot, row = raw >> 6, raw & 63
    base = row % dets * way.shape[1] + row // (tiles // way.shape[1])
    names = (slot // 2 % NEAR) * 8 + base
    sems = pltpu.SemaphoreType.DMA((PLANES + 1,))
    binned, cosine, sine = pl.pallas_call(
        bin_kernel,
        out_shape=[f32(near * BINS, TILE)] + [f32(PLANES * ANGLES, TILE)] * 2,
        in_specs=[VMEM] * 2,
        out_specs=[VMEM] * 3,
        scratch_shapes=[
            pltpu.SMEM((PLANES, TILE), I32),
            pltpu.SMEM((PLANES, TILE), F32),
            sems,
        ],
        compiler_params=SMALL,
        name="bin_tiles",
    )(packed, names)
    binned = exchange(binned, PLANE, BINS)
    sky = solve(own_kernel, (me, binned, prec), near, 3 * PLANES)
    sky = exchange(sky.reshape(near * 3 * PLANES, TILE), PLANE, 3 * PLANES)

    last = pl.pallas_call(
        scan_kernel,
        out_shape=f32(peers, TILE),
        in_specs=[VMEM] * 6,
        out_specs=VMEM,
        scratch_shapes=[
            pltpu.VMEM((near * 4 * PLANES, TILE), F32),
            pltpu.VMEM((PLANES * 8, 8, TILE), F32),
            pltpu.SMEM((PLANES, TILE), I32),
            sems,
        ],
        compiler_params=SMALL,
        name="scan_tiles",
    )(packed, names, cosine, sine, sky, own)
    *out, over = pl.pallas_call(
        end_kernel,
        out_shape=[f32(*amp.shape)] * 3 + [f32(1)],
        in_specs=[VMEM] * 3,
        out_specs=[VMEM] * 3 + [SMEM],
        compiler_params=SMALL,
        name="end_step",
    )(me, exchange(last, ALL, 1), own)
    over, *given = lax.optimization_barrier((over, *given))
    return lax.cond(
        over[0] > 0,
        lambda: tuple(slow(spot, me, prec, *given)),
        lambda: tuple(out),
    )


def solution(mesh):
    spans = mesh.shape["tm"]
    split_mesh = jax.sharding.Mesh(
        mesh.devices.reshape(spans, PLANES, NEAR // 2, 2), ("tm", "z", "x", "core")
    )
    return jax.shard_map(
        shards,
        mesh=split_mesh,
        in_specs=(P(DET, "tm"),) * 6 + (P("tm", DET, None, None), P(DET, None, None)),
        out_specs=(P(DET, "tm"),) * 3,
        check_vma=False,
    )
```

```python
import jax
import jax.numpy as jnp
import numpy as np
from jax import lax
from jax.experimental import pallas as pl
from jax.experimental.pallas import tpu as pltpu
from jax.sharding import PartitionSpec as P

TILE = 128
WINDOW = 256
STIFFNESS = 0.5

ROOM = 23
CHUNK = 2 * ROOM + 2
CODES = 2 * ROOM
HITS = 2 * ROOM + 1
ANGLES = 24
GROUP = 4
PER_STEP = 10
COUNT = 32
OVER = 33
HERE = 34
WAYS = 40
PLANES = 8
NEAR = 8
BINS = 3 * PLANES + 1
BF16 = jnp.bfloat16
F32 = jnp.float32
I32 = jnp.int32
NT = (((1,), (1,)), ((), ()))
NN = (((1,), (0,)), ((), ()))


def iota(shape, dim):
    return lax.broadcasted_iota(I32, shape, dim)


def dot(a, b, dims=NN):
    return lax.dot_general(a, b, dims, preferred_element_type=F32)


def split(x):
    high = x.astype(BF16)
    return high, (x - high.astype(F32)).astype(BF16)


def cos_sin(x):
    n = jnp.floor(x * np.float32(2.0 / np.pi) + 0.5)
    r = x - n * np.float32(1.5703125)
    r = r - n * np.float32(4.837512969970703e-4)
    r = r - n * np.float32(7.549789948768648e-8)
    z = r * r
    s = np.float32(-1.9515295891e-4) * z + np.float32(8.3321608736e-3)
    s = (s * z + np.float32(-1.6666654611e-1)) * z * r + r
    c = np.float32(2.443315711809948e-5) * z + np.float32(-1.388731625493765e-3)
    c = (c * z + np.float32(4.166664568298827e-2)) * z * z - 0.5 * z + 1.0
    q = n.astype(I32)
    odd = (q & 1) == 1
    cosine = jnp.where(odd, s, c)
    sine = jnp.where(odd, c, s)
    cosine = jnp.where(((q + 1) & 2) == 2, -cosine, cosine)
    sine = jnp.where((q & 2) == 2, -sine, sine)
    return cosine, sine


def tile_parts(pixels, cosine, sine, half):
    hot = iota((WINDOW, TILE), 0) == pixels
    hot = jnp.where(hot, 1.0, 0.0).astype(BF16)
    sub = iota((8, TILE), 0)
    part = sub & 3
    weight = jnp.where(part == 0, 1.0, jnp.where(part == 1, cosine, sine))
    weight = jnp.where(((sub >> 2) == half) & (part < 3), weight, 0.0)
    return hot, weight


def bin_tile(hot, weight):
    high = weight.astype(BF16).astype(F32)
    both = jnp.concatenate([high, weight - high], axis=0).astype(BF16)
    res = dot(both, hot, NT)
    return res[:8] + res[8:]


def scan_tile(hot, weight, value):
    high = value.astype(BF16).astype(F32)
    both = jnp.concatenate([high, value - high], axis=0).astype(BF16)
    res = dot(both, hot)
    return (res[:8] + res[8:]) * weight


def put_bins(acc_ref, out_ref, extra):
    pairs = acc_ref.shape[0] // 2
    left = iota((8, TILE), 1) < 64
    last = (iota((8, TILE), 0) & 3) == 3
    for u in range(pairs):
        for b in range(2):
            first = acc_ref[u, :, b * TILE : (b + 1) * TILE]
            second = acc_ref[pairs + u, :, b * TILE : (b + 1) * TILE]
            even = jnp.where(left, first, pltpu.roll(second, 64, 1))
            odd = jnp.where(left, pltpu.roll(first, 64, 1), second)
            for q, value in ((2 * b, even), (2 * b + 1, odd)):
                at = (q * pairs + u) * 8
                out_ref[at : at + 8, :] = jnp.where(last, extra[u % len(extra)], value)


def get_sky(in_ref, sky_ref):
    pairs = sky_ref.shape[0] // 2
    left = iota((8, TILE), 1) < 64
    for u in range(pairs):
        for b in range(2):
            at = (2 * b * pairs + u) * 8
            even = in_ref[at : at + 8, :]
            at = ((2 * b + 1) * pairs + u) * 8
            odd = in_ref[at : at + 8, :]
            sky_ref[u, :, b * TILE : (b + 1) * TILE] = jnp.where(left, even, pltpu.roll(odd, 64, 1))
            sky_ref[pairs + u, :, b * TILE : (b + 1) * TILE] = jnp.where(
                left, pltpu.roll(even, 64, 1), odd
            )


def coded(number):
    base = number & 7
    return (number >> 3) * 128 + (base >> 2) + (base & 3) * 16


def pack_kernel(*refs):
    operands, (out_ref, own_ref), kept = refs[:7], refs[7:9], refs[9:16]
    slot_ref, way_ref, res_ref, amp_ref, pixel_ref, next_ref, sems = refs[16:]
    pix_ref, ang_ref, hits_ref = kept[4:]
    targets = kept + (slot_ref, way_ref, res_ref, amp_ref)
    copies = [
        pltpu.make_async_copy(operands[k % 7], target, sems.at[k])
        for k, target in enumerate(targets)
    ]
    for copy in copies:
        copy.start()
    own_ref[...] = jnp.zeros_like(own_ref)
    out_ref[...] = jnp.zeros_like(out_ref)
    for z in range(PLANES):
        next_ref[z] = z * CHUNK
    for copy in copies:
        copy.wait()
    dets, bases = way_ref.shape
    per_det = slot_ref.shape[1]
    lane1 = iota((1, TILE), 1)
    values = jnp.zeros((1, TILE), F32)
    amps = jnp.zeros((1, TILE), F32)
    for d in range(dets):
        for b in range(bases):
            k = d * bases + b
            values = jnp.where((lane1 == WAYS + k) | (lane1 == 72 + k), way_ref[d, b], values)
            values = jnp.where(lane1 == 64 + k, res_ref[d, b], values)
            amps = jnp.where(lane1 == k, amp_ref[d, b], amps)
    own_ref[0:1, :] = values
    own_ref[1:2, :] = amps
    sub, lane = iota((PLANES, TILE), 0), iota((PLANES, TILE), 1)
    at_row = sub * CHUNK + lane
    pix = pix_ref[...]
    pixel_ref[...] = ((pix & 192) << 1) + (pix & 63)

    def tile_step(t, codes):
        for d in range(dets):
            slot = slot_ref[d, t]
            plane = slot // (2 * NEAR)
            at = next_ref[plane]
            next_ref[plane] = at + 1
            at = jnp.minimum(at, out_ref.shape[0] - ROOM - 1)
            row = t * dets + d
            out_ref[pl.ds(at, 1), :] = ang_ref[pl.ds(row, 1), :]
            pixels = pixel_ref[pl.ds(row, 1), :] + (slot & 1) * 64
            out_ref[pl.ds(at + ROOM, 1), :] = pixels.astype(F32)
            codes = jnp.where(at_row == at, slot * 64 + row, codes)
        return codes

    codes = lax.fori_loop(0, per_det, tile_step, jnp.zeros((PLANES, TILE), I32), unroll=4)
    over = jnp.int32(0)
    for z in range(PLANES):
        count = next_ref[z] - z * CHUNK
        over = jnp.maximum(over, jnp.where(count > ROOM, 1, 0))
        codes = jnp.where((sub == z) & (lane == COUNT), coded(jnp.minimum(count, ROOM)), codes)
    codes = jnp.where(lane == OVER, coded(over), codes)
    codes = jnp.where(lane == HERE, coded(sub), codes)
    codes = jnp.where(lane < WAYS, codes.astype(F32), values)
    out_ref[pl.ds(CODES, PLANES, stride=CHUNK), :] = codes
    hits = jnp.concatenate([hits_ref[0:1, :], hits_ref[1:2, :]], axis=1).astype(F32)
    out_ref[pl.ds(HITS, PLANES, stride=CHUNK), :] = jnp.broadcast_to(hits, (PLANES, TILE))


def start_codes(in_ref, code_ref, sems):
    name_in, way_in = in_ref
    names, ways = code_ref
    copies = [
        pltpu.make_async_copy(name_in, names, sems.at[PLANES]),
    ]
    for z in range(PLANES):
        copies.append(
            pltpu.make_async_copy(
                way_in.at[pl.ds(z * CHUNK + CODES, 1), :], ways.at[pl.ds(z, 1), :], sems.at[z]
            )
        )
    for copy in copies:
        copy.start()
    return copies


def each_pair(in_ref, names, cos_ref, sin_ref, use):
    part, quarter = iota((16, TILE), 0) & 3, iota((16, TILE), 0) >> 2
    first, second = part == 0, part == 1
    quarter = jnp.where(part < 3, quarter, -1)
    pixel = iota((TILE, TILE), 0).astype(F32).astype(BF16)
    counts = [names[z, COUNT] for z in range(PLANES)]
    ends = []
    for z in range(PLANES):
        ends.append(counts[z] if z % GROUP == 0 else ends[-1] + counts[z])
    steps = jnp.int32(0)
    for z in range(GROUP - 1, PLANES, GROUP):
        steps = jnp.maximum(steps, (ends[z] + PER_STEP - 1) // PER_STEP)

    def tile(group, i):
        low = group * GROUP
        z, start = jnp.int32(low), jnp.int32(0)
        for k in range(GROUP - 1):
            z = z + jnp.where(i >= ends[low + k], 1, 0)
            start = jnp.where(i >= ends[low + k], ends[low + k], start)
        p = jnp.minimum(i - start, ROOM - 1)
        code = names[z, p]
        mine = in_ref[pl.ds(z * CHUNK + ROOM + p, 1), :].astype(I32)
        place = jnp.broadcast_to((mine & 127).astype(F32), (TILE, TILE)).astype(BF16)
        hot = jnp.maximum(1.0 - jnp.abs(pixel - place), 0.0)
        row = pl.ds(z * ANGLES + p, 1)
        weight = jnp.where(first, 1.0, jnp.where(second, cos_ref[row, :], sin_ref[row, :]))
        weight = jnp.where(quarter == (mine >> 7), weight, 0.0)
        return (z, code >> 3, code & 7, i < ends[low + GROUP - 1]), hot, weight

    def some(g, carry):
        for group in range(PLANES // GROUP):
            for k in range(0, PER_STEP, 2):
                use(*zip(*(tile(group, g * PER_STEP + k + n) for n in range(2))))
        return carry

    lax.fori_loop(0, steps, some, 0)


def table_rows(q, owner, z, chunk, count):
    return pl.ds((q * NEAR + owner) * chunk + z, count, stride=PLANES)


def halves(x):
    high, low = split(x)
    return jnp.concatenate([high, low], axis=0)


def bin_kernel(in_ref, name_ref, out_ref, cos_ref, sin_ref, names, ways, sems):
    copies = start_codes((name_ref, in_ref), (names, ways), sems)
    for z in range(PLANES):
        c, s = cos_sin(2.0 * in_ref[z * CHUNK : z * CHUNK + ANGLES, :])
        cos_ref[z * ANGLES : (z + 1) * ANGLES, :] = c
        sin_ref[z * ANGLES : (z + 1) * ANGLES, :] = s
    out_ref[...] = jnp.zeros_like(out_ref)
    for copy in copies:
        copy.wait()
    hits = in_ref[pl.ds(HITS, PLANES, stride=CHUNK), :].astype(BF16)
    lane, deep = iota((TILE, TILE), 1), iota((TILE, TILE), 0)
    here = (lane & 1) * 64 + names[0, HERE] * NEAR + ((lane >> 1) & (NEAR - 1))
    moved = dot(hits, jnp.where(deep == here, 1.0, 0.0).astype(BF16))
    moved = jnp.where(iota((PLANES, TILE), 1) >> 4 == iota((PLANES, TILE), 0), moved, 0.0)
    moved = jnp.sum(moved, axis=0, keepdims=True)
    for at in range(BINS - 1, out_ref.shape[0], BINS):
        out_ref[at : at + 1, :] = moved

    def use(tiles, hots, weights):
        both = jnp.concatenate([halves(weight) for weight in weights], axis=0)
        res = dot(both, jnp.concatenate(hots, axis=0), NT)
        for n, (z, owner, base, valid) in enumerate(tiles):
            height = jnp.where(valid, ways[z, WAYS + base], 0.0)
            mine = res[32 * n : 32 * n + 32, n * TILE : (n + 1) * TILE]
            mine = (mine[:16] + mine[16:]) * height
            for q in range(4):
                rows = table_rows(q, owner, z, BINS, 3)
                out_ref[rows, :] = out_ref[rows, :] + mine[4 * q : 4 * q + 3]

    each_pair(in_ref, names, cos_ref, sin_ref, use)


def own_kernel(me_ref, in_ref, prec_ref, out_ref):
    peers = in_ref.shape[0] // BINS
    sources = peers * PLANES
    owner = me_ref[0:1, :] & (NEAR - 1)

    def take(c):
        if c < 3:
            at = [w * BINS + c * PLANES for w in range(peers)]
            return jnp.concatenate([in_ref[a : a + PLANES, :] for a in at], axis=0)
        mine = iota((PLANES, TILE), 1) >> 4 == iota((PLANES, TILE), 0)
        at = [w * BINS + BINS - 1 for w in range(peers)]
        return jnp.concatenate([jnp.where(mine, in_ref[a : a + 1, :], 0.0) for a in at], axis=0)

    def put(c, value):
        out_ref[:, c * PLANES : (c + 1) * PLANES, :] = value.reshape(peers, PLANES, TILE)

    def place(lane, k):
        return (lane & 15) == 2 * owner + k

    own_solve(place, me_ref[1:2, :], sources, take, prec_ref, put)


def slow_own_kernel(me_ref, in_ref, prec_ref, out_ref):
    sources = in_ref.shape[0] // 4

    def take(c):
        return in_ref[pl.ds(c, sources, stride=4), :]

    def put(c, value):
        out_ref[pl.ds(c, sources, stride=4), :] = value

    def place(lane, k):
        return lane == me_ref[0:1, :] + 64 * k

    own_solve(place, me_ref[1:2, :], sources, take, prec_ref, put)
    put(3, jnp.zeros((sources, TILE), F32))


def own_solve(place, quarter, sources, take, prec_ref, put):
    subs = prec_ref.shape[1]
    ids = take(3).astype(BF16)
    lane = iota((16, TILE), 1)
    row = iota((16, TILE), 0)
    pick = jnp.where(place(lane, row) & (row < 2), 1.0, 0.0).astype(BF16)
    id_rows = dot(pick, ids, NT).astype(I32)
    sub = iota((subs, sources), 0)
    hot = jnp.concatenate(
        [
            jnp.where(sub == id_rows[0:1, :], 1.0, 0.0),
            jnp.where(sub == id_rows[1:2, :], 1.0, 0.0),
        ],
        axis=0,
    ).astype(BF16)
    left = iota((subs, TILE), 1) < 64
    binned = []
    for c in range(3):
        high, low = split(take(c))
        res = dot(hot, jnp.concatenate([high, low], axis=1))
        res = res[:, :TILE] + res[:, TILE:]
        res = jnp.where(left, res[:subs], res[subs:])
        binned.append(res + pltpu.roll(res, 64, 1))

    quarter = jnp.broadcast_to(quarter, (subs, TILE))
    keep = (iota((subs, TILE), 1) >> 6) == (quarter & 1)
    block = quarter >> 1
    prec = []
    for e in range(6):
        value = jnp.where(block == 0, prec_ref[e, :, :TILE], prec_ref[e, :, TILE:])
        value = jnp.where(keep, value, 0.0)
        prec.append(value + pltpu.roll(value, 64, 1))
    sky = [
        prec[0] * binned[0] + prec[1] * binned[1] + prec[2] * binned[2],
        prec[1] * binned[0] + prec[3] * binned[1] + prec[4] * binned[2],
        prec[2] * binned[0] + prec[4] * binned[1] + prec[5] * binned[2],
    ]

    deep, wide = iota((TILE, TILE), 0), iota((TILE, TILE), 1)
    spread = jnp.where(place(deep, wide >> 6), 1.0, 0.0).astype(BF16)
    named = dot(ids, spread).astype(I32)
    back = jnp.where(named == (iota((sources, TILE), 1) & 63), 1.0, 0.0).astype(BF16)
    back = jnp.concatenate([back, back], axis=1)
    gap = jnp.zeros((64 - subs, TILE), F32)
    for c in range(3):
        first = jnp.where(left, sky[c], 0.0)
        second = jnp.where(left, 0.0, sky[c])
        high, low = split(jnp.concatenate([first, gap, second, gap], axis=0))
        put(c, dot(back, jnp.concatenate([high, low], axis=0)))


def scan_kernel(
    in_ref, name_ref, cos_ref, sin_ref, sky_in_ref, own_ref, out_ref, sky_ref, sum_ref, names, sems
):
    copy = pltpu.make_async_copy(name_ref, names, sems.at[0])
    copy.start()
    for peer in range(4 * NEAR):
        for c in range(4):
            at = (peer * 4 + c) * PLANES
            here = (peer * 3 + c) * PLANES
            sky_ref[at : at + PLANES, :] = (
                sky_in_ref[here : here + PLANES, :] if c < 3 else jnp.zeros((PLANES, TILE), F32)
            )
    sum_ref[...] = jnp.zeros_like(sum_ref)
    copy.wait()

    def use(tiles, hots, weights):
        both = []
        for z, owner, _, _ in tiles:
            value = [sky_ref[table_rows(q, owner, z, 4 * PLANES, 4), :] for q in range(4)]
            both.append(halves(jnp.concatenate(value, axis=0)))
        res = dot(jnp.concatenate(both, axis=0), jnp.concatenate(hots, axis=1))
        for n, (z, _, base, valid) in enumerate(tiles):
            mine = res[32 * n : 32 * n + 32, n * TILE : (n + 1) * TILE]
            mine = (mine[:16] + mine[16:]) * weights[n]
            rows = pl.ds(pl.multiple_of((z * 8 + base) * 8, 8), 8)
            mine = (mine[:8] + mine[8:]) * jnp.where(valid, 1.0, 0.0)
            sum_ref[rows, :] = sum_ref[rows, :] + mine

    each_pair(in_ref, names, cos_ref, sin_ref, use)
    count = PLANES * 8
    sums = sum_ref[pl.ds(0, count, stride=8), :]
    for k in range(1, 8):
        sums = sums + sum_ref[pl.ds(k, count, stride=8), :]
    sums = jnp.sum(sums, axis=1, keepdims=True)
    lane, sub = iota((count, TILE), 1), iota((count, TILE), 0)
    row = jnp.sum(jnp.where(lane == sub, sums, 0.0), axis=0, keepdims=True)
    row = row * np.float32(1.0 / 1024)
    lane = iota((1, TILE), 1)
    row = jnp.where(lane < 64, row, jnp.where(lane < 80, own_ref[0:1, :], 0.0))
    over = names[0, OVER]
    for z in range(1, PLANES):
        over = jnp.maximum(over, names[z, OVER])
    row = jnp.where(lane == 96, over.astype(F32), row)
    out_ref[...] = jnp.broadcast_to(row, out_ref.shape)


def end_kernel(me_ref, in_ref, own_ref, amp_out, res_out, dir_out, over_out):
    dets, bases = amp_out.shape
    spans = in_ref.shape[0] // (PLANES * NEAR)
    lane = iota((NEAR, TILE), 1)
    valid = lane < PLANES * 8
    base = lane % bases
    scan, way, rest = [], [], []
    over = jnp.zeros((NEAR, TILE), F32)
    for i in range(spans):
        a = w = r = jnp.zeros((NEAR, TILE), F32)
        for z in range(PLANES):
            at = (i * PLANES + z) * NEAR
            x = in_ref[at : at + NEAR, :]
            a = a + x
            over = jnp.maximum(over, x)
            group = lane >> 3
            r = r + pltpu.roll(jnp.where(group == 8, x, 0.0), (z * 8 - 64) % TILE, 1)
            w = w + pltpu.roll(jnp.where(group == 9, x, 0.0), (z * 8 - 72) % TILE, 1)
        scan.append(a)
        way.append(w)
        rest.append(r)
    over = jnp.where(lane == 96, over, 0.0)
    zero = jnp.zeros((NEAR, TILE), F32)
    applied = []
    for i in range(spans):
        from_left = pltpu.roll(way[i - 1] if i else zero, TILE - (bases - 1), 1)
        from_right = pltpu.roll(way[i + 1] if i < spans - 1 else zero, bases - 1, 1)
        before = jnp.where(base == 0, from_left, pltpu.roll(way[i], 1, 1))
        after = jnp.where(base == bases - 1, from_right, pltpu.roll(way[i], TILE - 1, 1))
        v = scan[i] + way[i] + STIFFNESS * (2.0 * way[i] - before - after)
        applied.append(jnp.where(valid, v, 0.0))

    def total(terms):
        v = terms[0]
        for term in terms[1:]:
            v = v + term
        return jnp.sum(jnp.sum(v, axis=0, keepdims=True), axis=1, keepdims=True)

    now = total([r * r for r in rest])
    factor = now / total([w * a for w, a in zip(way, applied)])
    fresh = [r - factor * a for r, a in zip(rest, applied)]
    ratio = total([f * f for f in fresh]) / now
    sub = iota((NEAR, TILE), 0)
    det = jnp.broadcast_to(me_ref[0:1, :], (NEAR, TILE))
    span = jnp.broadcast_to(me_ref[1:2, :], (NEAR, TILE))
    here = (sub == (det & (NEAR - 1))) & ((lane >> 3) == (det >> 3))
    mine = zero
    for i in range(spans):
        mine = mine + jnp.where(here & (span == i), fresh[i], 0.0)
    for shift in (64, 32, 16, 8):
        mine = mine + pltpu.roll(mine, shift, 1)
    mine = jnp.sum(mine, axis=0, keepdims=True)
    my_way = own_ref[0:1, 72:80]
    my_fresh = mine[:, 0:8]
    moved = own_ref[1:2, 0:8] + factor * my_way
    turn = my_fresh + ratio * my_way
    for d in range(dets):
        lo, hi = d * bases, (d + 1) * bases
        amp_out[d : d + 1, :] = moved[:, lo:hi]
        res_out[d : d + 1, :] = my_fresh[:, lo:hi]
        dir_out[d : d + 1, :] = turn[:, lo:hi]
    over_out[0] = jnp.max(over)


def slow_bin_kernel(slot_ref, dir_ref, pix_ref, ang_ref, hits_ref, out_ref, cos_ref, sin_ref, acc_ref):
    c, s = cos_sin(2.0 * ang_ref[...])
    cos_ref[...] = c
    sin_ref[...] = s
    acc_ref[...] = jnp.zeros_like(acc_ref)
    tiles = pix_ref.shape[0]
    dets, bases = dir_ref.shape
    span = tiles // dets // bases

    def group(g, carry):
        det, base = g % dets, g // dets
        height = dir_ref[det, base]
        for t in range(span):
            tile = base * span + t
            slot = slot_ref[det, tile]
            row = pl.ds(tile * dets + det, 1)
            hot, weight = tile_parts(
                pix_ref[row, :], cos_ref[row, :], sin_ref[row, :], (slot >> 1) & 1
            )
            place = (slot & 1) * (acc_ref.shape[0] // 2) + (slot >> 2)
            acc_ref[place] = acc_ref[place] + bin_tile(hot, weight) * height
        return carry

    lax.fori_loop(0, dets * bases, group, 0)

    put_bins(acc_ref, out_ref, [jnp.broadcast_to(hits_ref[...], (8, TILE))])


def slow_scan_kernel(
    slot_ref, dir_ref, res_ref, pix_ref, ang_ref, in_ref, out_ref, cos_ref, sin_ref, sky_ref, sum_ref
):
    c, s = cos_sin(2.0 * ang_ref[...])
    cos_ref[...] = c
    sin_ref[...] = s
    get_sky(in_ref, sky_ref)
    pairs = sky_ref.shape[0] // 2
    tiles = pix_ref.shape[0]
    dets, bases = dir_ref.shape
    span = tiles // dets // bases

    def group(g, carry):
        det, base = g % dets, g // dets
        total = jnp.zeros((8, TILE), F32)
        for t in range(span):
            tile = base * span + t
            slot = slot_ref[det, tile]
            row = pl.ds(tile * dets + det, 1)
            hot, weight = tile_parts(
                pix_ref[row, :], cos_ref[row, :], sin_ref[row, :], (slot >> 1) & 1
            )
            place = (slot & 1) * pairs + (slot >> 2)
            total = total + scan_tile(hot, weight, sky_ref[place])
        sum_ref[pl.ds(det * bases + base, 1), :] = jnp.sum(total, axis=0, keepdims=True)
        return carry

    lax.fori_loop(0, dets * bases, group, 0)
    count = dets * bases
    sums = jnp.sum(sum_ref[...], axis=1, keepdims=True) * np.float32(1.0 / (span * TILE))
    lane, sub = iota((count, TILE), 1), iota((count, TILE), 0)
    row = jnp.sum(jnp.where(lane == sub, sums, 0.0), axis=0, keepdims=True)
    lane = iota((1, TILE), 1)
    for d in range(dets):
        for b in range(bases):
            k = d * bases + b
            row = jnp.where(lane == count + k, dir_ref[d, b], row)
            row = jnp.where(lane == 2 * count + k, res_ref[d, b], row)
    out_ref[...] = jnp.broadcast_to(row, out_ref.shape)


def slow_end_kernel(me_ref, in_ref, amp_ref, amp_out, res_out, dir_out, keep_ref):
    rows = in_ref.shape[0]
    dets, bases = amp_ref.shape
    count = dets * bases
    owners = me_ref[2]
    x = in_ref[...]
    lane = iota((rows, TILE), 1)
    valid = lane < count
    base = lane % bases
    scan = jnp.where(valid, x, 0.0)
    way = jnp.where(valid, pltpu.roll(x, TILE - count, 1), 0.0)
    rest = jnp.where(valid, pltpu.roll(x, TILE - 2 * count, 1), 0.0)
    step = rows // 4
    zero = jnp.zeros((step, TILE), F32)
    from_left = pltpu.roll(jnp.concatenate([zero, way[:-step]], axis=0), TILE - (bases - 1), 1)
    from_right = pltpu.roll(jnp.concatenate([way[step:], zero], axis=0), bases - 1, 1)
    before = jnp.where(base == 0, from_left, pltpu.roll(way, 1, 1))
    after = jnp.where(base == bases - 1, from_right, pltpu.roll(way, TILE - 1, 1))
    applied = scan + way + STIFFNESS * (2.0 * way - before - after)
    applied = jnp.where(valid, applied, 0.0)

    def total(v):
        return jnp.sum(jnp.sum(v, axis=0, keepdims=True), axis=1, keepdims=True)

    now = total(rest * rest)
    factor = now / total(way * applied)
    fresh = rest - factor * applied
    ratio = total(fresh * fresh) / now
    keep_ref[0] = fresh
    keep_ref[1] = way
    mine = me_ref[1] * step + me_ref[0]
    my_fresh = keep_ref[0, pl.ds(mine, 1), :]
    my_way = keep_ref[1, pl.ds(mine, 1), :]
    move = factor * my_way
    turn = my_fresh + ratio * my_way
    for d in range(dets):
        lo, hi = d * bases, (d + 1) * bases
        amp_out[d : d + 1, :] = amp_ref[d : d + 1, :] + move[:, lo:hi]
        res_out[d : d + 1, :] = my_fresh[:, lo:hi]
        dir_out[d : d + 1, :] = turn[:, lo:hi]


SMEM = pl.BlockSpec(memory_space=pltpu.SMEM)
VMEM = pl.BlockSpec(memory_space=pltpu.VMEM)
SMALL = pltpu.CompilerParams(vmem_limit_bytes=12 << 20)
DET = ("z", "x", "core")
ALL = ("tm",) + DET
PLANE = ("tm", "x", "core")


def exchange(value, axes, rows):
    if rows % 4:
        moved = lax.all_to_all(value.reshape(-1, 1, TILE), axes, 0, 0, tiled=True)
        return moved.reshape(value.shape)
    peers = value.shape[0] // rows
    moved = lax.all_to_all(value.reshape(peers, rows, TILE), axes, 0, 0, tiled=True)
    return moved.reshape(value.shape)


def f32(*shape):
    return jax.ShapeDtypeStruct(shape, F32)


def slow(owners, me, prec, places, way, res, amp, pix, ang, hits):
    spot = jnp.stack([me[0, 0], me[1, 0], jnp.int32(owners)])
    tiles = pix.shape[0]
    slots = hits.shape[1] * 2
    peers = 4 * hits.shape[1]
    hit_row = hits.reshape(1, slots).astype(F32)
    table = [pltpu.VMEM((tiles, TILE), F32)] * 2 + [pltpu.VMEM((slots // 2, 8, WINDOW), F32)]
    binned = pl.pallas_call(
        slow_bin_kernel,
        out_shape=f32(peers * 4, TILE),
        in_specs=[SMEM, SMEM, VMEM, VMEM, VMEM],
        out_specs=VMEM,
        scratch_shapes=table,
        name="slow_bin",
    )(places, way, pix, ang, hit_row)
    sky = solve(slow_own_kernel, (me, exchange(binned, ALL, 4), prec), peers * 4)
    last = pl.pallas_call(
        slow_scan_kernel,
        out_shape=f32(peers, TILE),
        in_specs=[SMEM, SMEM, SMEM, VMEM, VMEM, VMEM],
        out_specs=VMEM,
        scratch_shapes=table + [pltpu.VMEM((8, TILE), F32)],
        name="slow_scan",
    )(places, way, res, pix, ang, exchange(sky, ALL, 4))
    return pl.pallas_call(
        slow_end_kernel,
        out_shape=[f32(*amp.shape)] * 3,
        in_specs=[SMEM, VMEM, VMEM],
        out_specs=[VMEM] * 3,
        scratch_shapes=[pltpu.VMEM((2, peers, TILE), F32)],
        name="slow_end",
    )(spot, exchange(last, ALL, 1), amp)


def solve(kernel, args, *shape):
    shape = shape + (TILE,)
    return pl.pallas_call(
        kernel,
        out_shape=f32(*shape),
        in_specs=[VMEM] * 3,
        out_specs=VMEM,
        compiler_params=SMALL,
        name=kernel.__name__,
    )(*args)


def shards(amp, res, way, pix, ang, places, hits, prec):
    dets, samples = pix.shape
    per_det = samples // TILE
    tiles = dets * per_det
    owners = hits.shape[2]
    peers = 4 * owners
    near = 4 * NEAR

    def rows_of(v):
        return v.reshape(dets, per_det, TILE).transpose(1, 0, 2).reshape(tiles, TILE)

    pix, ang = rows_of(pix), rows_of(ang)
    hits = hits.reshape(owners, 2).T
    prec = prec.transpose(1, 0, 2)
    first = lax.broadcasted_iota(I32, (8, TILE), 0) == 0
    me = jnp.where(first, lax.axis_index(DET), lax.axis_index("tm")).astype(I32)

    me, places = lax.optimization_barrier((me, places))
    given = (places, way, res, amp, pix, ang, hits)
    given = tuple(pltpu.with_memory_space_constraint(v, pltpu.HBM) for v in given)
    packed, own, *given = pl.pallas_call(
        pack_kernel,
        out_shape=[f32(PLANES * CHUNK, TILE), f32(8, TILE)]
        + [jax.ShapeDtypeStruct(v.shape, v.dtype) for v in given],
        in_specs=[pl.BlockSpec(memory_space=pltpu.HBM)] * 7,
        out_specs=[VMEM] * 9,
        scratch_shapes=[pltpu.SMEM(v.shape, v.dtype) for v in given[:4]]
        + [
            pltpu.VMEM((tiles, TILE), I32),
            pltpu.SMEM((PLANES,), I32),
            pltpu.SemaphoreType.DMA((11,)),
        ],
        compiler_params=SMALL,
        name="pack_tiles",
    )(*given)
    packed = exchange(packed, "z", CHUNK)

    raw = packed.reshape(PLANES, CHUNK, TILE)[:, CODES].astype(I32)
    slot, row = raw >> 6, raw & 63
    base = row % dets * way.shape[1] + row // (tiles // way.shape[1])
    names = (slot // 2 % NEAR) * 8 + base
    sems = pltpu.SemaphoreType.DMA((PLANES + 1,))
    binned, cosine, sine = pl.pallas_call(
        bin_kernel,
        out_shape=[f32(near * BINS, TILE)] + [f32(PLANES * ANGLES, TILE)] * 2,
        in_specs=[VMEM] * 2,
        out_specs=[VMEM] * 3,
        scratch_shapes=[
            pltpu.SMEM((PLANES, TILE), I32),
            pltpu.SMEM((PLANES, TILE), F32),
            sems,
        ],
        compiler_params=SMALL,
        name="bin_tiles",
    )(packed, names)
    binned = exchange(binned, PLANE, BINS)
    sky = solve(own_kernel, (me, binned, prec), near, 3 * PLANES)
    sky = exchange(sky.reshape(near * 3 * PLANES, TILE), PLANE, 3 * PLANES)

    last = pl.pallas_call(
        scan_kernel,
        out_shape=f32(peers, TILE),
        in_specs=[VMEM] * 6,
        out_specs=VMEM,
        scratch_shapes=[
            pltpu.VMEM((near * 4 * PLANES, TILE), F32),
            pltpu.VMEM((PLANES * 64, TILE), F32),
            pltpu.SMEM((PLANES, TILE), I32),
            sems,
        ],
        compiler_params=SMALL,
        name="scan_tiles",
    )(packed, names, cosine, sine, sky, own)
    *out, over = pl.pallas_call(
        end_kernel,
        out_shape=[f32(*amp.shape)] * 3 + [f32(1)],
        in_specs=[VMEM] * 3,
        out_specs=[VMEM] * 3 + [SMEM],
        compiler_params=SMALL,
        name="end_step",
    )(me, exchange(last, ALL, 1), own)
    over, *given = lax.optimization_barrier((over, *given))
    return lax.cond(
        over[0] > 0,
        lambda: tuple(slow(owners, me, prec, *given)),
        lambda: tuple(out),
    )


def solution(mesh):
    spans = mesh.shape["tm"]
    split_mesh = jax.sharding.Mesh(
        mesh.devices.reshape(spans, PLANES, NEAR // 2, 2), ("tm", "z", "x", "core")
    )
    return jax.shard_map(
        shards,
        mesh=split_mesh,
        in_specs=(P(DET, "tm"),) * 6 + (P("tm", DET, None, None), P(DET, None, None)),
        out_specs=(P(DET, "tm"),) * 3,
        check_vma=False,
    )
```

```python
import jax
import jax.numpy as jnp
import numpy as np
from jax import lax
from jax.experimental import pallas as pl
from jax.experimental.pallas import tpu as pltpu
from jax.sharding import PartitionSpec as P

TILE = 128
WINDOW = 256
STIFFNESS = 0.5

ROOM = 23
CHUNK = 2 * ROOM + 2
CODES = 2 * ROOM
HITS = 2 * ROOM + 1
ANGLES = 24
GROUP = 4
PER_STEP = 12
COUNT = 32
OVER = 33
HERE = 34
WAYS = 40
PLANES = 8
NEAR = 8
BINS = 3 * PLANES + 1
BF16 = jnp.bfloat16
F32 = jnp.float32
I32 = jnp.int32
NT = (((1,), (1,)), ((), ()))
NN = (((1,), (0,)), ((), ()))


def iota(shape, dim):
    return lax.broadcasted_iota(I32, shape, dim)


def dot(a, b, dims=NN):
    return lax.dot_general(a, b, dims, preferred_element_type=F32)


def split(x):
    high = x.astype(BF16)
    return high, (x - high.astype(F32)).astype(BF16)


def cos_sin(x):
    n = jnp.floor(x * np.float32(2.0 / np.pi) + 0.5)
    r = x - n * np.float32(1.5703125)
    r = r - n * np.float32(4.837512969970703e-4)
    r = r - n * np.float32(7.549789948768648e-8)
    z = r * r
    s = np.float32(-1.9515295891e-4) * z + np.float32(8.3321608736e-3)
    s = (s * z + np.float32(-1.6666654611e-1)) * z * r + r
    c = np.float32(2.443315711809948e-5) * z + np.float32(-1.388731625493765e-3)
    c = (c * z + np.float32(4.166664568298827e-2)) * z * z - 0.5 * z + 1.0
    q = n.astype(I32)
    odd = (q & 1) == 1
    cosine = jnp.where(odd, s, c)
    sine = jnp.where(odd, c, s)
    cosine = jnp.where(((q + 1) & 2) == 2, -cosine, cosine)
    sine = jnp.where((q & 2) == 2, -sine, sine)
    return cosine, sine


def tile_parts(pixels, cosine, sine, half):
    hot = iota((WINDOW, TILE), 0) == pixels
    hot = jnp.where(hot, 1.0, 0.0).astype(BF16)
    sub = iota((8, TILE), 0)
    part = sub & 3
    weight = jnp.where(part == 0, 1.0, jnp.where(part == 1, cosine, sine))
    weight = jnp.where(((sub >> 2) == half) & (part < 3), weight, 0.0)
    return hot, weight


def bin_tile(hot, weight):
    high = weight.astype(BF16).astype(F32)
    both = jnp.concatenate([high, weight - high], axis=0).astype(BF16)
    res = dot(both, hot, NT)
    return res[:8] + res[8:]


def scan_tile(hot, weight, value):
    high = value.astype(BF16).astype(F32)
    both = jnp.concatenate([high, value - high], axis=0).astype(BF16)
    res = dot(both, hot)
    return (res[:8] + res[8:]) * weight


def put_bins(acc_ref, out_ref, extra):
    pairs = acc_ref.shape[0] // 2
    left = iota((8, TILE), 1) < 64
    last = (iota((8, TILE), 0) & 3) == 3
    for u in range(pairs):
        for b in range(2):
            first = acc_ref[u, :, b * TILE : (b + 1) * TILE]
            second = acc_ref[pairs + u, :, b * TILE : (b + 1) * TILE]
            even = jnp.where(left, first, pltpu.roll(second, 64, 1))
            odd = jnp.where(left, pltpu.roll(first, 64, 1), second)
            for q, value in ((2 * b, even), (2 * b + 1, odd)):
                at = (q * pairs + u) * 8
                out_ref[at : at + 8, :] = jnp.where(last, extra[u % len(extra)], value)


def get_sky(in_ref, sky_ref):
    pairs = sky_ref.shape[0] // 2
    left = iota((8, TILE), 1) < 64
    for u in range(pairs):
        for b in range(2):
            at = (2 * b * pairs + u) * 8
            even = in_ref[at : at + 8, :]
            at = ((2 * b + 1) * pairs + u) * 8
            odd = in_ref[at : at + 8, :]
            sky_ref[u, :, b * TILE : (b + 1) * TILE] = jnp.where(left, even, pltpu.roll(odd, 64, 1))
            sky_ref[pairs + u, :, b * TILE : (b + 1) * TILE] = jnp.where(
                left, pltpu.roll(even, 64, 1), odd
            )


def coded(number):
    base = number & 7
    return (number >> 3) * 128 + (base >> 2) + (base & 3) * 16


def pack_kernel(*refs):
    operands, (out_ref, own_ref), kept = refs[:7], refs[7:9], refs[9:16]
    slot_ref, way_ref, res_ref, amp_ref, pixel_ref, next_ref, sems = refs[16:]
    pix_ref, ang_ref, hits_ref = kept[4:]
    targets = kept + (slot_ref, way_ref, res_ref, amp_ref)
    copies = [
        pltpu.make_async_copy(operands[k % 7], target, sems.at[k])
        for k, target in enumerate(targets)
    ]
    for copy in copies:
        copy.start()
    own_ref[...] = jnp.zeros_like(own_ref)
    out_ref[...] = jnp.zeros_like(out_ref)
    for z in range(PLANES):
        next_ref[z] = z * CHUNK
    for copy in copies:
        copy.wait()
    dets, bases = way_ref.shape
    per_det = slot_ref.shape[1]
    lane1 = iota((1, TILE), 1)
    values = jnp.zeros((1, TILE), F32)
    amps = jnp.zeros((1, TILE), F32)
    for d in range(dets):
        for b in range(bases):
            k = d * bases + b
            values = jnp.where((lane1 == WAYS + k) | (lane1 == 72 + k), way_ref[d, b], values)
            values = jnp.where(lane1 == 64 + k, res_ref[d, b], values)
            amps = jnp.where(lane1 == k, amp_ref[d, b], amps)
    own_ref[0:1, :] = values
    own_ref[1:2, :] = amps
    sub, lane = iota((PLANES, TILE), 0), iota((PLANES, TILE), 1)
    at_row = sub * CHUNK + lane
    pix = pix_ref[...]
    pixel_ref[...] = ((pix & 192) << 1) + (pix & 63)

    def tile_step(t, codes):
        for d in range(dets):
            slot = slot_ref[d, t]
            plane = slot // (2 * NEAR)
            at = next_ref[plane]
            next_ref[plane] = at + 1
            at = jnp.minimum(at, out_ref.shape[0] - ROOM - 1)
            row = t * dets + d
            out_ref[pl.ds(at, 1), :] = ang_ref[pl.ds(row, 1), :]
            pixels = pixel_ref[pl.ds(row, 1), :] + (slot & 1) * 64
            out_ref[pl.ds(at + ROOM, 1), :] = pixels.astype(F32)
            codes = jnp.where(at_row == at, slot * 64 + row, codes)
        return codes

    codes = lax.fori_loop(0, per_det, tile_step, jnp.zeros((PLANES, TILE), I32), unroll=4)
    over = jnp.int32(0)
    for z in range(PLANES):
        count = next_ref[z] - z * CHUNK
        over = jnp.maximum(over, jnp.where(count > ROOM, 1, 0))
        codes = jnp.where((sub == z) & (lane == COUNT), coded(jnp.minimum(count, ROOM)), codes)
    codes = jnp.where(lane == OVER, coded(over), codes)
    codes = jnp.where(lane == HERE, coded(sub), codes)
    codes = jnp.where(lane < WAYS, codes.astype(F32), values)
    out_ref[pl.ds(CODES, PLANES, stride=CHUNK), :] = codes
    hits = jnp.concatenate([hits_ref[0:1, :], hits_ref[1:2, :]], axis=1).astype(F32)
    out_ref[pl.ds(HITS, PLANES, stride=CHUNK), :] = jnp.broadcast_to(hits, (PLANES, TILE))


def start_codes(in_ref, code_ref, sems):
    name_in, way_in = in_ref
    names, ways = code_ref
    copies = [
        pltpu.make_async_copy(name_in, names, sems.at[PLANES]),
    ]
    for z in range(PLANES):
        copies.append(
            pltpu.make_async_copy(
                way_in.at[pl.ds(z * CHUNK + CODES, 1), :], ways.at[pl.ds(z, 1), :], sems.at[z]
            )
        )
    for copy in copies:
        copy.start()
    return copies


def each_pair(in_ref, names, cos_ref, sin_ref, use):
    part, quarter = iota((16, TILE), 0) & 3, iota((16, TILE), 0) >> 2
    first, second = part == 0, part == 1
    quarter = jnp.where(part < 3, quarter, -1)
    pixel = iota((TILE, TILE), 0).astype(F32).astype(BF16)
    counts = [names[z, COUNT] for z in range(PLANES)]
    ends = []
    for z in range(PLANES):
        ends.append(counts[z] if z % GROUP == 0 else ends[-1] + counts[z])
    steps = jnp.int32(0)
    for z in range(GROUP - 1, PLANES, GROUP):
        steps = jnp.maximum(steps, (ends[z] + PER_STEP - 1) // PER_STEP)

    def tile(group, i):
        low = group * GROUP
        z, start = jnp.int32(low), jnp.int32(0)
        for k in range(GROUP - 1):
            z = z + jnp.where(i >= ends[low + k], 1, 0)
            start = jnp.where(i >= ends[low + k], ends[low + k], start)
        p = jnp.minimum(i - start, ROOM - 1)
        code = names[z, p]
        mine = in_ref[pl.ds(z * CHUNK + ROOM + p, 1), :].astype(I32)
        place = jnp.broadcast_to((mine & 127).astype(F32), (TILE, TILE)).astype(BF16)
        hot = jnp.maximum(1.0 - jnp.abs(pixel - place), 0.0)
        row = pl.ds(z * ANGLES + p, 1)
        weight = jnp.where(first, 1.0, jnp.where(second, cos_ref[row, :], sin_ref[row, :]))
        weight = jnp.where(quarter == (mine >> 7), weight, 0.0)
        return (z, code >> 3, code & 7, i < ends[low + GROUP - 1]), hot, weight

    def some(g, carry):
        for group in range(PLANES // GROUP):
            for k in range(0, PER_STEP, 2):
                use(*zip(*(tile(group, g * PER_STEP + k + n) for n in range(2))))
        return carry

    lax.fori_loop(0, steps, some, 0)


def table_rows(q, owner, z, chunk, count):
    return pl.ds((q * NEAR + owner) * chunk + z, count, stride=PLANES)


def halves(x):
    high, low = split(x)
    return jnp.concatenate([high, low], axis=0)


def bin_kernel(in_ref, name_ref, out_ref, cos_ref, sin_ref, names, ways, sems):
    copies = start_codes((name_ref, in_ref), (names, ways), sems)
    for z in range(PLANES):
        c, s = cos_sin(2.0 * in_ref[z * CHUNK : z * CHUNK + ANGLES, :])
        cos_ref[z * ANGLES : (z + 1) * ANGLES, :] = c
        sin_ref[z * ANGLES : (z + 1) * ANGLES, :] = s
    out_ref[...] = jnp.zeros_like(out_ref)
    for copy in copies:
        copy.wait()
    hits = in_ref[pl.ds(HITS, PLANES, stride=CHUNK), :].astype(BF16)
    lane, deep = iota((TILE, TILE), 1), iota((TILE, TILE), 0)
    here = (lane & 1) * 64 + names[0, HERE] * NEAR + ((lane >> 1) & (NEAR - 1))
    moved = dot(hits, jnp.where(deep == here, 1.0, 0.0).astype(BF16))
    moved = jnp.where(iota((PLANES, TILE), 1) >> 4 == iota((PLANES, TILE), 0), moved, 0.0)
    moved = jnp.sum(moved, axis=0, keepdims=True)
    for at in range(BINS - 1, out_ref.shape[0], BINS):
        out_ref[at : at + 1, :] = moved

    def use(tiles, hots, weights):
        both = jnp.concatenate([halves(weight) for weight in weights], axis=0)
        res = dot(both, jnp.concatenate(hots, axis=0), NT)
        for n, (z, owner, base, valid) in enumerate(tiles):
            height = jnp.where(valid, ways[z, WAYS + base], 0.0)
            mine = res[32 * n : 32 * n + 32, n * TILE : (n + 1) * TILE]
            mine = (mine[:16] + mine[16:]) * height
            for q in range(4):
                rows = table_rows(q, owner, z, BINS, 3)
                out_ref[rows, :] = out_ref[rows, :] + mine[4 * q : 4 * q + 3]

    each_pair(in_ref, names, cos_ref, sin_ref, use)


def own_kernel(me_ref, in_ref, prec_ref, out_ref):
    peers = in_ref.shape[0] // BINS
    sources = peers * PLANES
    owner = me_ref[0:1, :] & (NEAR - 1)

    def take(c):
        if c < 3:
            at = [w * BINS + c * PLANES for w in range(peers)]
            return jnp.concatenate([in_ref[a : a + PLANES, :] for a in at], axis=0)
        mine = iota((PLANES, TILE), 1) >> 4 == iota((PLANES, TILE), 0)
        at = [w * BINS + BINS - 1 for w in range(peers)]
        return jnp.concatenate([jnp.where(mine, in_ref[a : a + 1, :], 0.0) for a in at], axis=0)

    def put(c, value):
        out_ref[:, c * PLANES : (c + 1) * PLANES, :] = value.reshape(peers, PLANES, TILE)

    def place(lane, k):
        return (lane & 15) == 2 * owner + k

    own_solve(place, me_ref[1:2, :], sources, take, prec_ref, put)


def slow_own_kernel(me_ref, in_ref, prec_ref, out_ref):
    sources = in_ref.shape[0] // 4

    def take(c):
        return in_ref[pl.ds(c, sources, stride=4), :]

    def put(c, value):
        out_ref[pl.ds(c, sources, stride=4), :] = value

    def place(lane, k):
        return lane == me_ref[0:1, :] + 64 * k

    own_solve(place, me_ref[1:2, :], sources, take, prec_ref, put)
    put(3, jnp.zeros((sources, TILE), F32))


def own_solve(place, quarter, sources, take, prec_ref, put):
    subs = prec_ref.shape[1]
    ids = take(3).astype(BF16)
    lane = iota((16, TILE), 1)
    row = iota((16, TILE), 0)
    pick = jnp.where(place(lane, row) & (row < 2), 1.0, 0.0).astype(BF16)
    id_rows = dot(pick, ids, NT).astype(I32)
    sub = iota((subs, sources), 0)
    hot = jnp.concatenate(
        [
            jnp.where(sub == id_rows[0:1, :], 1.0, 0.0),
            jnp.where(sub == id_rows[1:2, :], 1.0, 0.0),
        ],
        axis=0,
    ).astype(BF16)
    left = iota((subs, TILE), 1) < 64
    binned = []
    for c in range(3):
        high, low = split(take(c))
        res = dot(hot, jnp.concatenate([high, low], axis=1))
        res = res[:, :TILE] + res[:, TILE:]
        res = jnp.where(left, res[:subs], res[subs:])
        binned.append(res + pltpu.roll(res, 64, 1))

    quarter = jnp.broadcast_to(quarter, (subs, TILE))
    keep = (iota((subs, TILE), 1) >> 6) == (quarter & 1)
    block = quarter >> 1
    prec = []
    for e in range(6):
        value = jnp.where(block == 0, prec_ref[e, :, :TILE], prec_ref[e, :, TILE:])
        value = jnp.where(keep, value, 0.0)
        prec.append(value + pltpu.roll(value, 64, 1))
    sky = [
        prec[0] * binned[0] + prec[1] * binned[1] + prec[2] * binned[2],
        prec[1] * binned[0] + prec[3] * binned[1] + prec[4] * binned[2],
        prec[2] * binned[0] + prec[4] * binned[1] + prec[5] * binned[2],
    ]

    deep, wide = iota((TILE, TILE), 0), iota((TILE, TILE), 1)
    spread = jnp.where(place(deep, wide >> 6), 1.0, 0.0).astype(BF16)
    named = dot(ids, spread).astype(I32)
    back = jnp.where(named == (iota((sources, TILE), 1) & 63), 1.0, 0.0).astype(BF16)
    back = jnp.concatenate([back, back], axis=1)
    gap = jnp.zeros((64 - subs, TILE), F32)
    for c in range(3):
        first = jnp.where(left, sky[c], 0.0)
        second = jnp.where(left, 0.0, sky[c])
        high, low = split(jnp.concatenate([first, gap, second, gap], axis=0))
        put(c, dot(back, jnp.concatenate([high, low], axis=0)))


def scan_kernel(
    in_ref, name_ref, cos_ref, sin_ref, sky_in_ref, own_ref, out_ref, sky_ref, sum_ref, names, sems
):
    copy = pltpu.make_async_copy(name_ref, names, sems.at[0])
    copy.start()
    for peer in range(4 * NEAR):
        for c in range(4):
            at = (peer * 4 + c) * PLANES
            here = (peer * 3 + c) * PLANES
            sky_ref[at : at + PLANES, :] = (
                sky_in_ref[here : here + PLANES, :] if c < 3 else jnp.zeros((PLANES, TILE), F32)
            )
    sum_ref[...] = jnp.zeros_like(sum_ref)
    copy.wait()

    def use(tiles, hots, weights):
        both = []
        for z, owner, _, _ in tiles:
            value = [sky_ref[table_rows(q, owner, z, 4 * PLANES, 4), :] for q in range(4)]
            both.append(halves(jnp.concatenate(value, axis=0)))
        res = dot(jnp.concatenate(both, axis=0), jnp.concatenate(hots, axis=1))
        for n, (z, _, base, valid) in enumerate(tiles):
            mine = res[32 * n : 32 * n + 32, n * TILE : (n + 1) * TILE]
            mine = (mine[:16] + mine[16:]) * weights[n]
            rows = pl.ds(pl.multiple_of((z * 8 + base) * 8, 8), 8)
            mine = (mine[:8] + mine[8:]) * jnp.where(valid, 1.0, 0.0)
            sum_ref[rows, :] = sum_ref[rows, :] + mine

    each_pair(in_ref, names, cos_ref, sin_ref, use)
    count = PLANES * 8
    sums = sum_ref[pl.ds(0, count, stride=8), :]
    for k in range(1, 8):
        sums = sums + sum_ref[pl.ds(k, count, stride=8), :]
    sums = jnp.sum(sums, axis=1, keepdims=True)
    lane, sub = iota((count, TILE), 1), iota((count, TILE), 0)
    row = jnp.sum(jnp.where(lane == sub, sums, 0.0), axis=0, keepdims=True)
    row = row * np.float32(1.0 / 1024)
    lane = iota((1, TILE), 1)
    row = jnp.where(lane < 64, row, jnp.where(lane < 80, own_ref[0:1, :], 0.0))
    over = names[0, OVER]
    for z in range(1, PLANES):
        over = jnp.maximum(over, names[z, OVER])
    row = jnp.where(lane == 96, over.astype(F32), row)
    out_ref[...] = jnp.broadcast_to(row, out_ref.shape)


def end_kernel(me_ref, in_ref, own_ref, amp_out, res_out, dir_out, over_out):
    dets, bases = amp_out.shape
    spans = in_ref.shape[0] // (PLANES * NEAR)
    lane = iota((NEAR, TILE), 1)
    valid = lane < PLANES * 8
    base = lane % bases
    scan, way, rest = [], [], []
    over = jnp.zeros((NEAR, TILE), F32)
    for i in range(spans):
        a = w = r = jnp.zeros((NEAR, TILE), F32)
        for z in range(PLANES):
            at = (i * PLANES + z) * NEAR
            x = in_ref[at : at + NEAR, :]
            a = a + x
            over = jnp.maximum(over, x)
            group = lane >> 3
            r = r + pltpu.roll(jnp.where(group == 8, x, 0.0), (z * 8 - 64) % TILE, 1)
            w = w + pltpu.roll(jnp.where(group == 9, x, 0.0), (z * 8 - 72) % TILE, 1)
        scan.append(a)
        way.append(w)
        rest.append(r)
    over = jnp.where(lane == 96, over, 0.0)
    zero = jnp.zeros((NEAR, TILE), F32)
    applied = []
    for i in range(spans):
        from_left = pltpu.roll(way[i - 1] if i else zero, TILE - (bases - 1), 1)
        from_right = pltpu.roll(way[i + 1] if i < spans - 1 else zero, bases - 1, 1)
        before = jnp.where(base == 0, from_left, pltpu.roll(way[i], 1, 1))
        after = jnp.where(base == bases - 1, from_right, pltpu.roll(way[i], TILE - 1, 1))
        v = scan[i] + way[i] + STIFFNESS * (2.0 * way[i] - before - after)
        applied.append(jnp.where(valid, v, 0.0))

    def total(terms):
        v = terms[0]
        for term in terms[1:]:
            v = v + term
        return jnp.sum(jnp.sum(v, axis=0, keepdims=True), axis=1, keepdims=True)

    now = total([r * r for r in rest])
    factor = now / total([w * a for w, a in zip(way, applied)])
    fresh = [r - factor * a for r, a in zip(rest, applied)]
    ratio = total([f * f for f in fresh]) / now
    sub = iota((NEAR, TILE), 0)
    det = jnp.broadcast_to(me_ref[0:1, :], (NEAR, TILE))
    span = jnp.broadcast_to(me_ref[1:2, :], (NEAR, TILE))
    here = (sub == (det & (NEAR - 1))) & ((lane >> 3) == (det >> 3))
    mine = zero
    for i in range(spans):
        mine = mine + jnp.where(here & (span == i), fresh[i], 0.0)
    for shift in (64, 32, 16, 8):
        mine = mine + pltpu.roll(mine, shift, 1)
    mine = jnp.sum(mine, axis=0, keepdims=True)
    my_way = own_ref[0:1, 72:80]
    my_fresh = mine[:, 0:8]
    moved = own_ref[1:2, 0:8] + factor * my_way
    turn = my_fresh + ratio * my_way
    for d in range(dets):
        lo, hi = d * bases, (d + 1) * bases
        amp_out[d : d + 1, :] = moved[:, lo:hi]
        res_out[d : d + 1, :] = my_fresh[:, lo:hi]
        dir_out[d : d + 1, :] = turn[:, lo:hi]
    over_out[0] = jnp.max(over)


def slow_bin_kernel(slot_ref, dir_ref, pix_ref, ang_ref, hits_ref, out_ref, cos_ref, sin_ref, acc_ref):
    c, s = cos_sin(2.0 * ang_ref[...])
    cos_ref[...] = c
    sin_ref[...] = s
    acc_ref[...] = jnp.zeros_like(acc_ref)
    tiles = pix_ref.shape[0]
    dets, bases = dir_ref.shape
    span = tiles // dets // bases

    def group(g, carry):
        det, base = g % dets, g // dets
        height = dir_ref[det, base]
        for t in range(span):
            tile = base * span + t
            slot = slot_ref[det, tile]
            row = pl.ds(tile * dets + det, 1)
            hot, weight = tile_parts(
                pix_ref[row, :], cos_ref[row, :], sin_ref[row, :], (slot >> 1) & 1
            )
            place = (slot & 1) * (acc_ref.shape[0] // 2) + (slot >> 2)
            acc_ref[place] = acc_ref[place] + bin_tile(hot, weight) * height
        return carry

    lax.fori_loop(0, dets * bases, group, 0)

    put_bins(acc_ref, out_ref, [jnp.broadcast_to(hits_ref[...], (8, TILE))])


def slow_scan_kernel(
    slot_ref, dir_ref, res_ref, pix_ref, ang_ref, in_ref, out_ref, cos_ref, sin_ref, sky_ref, sum_ref
):
    c, s = cos_sin(2.0 * ang_ref[...])
    cos_ref[...] = c
    sin_ref[...] = s
    get_sky(in_ref, sky_ref)
    pairs = sky_ref.shape[0] // 2
    tiles = pix_ref.shape[0]
    dets, bases = dir_ref.shape
    span = tiles // dets // bases

    def group(g, carry):
        det, base = g % dets, g // dets
        total = jnp.zeros((8, TILE), F32)
        for t in range(span):
            tile = base * span + t
            slot = slot_ref[det, tile]
            row = pl.ds(tile * dets + det, 1)
            hot, weight = tile_parts(
                pix_ref[row, :], cos_ref[row, :], sin_ref[row, :], (slot >> 1) & 1
            )
            place = (slot & 1) * pairs + (slot >> 2)
            total = total + scan_tile(hot, weight, sky_ref[place])
        sum_ref[pl.ds(det * bases + base, 1), :] = jnp.sum(total, axis=0, keepdims=True)
        return carry

    lax.fori_loop(0, dets * bases, group, 0)
    count = dets * bases
    sums = jnp.sum(sum_ref[...], axis=1, keepdims=True) * np.float32(1.0 / (span * TILE))
    lane, sub = iota((count, TILE), 1), iota((count, TILE), 0)
    row = jnp.sum(jnp.where(lane == sub, sums, 0.0), axis=0, keepdims=True)
    lane = iota((1, TILE), 1)
    for d in range(dets):
        for b in range(bases):
            k = d * bases + b
            row = jnp.where(lane == count + k, dir_ref[d, b], row)
            row = jnp.where(lane == 2 * count + k, res_ref[d, b], row)
    out_ref[...] = jnp.broadcast_to(row, out_ref.shape)


def slow_end_kernel(me_ref, in_ref, amp_ref, amp_out, res_out, dir_out, keep_ref):
    rows = in_ref.shape[0]
    dets, bases = amp_ref.shape
    count = dets * bases
    owners = me_ref[2]
    x = in_ref[...]
    lane = iota((rows, TILE), 1)
    valid = lane < count
    base = lane % bases
    scan = jnp.where(valid, x, 0.0)
    way = jnp.where(valid, pltpu.roll(x, TILE - count, 1), 0.0)
    rest = jnp.where(valid, pltpu.roll(x, TILE - 2 * count, 1), 0.0)
    step = rows // 4
    zero = jnp.zeros((step, TILE), F32)
    from_left = pltpu.roll(jnp.concatenate([zero, way[:-step]], axis=0), TILE - (bases - 1), 1)
    from_right = pltpu.roll(jnp.concatenate([way[step:], zero], axis=0), bases - 1, 1)
    before = jnp.where(base == 0, from_left, pltpu.roll(way, 1, 1))
    after = jnp.where(base == bases - 1, from_right, pltpu.roll(way, TILE - 1, 1))
    applied = scan + way + STIFFNESS * (2.0 * way - before - after)
    applied = jnp.where(valid, applied, 0.0)

    def total(v):
        return jnp.sum(jnp.sum(v, axis=0, keepdims=True), axis=1, keepdims=True)

    now = total(rest * rest)
    factor = now / total(way * applied)
    fresh = rest - factor * applied
    ratio = total(fresh * fresh) / now
    keep_ref[0] = fresh
    keep_ref[1] = way
    mine = me_ref[1] * step + me_ref[0]
    my_fresh = keep_ref[0, pl.ds(mine, 1), :]
    my_way = keep_ref[1, pl.ds(mine, 1), :]
    move = factor * my_way
    turn = my_fresh + ratio * my_way
    for d in range(dets):
        lo, hi = d * bases, (d + 1) * bases
        amp_out[d : d + 1, :] = amp_ref[d : d + 1, :] + move[:, lo:hi]
        res_out[d : d + 1, :] = my_fresh[:, lo:hi]
        dir_out[d : d + 1, :] = turn[:, lo:hi]


SMEM = pl.BlockSpec(memory_space=pltpu.SMEM)
VMEM = pl.BlockSpec(memory_space=pltpu.VMEM)
SMALL = pltpu.CompilerParams(vmem_limit_bytes=12 << 20)
DET = ("z", "x", "core")
ALL = ("tm",) + DET
PLANE = ("tm", "x", "core")


def exchange(value, axes, rows):
    if rows % 4:
        moved = lax.all_to_all(value.reshape(-1, 1, TILE), axes, 0, 0, tiled=True)
        return moved.reshape(value.shape)
    peers = value.shape[0] // rows
    moved = lax.all_to_all(value.reshape(peers, rows, TILE), axes, 0, 0, tiled=True)
    return moved.reshape(value.shape)


def f32(*shape):
    return jax.ShapeDtypeStruct(shape, F32)


def slow(owners, me, prec, places, way, res, amp, pix, ang, hits):
    spot = jnp.stack([me[0, 0], me[1, 0], jnp.int32(owners)])
    tiles = pix.shape[0]
    slots = hits.shape[1] * 2
    peers = 4 * hits.shape[1]
    hit_row = hits.reshape(1, slots).astype(F32)
    table = [pltpu.VMEM((tiles, TILE), F32)] * 2 + [pltpu.VMEM((slots // 2, 8, WINDOW), F32)]
    binned = pl.pallas_call(
        slow_bin_kernel,
        out_shape=f32(peers * 4, TILE),
        in_specs=[SMEM, SMEM, VMEM, VMEM, VMEM],
        out_specs=VMEM,
        scratch_shapes=table,
        name="slow_bin",
    )(places, way, pix, ang, hit_row)
    sky = solve(slow_own_kernel, (me, exchange(binned, ALL, 4), prec), peers * 4)
    last = pl.pallas_call(
        slow_scan_kernel,
        out_shape=f32(peers, TILE),
        in_specs=[SMEM, SMEM, SMEM, VMEM, VMEM, VMEM],
        out_specs=VMEM,
        scratch_shapes=table + [pltpu.VMEM((8, TILE), F32)],
        name="slow_scan",
    )(places, way, res, pix, ang, exchange(sky, ALL, 4))
    return pl.pallas_call(
        slow_end_kernel,
        out_shape=[f32(*amp.shape)] * 3,
        in_specs=[SMEM, VMEM, VMEM],
        out_specs=[VMEM] * 3,
        scratch_shapes=[pltpu.VMEM((2, peers, TILE), F32)],
        name="slow_end",
    )(spot, exchange(last, ALL, 1), amp)


def solve(kernel, args, *shape):
    shape = shape + (TILE,)
    return pl.pallas_call(
        kernel,
        out_shape=f32(*shape),
        in_specs=[VMEM] * 3,
        out_specs=VMEM,
        compiler_params=SMALL,
        name=kernel.__name__,
    )(*args)


def shards(amp, res, way, pix, ang, places, hits, prec):
    dets, samples = pix.shape
    per_det = samples // TILE
    tiles = dets * per_det
    owners = hits.shape[2]
    peers = 4 * owners
    near = 4 * NEAR

    def rows_of(v):
        return v.reshape(dets, per_det, TILE).transpose(1, 0, 2).reshape(tiles, TILE)

    pix, ang = rows_of(pix), rows_of(ang)
    hits = hits.reshape(owners, 2).T
    prec = prec.transpose(1, 0, 2)
    first = lax.broadcasted_iota(I32, (8, TILE), 0) == 0
    me = jnp.where(first, lax.axis_index(DET), lax.axis_index("tm")).astype(I32)

    me, places = lax.optimization_barrier((me, places))
    given = (places, way, res, amp, pix, ang, hits)
    given = tuple(pltpu.with_memory_space_constraint(v, pltpu.HBM) for v in given)
    packed, own, *given = pl.pallas_call(
        pack_kernel,
        out_shape=[f32(PLANES * CHUNK, TILE), f32(8, TILE)]
        + [jax.ShapeDtypeStruct(v.shape, v.dtype) for v in given],
        in_specs=[pl.BlockSpec(memory_space=pltpu.HBM)] * 7,
        out_specs=[VMEM] * 9,
        scratch_shapes=[pltpu.SMEM(v.shape, v.dtype) for v in given[:4]]
        + [
            pltpu.VMEM((tiles, TILE), I32),
            pltpu.SMEM((PLANES,), I32),
            pltpu.SemaphoreType.DMA((11,)),
        ],
        compiler_params=SMALL,
        name="pack_tiles",
    )(*given)
    packed = exchange(packed, "z", CHUNK)

    raw = packed.reshape(PLANES, CHUNK, TILE)[:, CODES].astype(I32)
    slot, row = raw >> 6, raw & 63
    base = row % dets * way.shape[1] + row // (tiles // way.shape[1])
    names = (slot // 2 % NEAR) * 8 + base
    sems = pltpu.SemaphoreType.DMA((PLANES + 1,))
    binned, cosine, sine = pl.pallas_call(
        bin_kernel,
        out_shape=[f32(near * BINS, TILE)] + [f32(PLANES * ANGLES, TILE)] * 2,
        in_specs=[VMEM] * 2,
        out_specs=[VMEM] * 3,
        scratch_shapes=[
            pltpu.SMEM((PLANES, TILE), I32),
            pltpu.SMEM((PLANES, TILE), F32),
            sems,
        ],
        compiler_params=SMALL,
        name="bin_tiles",
    )(packed, names)
    binned = exchange(binned, PLANE, BINS)
    sky = solve(own_kernel, (me, binned, prec), near, 3 * PLANES)
    sky = exchange(sky.reshape(near * 3 * PLANES, TILE), PLANE, 3 * PLANES)

    last = pl.pallas_call(
        scan_kernel,
        out_shape=f32(peers, TILE),
        in_specs=[VMEM] * 6,
        out_specs=VMEM,
        scratch_shapes=[
            pltpu.VMEM((near * 4 * PLANES, TILE), F32),
            pltpu.VMEM((PLANES * 64, TILE), F32),
            pltpu.SMEM((PLANES, TILE), I32),
            sems,
        ],
        compiler_params=SMALL,
        name="scan_tiles",
    )(packed, names, cosine, sine, sky, own)
    *out, over = pl.pallas_call(
        end_kernel,
        out_shape=[f32(*amp.shape)] * 3 + [f32(1)],
        in_specs=[VMEM] * 3,
        out_specs=[VMEM] * 3 + [SMEM],
        compiler_params=SMALL,
        name="end_step",
    )(me, exchange(last, ALL, 1), own)
    over, *given = lax.optimization_barrier((over, *given))
    return lax.cond(
        over[0] > 0,
        lambda: tuple(slow(owners, me, prec, *given)),
        lambda: tuple(out),
    )


def solution(mesh):
    spans = mesh.shape["tm"]
    split_mesh = jax.sharding.Mesh(
        mesh.devices.reshape(spans, PLANES, NEAR // 2, 2), ("tm", "z", "x", "core")
    )
    return jax.shard_map(
        shards,
        mesh=split_mesh,
        in_specs=(P(DET, "tm"),) * 6 + (P("tm", DET, None, None), P(DET, None, None)),
        out_specs=(P(DET, "tm"),) * 3,
        check_vma=False,
    )
```
